32 devices in a mesh: groups: 2 (over x), slab: 16 (over z, y, core).
Axes of the slice: x: 2, y: 2, z: 4, core: 2. Of those that a mesh axis runs over, the one named last changes fastest.
Arguments:
- volume: float32 [2, 1024, 1024], P('groups', 'slab'), parts along dimension 0, may hold values from -6 to 6
- noise: float32 [2, 1024, 1024], P('groups', 'slab'), parts along dimension 0, may hold values from -6 to 6
- measured: float32 [2, 1024, 16, 1024], P('groups', 'slab'), parts along dimension 0, may hold values from -20 to 20
- angles: int32 [32], P('groups'), parts along dimension 0, may hold values from 0 to 179
- offsets: int32 [32], P('groups'), parts along dimension 0, may hold values from -32 to 32
- step_size: float32 [2], P('groups'), parts along dimension 0, may hold values from 0.1 to 0.4
- lift_w: float32 [64], replicated, may hold values from -4 to 4
- lift_b: float32 [64], replicated, may hold values from -4 to 4
- conv_a: bfloat16 [9, 64, 64], replicated, may hold values from -0.25 to 0.25
- bias_a: float32 [64], replicated, may hold values from -4 to 4
- conv_b: bfloat16 [9, 64, 64], replicated, may hold values from -0.25 to 0.25
- out_w: float32 [64], replicated, may hold values from -0.75 to 0.75
Outputs:
- updated: float32 [2, 1024, 1024], P('groups', 'slab'), parts along dimension 0
The draws below stay inside these ranges and needn't reach their ends.
There are 2 independent parts, one for each index of `groups`. The reference program is written for one: setup_inputs(seed, part) draws one part's arguments, and reference() takes and returns one part's arrays. A program takes and returns all parts, laid end to end along the dimension named above; an argument that names none is the same for every part. Nothing has to cross between parts.
All inputs are finite; a program needn't handle non-finite values.
Results may differ from the reference program's by a relative error of at most 0.0025.
Values may be sent and summed in bfloat16 or wider, within the bound.
No kernel may reach another device: no remote copies, remote signals or barrier semaphores. Data moves between devices by JAX's collectives and lax.ppermute only.
A program may use at most 256 MiB of HBM per device.

```python
import math
import jax
import jax.numpy as jnp
from jax import lax

NX = 1024
NY = 1024
DET = 1024
CH = 64
VIEWS = 16
ANGLES = 180
OFFSET = 32
SLICES = 1


def draw_measured(key, part):
    first, second = jax.random.split(key, 2)
    ramp = 10.0 ** (jnp.arange(NY, dtype=jnp.float32) / (NY - 1))
    view_scale = jnp.exp(jax.random.uniform(second, (VIEWS,), jnp.float32, math.log(0.5), math.log(2.0)))
    scale = 0.5 * ramp[:, None, None] * view_scale[:, None]
    base = jax.random.normal(first, (SLICES, NY, VIEWS, DET), jnp.float32)
    values = base * scale
    return jnp.clip(values, -20.0, 20.0)


def touch_ends(entries, own_key, least, high):
    extent = entries.shape
    spot = [jax.random.randint(jax.random.fold_in(own_key, axis), (), 0, extent[axis]) for axis in range(len(extent))]
    entries = entries.at[tuple(spot)].set(least)
    longest = extent.index(max(extent))
    spot[longest] = (spot[longest] + 1) % extent[longest]
    return entries.at[tuple(spot)].set(high)


def steps_of(rng, dims, pieces, least, high):
    factor_of = 1.0
    for position, shards_of in pieces:
        steps = jax.random.uniform(jax.random.fold_in(jax.random.fold_in(rng, 6), position), (shards_of,), jnp.float32, least / len(pieces), high / len(pieces))
        factor_of = factor_of * jnp.repeat(jnp.exp(steps), dims[position] // shards_of).reshape((-1,) + (1,) * (len(dims) - 1 - position))
    return factor_of


def gaussian(stream_key, shape, scale, limit, cuts=(), kind=jnp.bfloat16):
    level = steps_of(stream_key, shape, cuts, -0.22, 0.18) if cuts else 1.0
    result = jax.random.normal(stream_key, shape, jnp.float32) * scale * level
    return jnp.minimum(jnp.maximum(result, -limit), limit).astype(kind)


def setup_inputs(seed: int = 0, part: int = 0) -> dict:
    splits = jax.random.split(jax.random.key(seed), 13)
    part_keys = jax.random.split(jax.random.fold_in(splits[12], part), 13)
    return {
        "volume": gaussian(part_keys[0], (SLICES, NX, NY), 1.0, 6.0, ((1, 16),), jnp.float32),
        "noise": gaussian(part_keys[1], (SLICES, NX, NY), 1.0, 6.0, ((1, 16),), jnp.float32),
        "measured": draw_measured(jax.random.fold_in(jax.random.fold_in(splits[12], part), 71), part),
        "angles": touch_ends(jax.random.randint(part_keys[3], (VIEWS,), 0, ANGLES), jax.random.fold_in(part_keys[3], 1), 0, ANGLES - 1).astype(jnp.int32),
        "offsets": touch_ends(jax.random.randint(part_keys[4], (VIEWS,), 0 - OFFSET, OFFSET + 1), jax.random.fold_in(part_keys[4], 1), 0 - OFFSET, OFFSET).astype(jnp.int32),
        "step_size": jnp.clip(jnp.exp(jax.random.uniform(part_keys[5], (1,), jnp.float32, math.log(0.1), math.log(0.4))), 0.1, 0.4),
        "lift_w": gaussian(splits[6], (CH,), 1.0, 4.0, (), jnp.float32),
        "lift_b": gaussian(splits[7], (CH,), 1.0, 4.0, (), jnp.float32),
        "conv_a": gaussian(splits[8], (9, CH, CH), (9 * CH) ** -0.5, 0.25),
        "bias_a": gaussian(splits[9], (CH,), 1.0, 4.0, (), jnp.float32),
        "conv_b": gaussian(splits[10], (9, CH, CH), (9 * CH) ** -0.5, 0.25),
        "out_w": gaussian(splits[11], (CH,), CH ** -0.5, 0.75, (), jnp.float32),
    }


data_gain = 0.25

def conv_rows(padded_rows, kernel):
    rows = padded_rows.shape[-2] - 2
    width = padded_rows.shape[-1]
    padded = jnp.pad(padded_rows, [(0, 0)] * (padded_rows.ndim - 1) + [(1, 1)])
    total = None
    for i in range(3):
        for j in range(3):
            piece = padded[..., i:i + rows, j:j + width]
            flat = piece.reshape(piece.shape[0], -1)
            term = jnp.dot(kernel[3 * i + j], flat, preferred_element_type=jnp.float32)
            term = term.reshape((kernel.shape[1],) + piece.shape[1:])
            total = term if total is None else total + term
    return total

def make_tent(angle, offset):
    level = jnp.abs(jnp.cos(jnp.pi * angle.astype(jnp.float32) / ANGLES))
    spread = 0.6 + 0.4 * level
    bins = jnp.arange(DET, dtype=jnp.float32)[:, None]
    cells = jnp.arange(NX, dtype=jnp.float32)[None, :]
    target = (DET - 1) * 0.5 + (cells - (NX - 1) * 0.5) * spread + offset.astype(jnp.float32)
    return jnp.maximum(0.0, 1.0 - jnp.abs(bins - target)).astype(jnp.bfloat16)

def reference(volume, noise, measured, angles, offsets, step_size, lift_w, lift_b, conv_a, bias_a, conv_b, out_w):

    def score_plane(plane):
        h0 = jax.nn.silu(lift_w[:, None, None] * plane[None] + lift_b[:, None, None]).astype(jnp.bfloat16)
        h1 = jax.nn.silu(conv_rows(jnp.pad(h0, ((0, 0), (1, 1), (0, 0))), conv_a) + bias_a[:, None, None]).astype(jnp.bfloat16)
        mixed = conv_rows(jnp.pad(h1, ((0, 0), (1, 1), (0, 0))), conv_b) + h0.astype(jnp.float32)
        return lax.optimization_barrier(jnp.sum(out_w[:, None, None] * mixed, axis=0))
    score = lax.map(score_plane, volume)
    cells = jnp.transpose(volume.astype(jnp.bfloat16), (0, 2, 1))
    flat_cells = cells.reshape(-1, NX)
    per_view = jnp.moveaxis(measured, 2, 0)

    def one_view(carry, item):
        back, misfit = carry
        angle, offset, seen = item
        tent = make_tent(angle, offset)
        proj = jnp.dot(flat_cells, tent.T, preferred_element_type=jnp.float32)
        rows = proj - seen.reshape(-1, DET)
        misfit = misfit + jnp.sum(rows * rows)
        low = rows.astype(jnp.bfloat16)
        back = back + jnp.dot(low, tent, preferred_element_type=jnp.float32)
        return ((back, misfit), None)
    start = (jnp.zeros((SLICES * NY, NX), jnp.float32), jnp.zeros((), jnp.float32))
    (back, misfit), _ = lax.scan(one_view, start, (angles, offsets, per_view))
    backproj = jnp.transpose(back.reshape(SLICES, NY, NX), (0, 2, 1))
    weight = data_gain / jnp.sqrt(misfit / (SLICES * NY * VIEWS * DET) + 1e-06)
    step = step_size[0]
    return volume + step * (score - weight * backproj) + jnp.sqrt(2.0 * step) * noise
```

```python
import functools

import jax
import jax.numpy as jnp
from jax import lax
from jax.experimental import pallas as pl
from jax.experimental.pallas import tpu as pltpu
from jax.sharding import PartitionSpec as P

ANGLES = 180
LANES = 128

data_gain = 0.25

f32 = jnp.float32
bf16 = jnp.bfloat16
VMEM = pl.BlockSpec(memory_space=pltpu.VMEM)
SMEM = pl.BlockSpec(memory_space=pltpu.SMEM)


def pack_kernel(volume_ref, out_ref, first_ref, last_ref):
    rows = volume_ref.shape[1]
    peers = out_ref.shape[0]
    chunks = LANES // rows
    depth = rows // chunks
    for peer in range(peers):
        piece = volume_ref[0, :, peer * rows : (peer + 1) * rows]
        wide = jnp.concatenate([piece[k * depth : (k + 1) * depth] for k in range(chunks)], axis=1)
        out_ref[peer] = wide.astype(bf16)
    first_ref[...] = volume_ref[0, :2, :]
    last_ref[...] = volume_ref[0, rows - 2 :, :]


def split(value):
    high = value.astype(bf16).astype(f32)
    return high, (value - high).astype(bf16).astype(f32)


def prep_kernel(
    angles_ref, gain_ref, base_ref, conv_a_ref, bias_ref, conv_b_ref, own_ref,
    wa_ref, wb_ref, wr_ref, lift_ref, shift_ref, spread_ref,
):
    channels = conv_a_ref.shape[1]

    def column(row):
        return jnp.broadcast_to(row, (LANES, channels)).T

    lift_ref[0] = column(0.5 * gain_ref[...])
    lift_ref[1] = column(0.5 * base_ref[...])
    shift = column(0.5 * bias_ref[...])
    shift_ref[:channels] = shift
    shift_ref[channels:] = shift

    taps = [conv_a_ref[t].astype(f32) * 0.5 for t in range(9)]
    zero = jnp.zeros((channels, channels), f32)
    for r in range(2):
        for j in range(3):
            for e in range(0, 4, 2):
                pair = [taps[3 * (k - r) + j] if 0 <= k - r < 3 else zero for k in (e, e + 1)]
                at = (4 * j + e) * channels
                wa_ref[r * channels : (r + 1) * channels, at : at + 2 * channels] = jnp.concatenate(
                    pair, axis=1
                ).astype(bf16)

    own = column(own_ref[...])[:, :channels]
    row = lax.broadcasted_iota(jnp.int32, (8, LANES), 0)
    half = lax.broadcasted_iota(jnp.int32, (8, LANES), 1) // channels

    def both(line):
        return jnp.broadcast_to(jnp.concatenate([line, line], axis=1), (8, LANES))

    folded = [split(jnp.sum(own * conv_b_ref[t].astype(f32), axis=0, keepdims=True)) for t in range(9)]
    mine = split(own_ref[...])
    for q in range(5):
        at = slice(q * LANES, (q + 1) * LANES)
        for j in range(3):
            parts = []
            for s in range(2):
                block = jnp.zeros((8, LANES), f32)
                for i in range(3):
                    block = jnp.where(half + 2 * q - row == i, both(folded[3 * i + j][s]), block)
                parts.append(block)
            wb_ref[16 * j : 16 * j + 16, at] = jnp.concatenate(parts, axis=0).astype(bf16)
        if q < 4:
            parts = [jnp.where(half + 2 * q == row, both(mine[s]), 0.0) for s in range(2)]
            wr_ref[:, at] = jnp.concatenate(parts, axis=0).astype(bf16)

    level = jnp.abs(jnp.cos(jnp.pi * angles_ref[...].astype(f32) / ANGLES))
    spread_ref[...] = 0.6 + 0.4 * level


def shifted(block, step):
    width = block.shape[1]
    moved = pltpu.roll(block, (-step) % width, 1)
    lane = lax.broadcasted_iota(jnp.int32, (block.shape[0], LANES), 1)
    if step < 0:
        edge = jnp.where(lane == 0, jnp.zeros_like(moved[:, :LANES]), moved[:, :LANES])
        return jnp.concatenate([edge, moved[:, LANES:]], axis=1)
    edge = jnp.where(lane == LANES - 1, jnp.zeros_like(moved[:, -LANES:]), moved[:, -LANES:])
    return jnp.concatenate([moved[:, :-LANES], edge], axis=1)


def score_kernel(
    anchor_ref, low_ref, volume_ref, high_ref, lift_ref, bias_ref, wa_ref, wb_ref, wr_ref,
    out_ref, ext_ref, ring_a, ring_b, ring_c, h0_ref, h1_ref, *, height,
):
    rows, width = out_ref.shape
    ext_ref[6:8] = low_ref[...]
    ext_ref[8 : 8 + rows] = volume_ref[0]
    ext_ref[8 + rows : 16 + rows] = jnp.zeros((8, width), f32)
    ext_ref[8 + rows : 10 + rows] = high_ref[...]
    channels = lift_ref.shape[1]
    pairs = (rows + 2) // 2
    anchor = anchor_ref[0]
    tiles = width // LANES

    def lift(pair, ring):
        for k in range(2):
            row = 2 * pair + k
            place = anchor + row - 2
            keep = jnp.where((place >= 0) & (place < height), 1.0, 0.0).astype(f32)
            line = ext_ref[pl.ds(row + 6, 1), :]
            for c in range(0, channels, 16):
                gain = jnp.concatenate([lift_ref[0, c : c + 16] * keep] * tiles, axis=1)
                base = jnp.concatenate([lift_ref[1, c : c + 16] * keep] * tiles, axis=1)
                z = gain * line + base
                h = (z * jnp.tanh(z) + z).astype(bf16)
                at = k * channels + c
                ring[0, at : at + 16] = shifted(h, -1)
                ring[1, at : at + 16] = h
                ring[2, at : at + 16] = shifted(h, 1)
                h0_ref[pl.ds(pl.multiple_of(row * channels + c, 16), 16), :] = h

    def step(g, p0, p1, p2):
        lift(g + 2, p2)
        for n in range(0, width, 256):
            rhs = jnp.concatenate([r[j, :, n : n + 256] for j in range(3) for r in (p0, p1)], axis=0)
            acc = jnp.dot(wa_ref[...], rhs, preferred_element_type=f32)
            z = acc + jnp.concatenate([bias_ref[...]] * 2, axis=1)
            h = (z * jnp.tanh(z) + z).astype(bf16)
            h1_ref[pl.ds(pl.multiple_of(g * 2 * channels, 128), 2 * channels), n : n + 256] = h

    lift(0, ring_a)
    lift(1, ring_b)

    def three(it, carry):
        g = it * 3
        step(g, ring_a, ring_b, ring_c)
        step(g + 1, ring_b, ring_c, ring_a)
        step(g + 2, ring_c, ring_a, ring_b)
        return carry

    lax.fori_loop(0, pairs // 3, three, 0)

    @pl.when(anchor == 0)
    def _():
        h1_ref[0:channels] = jnp.zeros((channels, width), bf16)

    @pl.when(anchor + rows == height)
    def _():
        h1_ref[(rows + 1) * channels : (rows + 2) * channels] = jnp.zeros((channels, width), bf16)

    def eight(t, carry):
        at = pl.multiple_of(t * 8 * channels, 128)
        conv = jnp.dot(wb_ref[...], h1_ref[pl.ds(at, 10 * channels), :], preferred_element_type=f32)
        kept = jnp.dot(wr_ref[...], h0_ref[pl.ds(at + 2 * channels, 8 * channels), :], preferred_element_type=f32)
        total = kept[0:8] + kept[8:16] + (conv[16:24] + conv[24:32])
        total = total + shifted(conv[0:8] + conv[8:16], -1)
        total = total + shifted(conv[32:40] + conv[40:48], 1)
        out_ref[pl.ds(pl.multiple_of(t * 8, 8), 8), :] = total
        return carry

    lax.fori_loop(0, rows // 8, eight, 0)


def data_kernel(spread_ref, offset_ref, cells_in_ref, measured_ref, out_ref, cells_ref, *scratch):
    rows, views, det = measured_ref.shape[1:]
    peers = cells_in_ref.shape[0]
    nx = cells_ref.shape[1]
    chunks = LANES // rows
    depth = rows // chunks
    blocks = nx // LANES
    back_ref, sum_ref = scratch[:2]
    sets = [scratch[2 + 3 * k : 5 + 3 * k] for k in range(2)]

    for tile in range(nx // LANES):
        pieces = []
        for peer in range(tile * chunks, (tile + 1) * chunks):
            got = cells_in_ref[peer].astype(f32)
            pieces += [got[:, k * rows : (k + 1) * rows] for k in range(chunks)]
        cells_ref[:, tile * LANES : (tile + 1) * LANES] = jnp.concatenate(pieces, axis=0).T.astype(bf16)

    back_ref[...] = jnp.zeros_like(back_ref)
    sum_ref[...] = jnp.zeros_like(sum_ref)
    for line_ref, low_ref, _ in sets:
        low_ref[...] = jnp.zeros_like(low_ref)

    lane = lax.broadcasted_iota(jnp.int32, (LANES, 2 * LANES), 1).astype(f32)
    cell = lax.broadcasted_iota(jnp.int32, (LANES, 2 * LANES), 0).astype(f32)

    def window(view, b):
        spread = spread_ref[0, view]
        offset = offset_ref[0, view].astype(f32)
        begin = (det - 1) * 0.5 + (b * LANES - (nx - 1) * 0.5) * spread + offset
        return (begin + LANES).astype(jnp.int32) // LANES * LANES

    def forward(view, line_ref, low_ref, tent_ref):
        spread = spread_ref[0, view]
        offset = offset_ref[0, view].astype(f32)
        line_ref[:, :LANES] = jnp.zeros((rows, LANES), f32)
        line_ref[:, LANES + det :] = jnp.zeros((rows, LANES), f32)
        line_ref[:, LANES : LANES + det] = -measured_ref[0, :, view, :]
        for b in range(blocks):
            first = window(view, b)
            target = (det - 1) * 0.5 + (cell + (b * LANES - (nx - 1) * 0.5)) * spread + offset
            bins = lane + (first - LANES).astype(f32)
            tent = jnp.maximum(0.0, 1.0 - jnp.abs(bins - target)).astype(bf16)
            tent_ref[b] = tent
            at = pl.ds(pl.multiple_of(first, LANES), 2 * LANES)
            line_ref[:, at] += jnp.dot(
                cells_ref[:, b * LANES : (b + 1) * LANES], tent, preferred_element_type=f32
            )
        misfit = line_ref[:, LANES : LANES + det]
        low_ref[:, LANES : LANES + det] = misfit.astype(bf16)
        square = misfit * misfit
        total = square[:, :LANES]
        for k in range(1, det // LANES):
            total = total + square[:, k * LANES : (k + 1) * LANES]
        sum_ref[...] += total

    def backward(view, line_ref, low_ref, tent_ref):
        for b in range(blocks):
            at = pl.ds(pl.multiple_of(window(view, b), LANES), 2 * LANES)
            back_ref[:, b * LANES : (b + 1) * LANES] += lax.dot_general(
                low_ref[:, at], tent_ref[b], (((1,), (1,)), ((), ())), preferred_element_type=f32
            )

    def two(it, carry):
        for k in range(2):
            forward(2 * it + k, *sets[k])
        for k in range(2):
            backward(2 * it + k, *sets[k])
        return carry

    lax.fori_loop(0, views // 2, two, 0)

    whole = jnp.sum(sum_ref[...], keepdims=True)
    high = whole.astype(bf16)
    rest = whole - high.astype(f32)
    middle = rest.astype(bf16)
    final = (rest - middle.astype(f32)).astype(bf16)
    spot = lax.broadcasted_iota(jnp.int32, (out_ref.shape[1] - depth, LANES), 1)
    note = jnp.where(spot == 0, high.astype(f32), 0.0)
    note = jnp.where(spot == 1, middle.astype(f32), note)
    note = jnp.where(spot == 2, final.astype(f32), note).astype(bf16)
    for tile in range(nx // LANES):
        turned = back_ref[:, tile * LANES : (tile + 1) * LANES].T
        for k in range(chunks):
            peer = tile * chunks + k
            own = turned[k * rows : (k + 1) * rows]
            wide = jnp.concatenate([own[i * depth : (i + 1) * depth] for i in range(chunks)], axis=1)
            out_ref[peer, :depth] = wide.astype(bf16)
            out_ref[peer, depth:] = note


def combine_kernel(step_ref, volume_ref, noise_ref, score_ref, back_ref, out_ref, *, count):
    rows, width = score_ref.shape
    peers = back_ref.shape[0]
    chunks = LANES // rows
    depth = rows // chunks
    total = jnp.zeros((1, LANES), f32)
    for peer in range(peers):
        total = total + back_ref[peer, depth : depth + 8].astype(f32)[0:1]
    misfit = jnp.sum(total, keepdims=True)
    step = jnp.full((1, 1), step_ref[0], f32)
    weight = data_gain / jnp.sqrt(misfit / count + 1e-06)
    sway = jnp.sqrt(2.0 * step)
    for tile in range(width // LANES):
        at = slice(tile * LANES, (tile + 1) * LANES)
        got = [back_ref[tile * chunks + k, :depth].astype(f32) for k in range(chunks)]
        back = jnp.concatenate(
            [jnp.concatenate([g[:, k * rows : (k + 1) * rows] for g in got], axis=1) for k in range(chunks)], axis=0
        )
        moved = step * (score_ref[:, at] - weight * back)
        out_ref[0, :, at] = volume_ref[0, :, at] + moved + sway * noise_ref[0, :, at]


def per_device(
    volume,
    noise,
    measured,
    angles,
    offsets,
    step_size,
    lift_w,
    lift_b,
    conv_a,
    bias_a,
    conv_b,
    out_w,
):
    slices, rows, width = volume.shape
    views, det = measured.shape[2:]
    channels = lift_w.shape[0]
    peers = lax.axis_size("slab")
    height = peers * rows
    chunks = LANES // rows
    depth = rows // chunks

    def call(kernel, mebibytes, **kwargs):
        return pl.pallas_call(
            kernel, compiler_params=pltpu.CompilerParams(vmem_limit_bytes=mebibytes << 20), **kwargs
        )

    def spec(shape, dtype):
        return jax.ShapeDtypeStruct(shape, dtype)

    payload, first, last = call(
        pack_kernel,
        2,
        out_shape=(spec((peers, depth, LANES), bf16), spec((2, width), f32), spec((2, width), f32)),
        in_specs=[VMEM],
        out_specs=(VMEM,) * 3,
    )(volume)
    cells = lax.all_to_all(payload, "slab", 0, 0)
    low = lax.ppermute(last, "slab", [(i, i + 1) for i in range(peers - 1)])
    high = lax.ppermute(first, "slab", [(i + 1, i) for i in range(peers - 1)])

    def line(array):
        return array.reshape(1, -1)

    wa, wb, wr, lift, bias, spread = call(
        prep_kernel,
        4,
        out_shape=(
            spec((2 * channels, 12 * channels), bf16),
            spec((48, 10 * channels), bf16),
            spec((16, 8 * channels), bf16),
            spec((2, channels, LANES), f32),
            spec((2 * channels, LANES), f32),
            spec((1, views), f32),
        ),
        in_specs=[VMEM] * 7,
        out_specs=(VMEM,) * 6,
    )(line(angles), line(lift_w), line(lift_b), conv_a, line(bias_a), conv_b, line(out_w))

    anchor = (lax.axis_index("slab") * rows).astype(jnp.int32).reshape(1)
    ring = pltpu.VMEM((3, 2 * channels, width), bf16)
    score = call(
        functools.partial(score_kernel, height=height),
        28,
        out_shape=spec((rows, width), f32),
        in_specs=[SMEM] + [VMEM] * 8,
        out_specs=VMEM,
        scratch_shapes=[
            pltpu.VMEM((rows + 16, width), f32),
            ring,
            ring,
            ring,
            pltpu.VMEM(((rows + 6) * channels, width), bf16),
            pltpu.VMEM(((rows + 2) * channels, width), bf16),
        ],
    )(anchor, low, volume, high, lift, bias, wa, wb, wr)

    nx = height
    wide = det + 2 * LANES
    lines = [
        pltpu.VMEM((rows, wide), f32),
        pltpu.VMEM((rows, wide), bf16),
        pltpu.VMEM((nx // LANES, LANES, 2 * LANES), bf16),
    ]
    sent = call(
        data_kernel,
        12,
        out_shape=spec((peers, depth + 8, LANES), bf16),
        in_specs=[SMEM] * 2 + [VMEM] * 2,
        out_specs=VMEM,
        scratch_shapes=[
            pltpu.VMEM((rows, nx), bf16),
            pltpu.VMEM((rows, nx), f32),
            pltpu.VMEM((rows, LANES), f32),
            *lines,
            *lines,
        ],
    )(spread, line(offsets), cells, measured)
    returned = lax.all_to_all(sent, "slab", 0, 0)
    return call(
        functools.partial(combine_kernel, count=slices * peers * rows * views * det),
        3,
        out_shape=spec(volume.shape, f32),
        in_specs=[SMEM] + [VMEM] * 4,
        out_specs=VMEM,
    )(step_size, volume, noise, score, returned)


def solution(mesh):
    placed = (
        P("groups", "slab", None),
        P("groups", "slab", None),
        P("groups", "slab", None, None),
        P("groups"),
        P("groups"),
        P("groups"),
        P(),
        P(),
        P(),
        P(),
        P(),
        P(),
    )
    return jax.shard_map(
        per_device, mesh=mesh, in_specs=placed, out_specs=P("groups", "slab", None), check_vma=False
    )
```

```python
import functools

import jax
import jax.numpy as jnp
from jax import lax
from jax.experimental import pallas as pl
from jax.experimental.pallas import tpu as pltpu
from jax.sharding import PartitionSpec as P


ANGLES = 180
LANES = 128

data_gain = 0.25

f32 = jnp.float32
bf16 = jnp.bfloat16
VMEM = pl.BlockSpec(memory_space=pltpu.VMEM)
SMEM = pl.BlockSpec(memory_space=pltpu.SMEM)
HBM = pl.BlockSpec(memory_space=pltpu.HBM)


def pack_kernel(volume_ref, out_ref, first_ref, last_ref):
    rows = volume_ref.shape[1]
    peers = out_ref.shape[0]
    chunks = LANES // rows
    depth = rows // chunks
    for peer in range(peers):
        piece = volume_ref[0, :, peer * rows : (peer + 1) * rows]
        wide = jnp.concatenate([piece[k * depth : (k + 1) * depth] for k in range(chunks)], axis=1)
        out_ref[peer] = wide.astype(bf16)
    first_ref[...] = volume_ref[0, :2, :]
    last_ref[...] = volume_ref[0, rows - 2 :, :]


def split(value):
    high = value.astype(bf16).astype(f32)
    return high, (value - high).astype(bf16).astype(f32)


def prep_kernel(*refs):
    sources, (wa_ref, wb_ref, wr_ref, lift_ref, shift_ref, spread_ref) = refs[:7], refs[7:13]
    held, sems = refs[13:20], refs[20]
    copies = [
        pltpu.make_async_copy(source, target, sems.at[k]) for k, (source, target) in enumerate(zip(sources, held))
    ]
    for copy in copies:
        copy.start()
    for copy in copies:
        copy.wait()
    angles_ref, gain_ref, base_ref, conv_a_ref, bias_ref, conv_b_ref, own_ref = held
    channels = conv_a_ref.shape[1]

    def column(row):
        return jnp.broadcast_to(row, (LANES, channels)).T

    lift_ref[0] = column(0.5 * gain_ref[...])
    lift_ref[1] = column(0.5 * base_ref[...])
    shift = column(0.5 * bias_ref[...])
    shift_ref[:channels] = shift
    shift_ref[channels:] = shift

    taps = [conv_a_ref[t].astype(f32) * 0.5 for t in range(9)]
    zero = jnp.zeros((channels, channels), f32)
    for r in range(2):
        for j in range(3):
            for e in range(0, 4, 2):
                pair = [taps[3 * (k - r) + j] if 0 <= k - r < 3 else zero for k in (e, e + 1)]
                at = (4 * j + e) * channels
                wa_ref[r * channels : (r + 1) * channels, at : at + 2 * channels] = jnp.concatenate(
                    pair, axis=1
                ).astype(bf16)

    own = column(own_ref[...])[:, :channels]
    row = lax.broadcasted_iota(jnp.int32, (8, LANES), 0)
    half = lax.broadcasted_iota(jnp.int32, (8, LANES), 1) // channels

    def both(line):
        return jnp.broadcast_to(jnp.concatenate([line, line], axis=1), (8, LANES))

    folded = [split(jnp.sum(own * conv_b_ref[t].astype(f32), axis=0, keepdims=True)) for t in range(9)]
    mine = split(own_ref[...])
    for q in range(5):
        at = slice(q * LANES, (q + 1) * LANES)
        for j in range(3):
            parts = []
            for s in range(2):
                block = jnp.zeros((8, LANES), f32)
                for i in range(3):
                    block = jnp.where(half + 2 * q - row == i, both(folded[3 * i + j][s]), block)
                parts.append(block)
            wb_ref[16 * j : 16 * j + 16, at] = jnp.concatenate(parts, axis=0).astype(bf16)
        if q < 4:
            parts = [jnp.where(half + 2 * q == row, both(mine[s]), 0.0) for s in range(2)]
            wr_ref[:, at] = jnp.concatenate(parts, axis=0).astype(bf16)

    level = jnp.abs(jnp.cos(jnp.pi * angles_ref[...].astype(f32) / ANGLES))
    spread_ref[...] = 0.6 + 0.4 * level


def shifted(block, step):
    width = block.shape[1]
    moved = pltpu.roll(block, (-step) % width, 1)
    lane = lax.broadcasted_iota(jnp.int32, (block.shape[0], LANES), 1)
    if step < 0:
        edge = jnp.where(lane == 0, jnp.zeros_like(moved[:, :LANES]), moved[:, :LANES])
        return jnp.concatenate([edge, moved[:, LANES:]], axis=1)
    edge = jnp.where(lane == LANES - 1, jnp.zeros_like(moved[:, -LANES:]), moved[:, -LANES:])
    return jnp.concatenate([moved[:, :-LANES], edge], axis=1)


def score_kernel(
    anchor_ref, low_ref, volume_ref, high_ref, lift_ref, bias_ref, wa_ref, wb_ref, wr_ref,
    out_ref, ext_ref, ring_a, ring_b, ring_c, h0_ref, h1_ref, *, height,
):
    rows, width = out_ref.shape
    ext_ref[6:8] = low_ref[...]
    ext_ref[8 : 8 + rows] = volume_ref[0]
    ext_ref[8 + rows : 16 + rows] = jnp.zeros((8, width), f32)
    ext_ref[8 + rows : 10 + rows] = high_ref[...]
    channels = lift_ref.shape[1]
    pairs = (rows + 2) // 2
    anchor = anchor_ref[0]
    tiles = width // LANES

    def lift(pair, ring):
        for k in range(2):
            row = 2 * pair + k
            place = anchor + row - 2
            keep = jnp.where((place >= 0) & (place < height), 1.0, 0.0).astype(f32)
            line = ext_ref[pl.ds(row + 6, 1), :]
            for c in range(0, channels, 16):
                gain = jnp.concatenate([lift_ref[0, c : c + 16] * keep] * tiles, axis=1)
                base = jnp.concatenate([lift_ref[1, c : c + 16] * keep] * tiles, axis=1)
                z = gain * line + base
                h = (z * jnp.tanh(z) + z).astype(bf16)
                at = k * channels + c
                ring[0, at : at + 16] = shifted(h, -1)
                ring[1, at : at + 16] = h
                ring[2, at : at + 16] = shifted(h, 1)
                h0_ref[pl.ds(pl.multiple_of(row * channels + c, 16), 16), :] = h

    def step(g, p0, p1, p2):
        lift(g + 2, p2)
        for n in range(0, width, 256):
            rhs = jnp.concatenate([r[j, :, n : n + 256] for j in range(3) for r in (p0, p1)], axis=0)
            acc = jnp.dot(wa_ref[...], rhs, preferred_element_type=f32)
            z = acc + jnp.concatenate([bias_ref[...]] * 2, axis=1)
            h = (z * jnp.tanh(z) + z).astype(bf16)
            h1_ref[pl.ds(pl.multiple_of(g * 2 * channels, 128), 2 * channels), n : n + 256] = h

    lift(0, ring_a)
    lift(1, ring_b)

    def three(it, carry):
        g = it * 3
        step(g, ring_a, ring_b, ring_c)
        step(g + 1, ring_b, ring_c, ring_a)
        step(g + 2, ring_c, ring_a, ring_b)
        return carry

    lax.fori_loop(0, pairs // 3, three, 0)

    @pl.when(anchor == 0)
    def _():
        h1_ref[0:channels] = jnp.zeros((channels, width), bf16)

    @pl.when(anchor + rows == height)
    def _():
        h1_ref[(rows + 1) * channels : (rows + 2) * channels] = jnp.zeros((channels, width), bf16)

    def eight(t, carry):
        at = pl.multiple_of(t * 8 * channels, 128)
        conv = jnp.dot(wb_ref[...], h1_ref[pl.ds(at, 10 * channels), :], preferred_element_type=f32)
        kept = jnp.dot(wr_ref[...], h0_ref[pl.ds(at + 2 * channels, 8 * channels), :], preferred_element_type=f32)
        total = kept[0:8] + kept[8:16] + (conv[16:24] + conv[24:32])
        total = total + shifted(conv[0:8] + conv[8:16], -1)
        total = total + shifted(conv[32:40] + conv[40:48], 1)
        out_ref[pl.ds(pl.multiple_of(t * 8, 8), 8), :] = total
        return carry

    lax.fori_loop(0, rows // 8, eight, 0)


def data_kernel(spread_ref, offset_ref, cells_in_ref, measured_ref, out_ref, cells_ref, *scratch):
    rows, views, det = measured_ref.shape[1:]
    nx = cells_ref.shape[1]
    chunks = LANES // rows
    depth = rows // chunks
    blocks = nx // LANES
    back_ref, sum_ref, seen_ref, sems = scratch[:4]
    sets = [scratch[4 + 3 * k : 7 + 3 * k] for k in range(2)]
    part = views // 2

    def fetch(k):
        span = pl.ds(k * part, part)
        return pltpu.make_async_copy(measured_ref.at[0, :, span], seen_ref.at[:, span], sems.at[k])

    fetch(0).start()
    fetch(1).start()

    for tile in range(nx // LANES):
        pieces = []
        for peer in range(tile * chunks, (tile + 1) * chunks):
            got = cells_in_ref[peer].astype(f32)
            pieces += [got[:, k * rows : (k + 1) * rows] for k in range(chunks)]
        cells_ref[:, tile * LANES : (tile + 1) * LANES] = jnp.concatenate(pieces, axis=0).T.astype(bf16)

    back_ref[...] = jnp.zeros_like(back_ref)
    sum_ref[...] = jnp.zeros_like(sum_ref)
    for line_ref, low_ref, _ in sets:
        low_ref[...] = jnp.zeros_like(low_ref)

    lane = lax.broadcasted_iota(jnp.int32, (LANES, 2 * LANES), 1).astype(f32)
    cell = lax.broadcasted_iota(jnp.int32, (LANES, 2 * LANES), 0).astype(f32)

    def window(view, b):
        spread = spread_ref[0, view]
        offset = offset_ref[0, view].astype(f32)
        begin = (det - 1) * 0.5 + (b * LANES - (nx - 1) * 0.5) * spread + offset
        return (begin + LANES).astype(jnp.int32) // LANES * LANES

    def forward(view, line_ref, low_ref, tent_ref):
        spread = spread_ref[0, view]
        offset = offset_ref[0, view].astype(f32)
        line_ref[:, :LANES] = jnp.zeros((rows, LANES), f32)
        line_ref[:, LANES + det :] = jnp.zeros((rows, LANES), f32)
        line_ref[:, LANES : LANES + det] = -seen_ref[:, view, :]
        for b in range(blocks):
            first = window(view, b)
            target = (det - 1) * 0.5 + (cell + (b * LANES - (nx - 1) * 0.5)) * spread + offset
            bins = lane + (first - LANES).astype(f32)
            tent = jnp.maximum(0.0, 1.0 - jnp.abs(bins - target)).astype(bf16)
            tent_ref[b] = tent
            at = pl.ds(pl.multiple_of(first, LANES), 2 * LANES)
            line_ref[:, at] += jnp.dot(
                cells_ref[:, b * LANES : (b + 1) * LANES], tent, preferred_element_type=f32
            )
        misfit = line_ref[:, LANES : LANES + det]
        low_ref[:, LANES : LANES + det] = misfit.astype(bf16)
        square = misfit * misfit
        total = square[:, :LANES]
        for k in range(1, det // LANES):
            total = total + square[:, k * LANES : (k + 1) * LANES]
        sum_ref[...] += total

    def backward(view, line_ref, low_ref, tent_ref):
        for b in range(blocks):
            at = pl.ds(pl.multiple_of(window(view, b), LANES), 2 * LANES)
            back_ref[:, b * LANES : (b + 1) * LANES] += lax.dot_general(
                low_ref[:, at], tent_ref[b], (((1,), (1,)), ((), ())), preferred_element_type=f32
            )

    def two(it, carry):
        for k in range(2):
            forward(2 * it + k, *sets[k])
        for k in range(2):
            backward(2 * it + k, *sets[k])
        return carry

    fetch(0).wait()
    lax.fori_loop(0, views // 4, two, 0)
    fetch(1).wait()
    lax.fori_loop(views // 4, views // 2, two, 0)

    whole = jnp.sum(sum_ref[...], keepdims=True)
    high = whole.astype(bf16)
    rest = whole - high.astype(f32)
    middle = rest.astype(bf16)
    final = (rest - middle.astype(f32)).astype(bf16)
    spot = lax.broadcasted_iota(jnp.int32, (out_ref.shape[1] - depth, LANES), 1)
    note = jnp.where(spot == 0, high.astype(f32), 0.0)
    note = jnp.where(spot == 1, middle.astype(f32), note)
    note = jnp.where(spot == 2, final.astype(f32), note).astype(bf16)
    for tile in range(nx // LANES):
        turned = back_ref[:, tile * LANES : (tile + 1) * LANES].T
        for k in range(chunks):
            peer = tile * chunks + k
            own = turned[k * rows : (k + 1) * rows]
            wide = jnp.concatenate([own[i * depth : (i + 1) * depth] for i in range(chunks)], axis=1)
            out_ref[peer, :depth] = wide.astype(bf16)
            out_ref[peer, depth:] = note


def combine_kernel(step_ref, volume_ref, noise_ref, score_ref, back_ref, out_ref, *, count):
    rows, width = score_ref.shape
    peers = back_ref.shape[0]
    chunks = LANES // rows
    depth = rows // chunks
    total = jnp.zeros((1, LANES), f32)
    for peer in range(peers):
        total = total + back_ref[peer, depth : depth + 8].astype(f32)[0:1]
    misfit = jnp.sum(total, keepdims=True)
    step = jnp.full((1, 1), step_ref[0], f32)
    weight = data_gain / jnp.sqrt(misfit / count + 1e-06)
    sway = jnp.sqrt(2.0 * step)
    for tile in range(width // LANES):
        at = slice(tile * LANES, (tile + 1) * LANES)
        got = [back_ref[tile * chunks + k, :depth].astype(f32) for k in range(chunks)]
        back = jnp.concatenate(
            [jnp.concatenate([g[:, k * rows : (k + 1) * rows] for g in got], axis=1) for k in range(chunks)], axis=0
        )
        moved = step * (score_ref[:, at] - weight * back)
        out_ref[0, :, at] = volume_ref[0, :, at] + moved + sway * noise_ref[0, :, at]


def per_device(
    volume,
    noise,
    measured,
    angles,
    offsets,
    step_size,
    lift_w,
    lift_b,
    conv_a,
    bias_a,
    conv_b,
    out_w,
):
    slices, rows, width = volume.shape
    views, det = measured.shape[2:]
    channels = lift_w.shape[0]
    peers = lax.axis_size("slab")
    height = peers * rows
    chunks = LANES // rows
    depth = rows // chunks

    def call(kernel, mebibytes, **kwargs):
        return pl.pallas_call(
            kernel, compiler_params=pltpu.CompilerParams(vmem_limit_bytes=mebibytes << 20), **kwargs
        )

    def spec(shape, dtype):
        return jax.ShapeDtypeStruct(shape, dtype)

    payload, first, last = call(
        pack_kernel,
        2,
        out_shape=(spec((peers, depth, LANES), bf16), spec((2, width), f32), spec((2, width), f32)),
        in_specs=[VMEM],
        out_specs=(VMEM,) * 3,
    )(volume)
    cells = lax.all_to_all(payload, "slab", 0, 0)
    low = lax.ppermute(last, "slab", [(i, i + 1) for i in range(peers - 1)])
    high = lax.ppermute(first, "slab", [(i + 1, i) for i in range(peers - 1)])

    def line(array):
        return array.reshape(1, -1)

    small = (line(angles), line(lift_w), line(lift_b), conv_a, line(bias_a), conv_b, line(out_w))
    wa, wb, wr, lift, bias, spread = call(
        prep_kernel,
        6,
        out_shape=(
            spec((2 * channels, 12 * channels), bf16),
            spec((48, 10 * channels), bf16),
            spec((16, 8 * channels), bf16),
            spec((2, channels, LANES), f32),
            spec((2 * channels, LANES), f32),
            spec((1, views), f32),
        ),
        in_specs=[HBM] * 7,
        out_specs=(VMEM,) * 6,
        scratch_shapes=[pltpu.VMEM(a.shape, a.dtype) for a in small] + [pltpu.SemaphoreType.DMA((7,))],
    )(*[pltpu.with_memory_space_constraint(a, pltpu.HBM) for a in small])

    nx = height
    wide = det + 2 * LANES
    lines = [
        pltpu.VMEM((rows, wide), f32),
        pltpu.VMEM((rows, wide), bf16),
        pltpu.VMEM((nx // LANES, LANES, 2 * LANES), bf16),
    ]
    sent = call(
        data_kernel,
        12,
        out_shape=spec((peers, depth + 8, LANES), bf16),
        in_specs=[SMEM] * 2 + [VMEM, HBM],
        out_specs=VMEM,
        scratch_shapes=[
            pltpu.VMEM((rows, nx), bf16),
            pltpu.VMEM((rows, nx), f32),
            pltpu.VMEM((rows, LANES), f32),
            pltpu.VMEM((rows, views, det), f32),
            pltpu.SemaphoreType.DMA((2,)),
            *lines,
            *lines,
        ],
    )(spread, pltpu.with_memory_space_constraint(line(offsets), pltpu.HBM), cells, pltpu.with_memory_space_constraint(measured, pltpu.HBM))
    returned = lax.all_to_all(sent, "slab", 0, 0)

    anchor = (lax.axis_index("slab") * rows).astype(jnp.int32).reshape(1)
    ring = pltpu.VMEM((3, 2 * channels, width), bf16)
    score = call(
        functools.partial(score_kernel, height=height),
        28,
        out_shape=spec((rows, width), f32),
        in_specs=[SMEM] + [VMEM] * 8,
        out_specs=VMEM,
        scratch_shapes=[
            pltpu.VMEM((rows + 16, width), f32),
            ring,
            ring,
            ring,
            pltpu.VMEM(((rows + 6) * channels, width), bf16),
            pltpu.VMEM(((rows + 2) * channels, width), bf16),
        ],
    )(anchor, low, volume, high, lift, bias, wa, wb, wr)
    return call(
        functools.partial(combine_kernel, count=slices * peers * rows * views * det),
        3,
        out_shape=spec(volume.shape, f32),
        in_specs=[SMEM] + [VMEM] * 4,
        out_specs=VMEM,
    )(step_size, volume, noise, score, returned)


def solution(mesh):
    placed = (
        P("groups", "slab", None),
        P("groups", "slab", None),
        P("groups", "slab", None, None),
        P("groups"),
        P("groups"),
        P("groups"),
        P(),
        P(),
        P(),
        P(),
        P(),
        P(),
    )
    return jax.shard_map(
        per_device, mesh=mesh, in_specs=placed, out_specs=P("groups", "slab", None), check_vma=False
    )
```

```python
import functools

import jax
import jax.numpy as jnp
from jax import lax
from jax.experimental import pallas as pl
from jax.experimental.pallas import tpu as pltpu
from jax.sharding import PartitionSpec as P


ANGLES = 180
LANES = 128

data_gain = 0.25

f32 = jnp.float32
bf16 = jnp.bfloat16
VMEM = pl.BlockSpec(memory_space=pltpu.VMEM)
SMEM = pl.BlockSpec(memory_space=pltpu.SMEM)
HBM = pl.BlockSpec(memory_space=pltpu.HBM)


def pack_kernel(volume_ref, out_ref, first_ref, last_ref):
    rows = volume_ref.shape[1]
    peers = out_ref.shape[0]
    chunks = LANES // rows
    depth = rows // chunks
    for peer in range(peers):
        piece = volume_ref[0, :, peer * rows : (peer + 1) * rows]
        wide = jnp.concatenate([piece[k * depth : (k + 1) * depth] for k in range(chunks)], axis=1)
        out_ref[peer] = wide.astype(bf16)
    first_ref[...] = volume_ref[0, :2, :]
    last_ref[...] = volume_ref[0, rows - 2 :, :]


def split(value):
    high = value.astype(bf16).astype(f32)
    return high, (value - high).astype(bf16).astype(f32)


def prep_kernel(*refs):
    sources, (wa_ref, wb_ref, wr_ref, lift_ref, shift_ref, spread_ref) = refs[:7], refs[7:13]
    held, sems = refs[13:20], refs[20]
    copies = [
        pltpu.make_async_copy(source, target, sems.at[k]) for k, (source, target) in enumerate(zip(sources, held))
    ]
    for copy in copies:
        copy.start()
    for copy in copies:
        copy.wait()
    angles_ref, gain_ref, base_ref, conv_a_ref, bias_ref, conv_b_ref, own_ref = held
    channels = conv_a_ref.shape[1]

    def column(row):
        return jnp.broadcast_to(row, (LANES, channels)).T

    lift_ref[0] = column(0.5 * gain_ref[...])
    lift_ref[1] = column(0.5 * base_ref[...])
    shift = column(0.5 * bias_ref[...])
    shift_ref[:channels] = shift
    shift_ref[channels:] = shift

    taps = [conv_a_ref[t].astype(f32) * 0.5 for t in range(9)]
    zero = jnp.zeros((channels, channels), f32)
    for r in range(2):
        for j in range(3):
            for e in range(0, 4, 2):
                pair = [taps[3 * (k - r) + j] if 0 <= k - r < 3 else zero for k in (e, e + 1)]
                at = (4 * j + e) * channels
                wa_ref[r * channels : (r + 1) * channels, at : at + 2 * channels] = jnp.concatenate(
                    pair, axis=1
                ).astype(bf16)

    own = column(own_ref[...])[:, :channels]
    row = lax.broadcasted_iota(jnp.int32, (8, LANES), 0)
    half = lax.broadcasted_iota(jnp.int32, (8, LANES), 1) // channels

    def both(line):
        return jnp.broadcast_to(jnp.concatenate([line, line], axis=1), (8, LANES))

    folded = [split(jnp.sum(own * conv_b_ref[t].astype(f32), axis=0, keepdims=True)) for t in range(9)]
    mine = split(own_ref[...])
    for q in range(5):
        at = slice(q * LANES, (q + 1) * LANES)
        for j in range(3):
            parts = []
            for s in range(2):
                block = jnp.zeros((8, LANES), f32)
                for i in range(3):
                    block = jnp.where(half + 2 * q - row == i, both(folded[3 * i + j][s]), block)
                parts.append(block)
            wb_ref[16 * j : 16 * j + 16, at] = jnp.concatenate(parts, axis=0).astype(bf16)
        if q < 4:
            parts = [jnp.where(half + 2 * q == row, both(mine[s]), 0.0) for s in range(2)]
            wr_ref[:, at] = jnp.concatenate(parts, axis=0).astype(bf16)

    level = jnp.abs(jnp.cos(jnp.pi * angles_ref[...].astype(f32) / ANGLES))
    spread_ref[...] = 0.6 + 0.4 * level


def shifted(block, step):
    width = block.shape[1]
    moved = pltpu.roll(block, (-step) % width, 1)
    lane = lax.broadcasted_iota(jnp.int32, (block.shape[0], LANES), 1)
    if step < 0:
        edge = jnp.where(lane == 0, jnp.zeros_like(moved[:, :LANES]), moved[:, :LANES])
        return jnp.concatenate([edge, moved[:, LANES:]], axis=1)
    edge = jnp.where(lane == LANES - 1, jnp.zeros_like(moved[:, -LANES:]), moved[:, -LANES:])
    return jnp.concatenate([moved[:, :-LANES], edge], axis=1)


def score_kernel(
    anchor_ref, low_ref, volume_ref, high_ref, lift_ref, bias_ref, wa_ref, wb_ref, wr_ref,
    out_ref, ext_ref, ring_a, ring_b, ring_c, h0_ref, h1_ref, *, height,
):
    rows, width = out_ref.shape
    ext_ref[6:8] = low_ref[...]
    ext_ref[8 : 8 + rows] = volume_ref[0]
    ext_ref[8 + rows : 16 + rows] = jnp.zeros((8, width), f32)
    ext_ref[8 + rows : 10 + rows] = high_ref[...]
    channels = lift_ref.shape[1]
    pairs = (rows + 2) // 2
    anchor = anchor_ref[0]
    tiles = width // LANES

    def lift(pair, ring):
        for k in range(2):
            row = 2 * pair + k
            place = anchor + row - 2
            keep = jnp.where((place >= 0) & (place < height), 1.0, 0.0).astype(f32)
            line = ext_ref[pl.ds(row + 6, 1), :]
            for c in range(0, channels, 16):
                gain = jnp.concatenate([lift_ref[0, c : c + 16] * keep] * tiles, axis=1)
                base = jnp.concatenate([lift_ref[1, c : c + 16] * keep] * tiles, axis=1)
                z = gain * line + base
                h = (z * jnp.tanh(z) + z).astype(bf16)
                at = k * channels + c
                ring[0, at : at + 16] = shifted(h, -1)
                ring[1, at : at + 16] = h
                ring[2, at : at + 16] = shifted(h, 1)
                h0_ref[pl.ds(pl.multiple_of(row * channels + c, 16), 16), :] = h

    def step(g, p0, p1, p2):
        lift(g + 2, p2)
        for n in range(0, width, 256):
            rhs = jnp.concatenate([r[j, :, n : n + 256] for j in range(3) for r in (p0, p1)], axis=0)
            acc = jnp.dot(wa_ref[...], rhs, preferred_element_type=f32)
            z = acc + jnp.concatenate([bias_ref[...]] * 2, axis=1)
            h = (z * jnp.tanh(z) + z).astype(bf16)
            h1_ref[pl.ds(pl.multiple_of(g * 2 * channels, 128), 2 * channels), n : n + 256] = h

    lift(0, ring_a)
    lift(1, ring_b)

    def three(it, carry):
        g = it * 3
        step(g, ring_a, ring_b, ring_c)
        step(g + 1, ring_b, ring_c, ring_a)
        step(g + 2, ring_c, ring_a, ring_b)
        return carry

    lax.fori_loop(0, pairs // 3, three, 0)

    @pl.when(anchor == 0)
    def _():
        h1_ref[0:channels] = jnp.zeros((channels, width), bf16)

    @pl.when(anchor + rows == height)
    def _():
        h1_ref[(rows + 1) * channels : (rows + 2) * channels] = jnp.zeros((channels, width), bf16)

    def eight(t, carry):
        at = pl.multiple_of(t * 8 * channels, 128)
        conv = jnp.dot(wb_ref[...], h1_ref[pl.ds(at, 10 * channels), :], preferred_element_type=f32)
        kept = jnp.dot(wr_ref[...], h0_ref[pl.ds(at + 2 * channels, 8 * channels), :], preferred_element_type=f32)
        total = kept[0:8] + kept[8:16] + (conv[16:24] + conv[24:32])
        total = total + shifted(conv[0:8] + conv[8:16], -1)
        total = total + shifted(conv[32:40] + conv[40:48], 1)
        out_ref[pl.ds(pl.multiple_of(t * 8, 8), 8), :] = total
        return carry

    lax.fori_loop(0, rows // 8, eight, 0)


def data_kernel(spread_ref, offset_ref, cells_in_ref, measured_ref, out_ref, cells_ref, back_ref, sum_ref, bin_ref, line_ref, sems, *scratch):
    rows, views, det = measured_ref.shape[1:]
    nx = cells_ref.shape[1]
    chunks = LANES // rows
    depth = rows // chunks
    blocks = nx // LANES
    sets = [scratch[2 * k : 2 * k + 2] for k in range(len(scratch) // 2)]
    body = slice(LANES, LANES + det)

    def fetch(view):
        return pltpu.make_async_copy(measured_ref.at[0, :, view], line_ref.at[view, :, body], sems.at[view])

    for view in range(views):
        fetch(view).start()

    for tile in range(nx // LANES):
        pieces = []
        for peer in range(tile * chunks, (tile + 1) * chunks):
            got = cells_in_ref[peer].astype(f32)
            pieces += [got[:, k * rows : (k + 1) * rows] for k in range(chunks)]
        cells_ref[:, tile * LANES : (tile + 1) * LANES] = (-jnp.concatenate(pieces, axis=0).T).astype(bf16)

    back_ref[...] = jnp.zeros_like(back_ref)
    sum_ref[...] = jnp.zeros_like(sum_ref)
    bin_ref[...] = lax.broadcasted_iota(jnp.int32, bin_ref.shape, 0).astype(jnp.int16)
    line_ref[:, :, :LANES] = jnp.zeros((views, rows, LANES), f32)
    line_ref[:, :, LANES + det :] = jnp.zeros((views, rows, LANES), f32)
    for low_ref, _ in sets:
        low_ref[...] = jnp.zeros_like(low_ref)

    cell = lax.broadcasted_iota(jnp.int32, (16, LANES), 1).astype(f32)

    def forward(view, low_ref, tent_ref):
        spread = spread_ref[0, view]
        offset = offset_ref[0, view].astype(f32)
        windows = []
        for b in range(blocks):
            begin = (det - 1) * 0.5 + (b * LANES - (nx - 1) * 0.5) * spread + offset
            first = jnp.floor(begin * (1.0 / LANES))
            at = pl.ds(pl.multiple_of((first.astype(jnp.int32) + 1) * LANES, LANES), 2 * LANES)
            windows.append(at)
            target = cell * spread + (begin - first * LANES)
            under = jnp.floor(target)
            near = (1.0 - (target - under)).astype(bf16)
            far = (1.0 - ((under + 1.0) - target)).astype(bf16)
            spot = under.astype(jnp.int32)
            this = jnp.concatenate([spot.astype(jnp.int16)] * 16, axis=0)
            after = jnp.concatenate([(spot + 1).astype(jnp.int16)] * 16, axis=0)
            near = jnp.concatenate([near] * 16, axis=0)
            far = jnp.concatenate([far] * 16, axis=0)
            bins = bin_ref[...]
            tent = jnp.where(bins == this, near, jnp.where(bins == after, far, jnp.zeros_like(far)))
            tent_ref[b] = tent
            line_ref[view, :, at] += lax.dot_general(
                cells_ref[:, b * LANES : (b + 1) * LANES],
                tent,
                (((1,), (1,)), ((), ())),
                preferred_element_type=f32,
            )
        misfit = line_ref[view, :, body]
        low_ref[:, body] = misfit.astype(bf16)
        square = misfit * misfit
        total = square[:, :LANES]
        for k in range(1, det // LANES):
            total = total + square[:, k * LANES : (k + 1) * LANES]
        sum_ref[...] += total
        return windows

    def backward(windows, low_ref, tent_ref):
        for b, at in enumerate(windows):
            back_ref[:, b * LANES : (b + 1) * LANES] += jnp.dot(
                low_ref[:, at], tent_ref[b], preferred_element_type=f32
            )

    def several(it, carry):
        for k in range(len(sets)):
            fetch(len(sets) * it + k).wait()
        windows = [forward(len(sets) * it + k, *sets[k]) for k in range(len(sets))]
        for k in range(len(sets)):
            backward(windows[k], *sets[k])
        return carry

    lax.fori_loop(0, views // len(sets), several, 0)

    whole = jnp.sum(sum_ref[...], keepdims=True)
    high = whole.astype(bf16)
    rest = whole - high.astype(f32)
    middle = rest.astype(bf16)
    final = (rest - middle.astype(f32)).astype(bf16)
    spot = lax.broadcasted_iota(jnp.int32, (out_ref.shape[1] - depth, LANES), 1)
    note = jnp.where(spot == 0, high.astype(f32), 0.0)
    note = jnp.where(spot == 1, middle.astype(f32), note)
    note = jnp.where(spot == 2, final.astype(f32), note).astype(bf16)
    for tile in range(nx // LANES):
        turned = back_ref[:, tile * LANES : (tile + 1) * LANES].T
        for k in range(chunks):
            peer = tile * chunks + k
            own = turned[k * rows : (k + 1) * rows]
            wide = jnp.concatenate([own[i * depth : (i + 1) * depth] for i in range(chunks)], axis=1)
            out_ref[peer, :depth] = wide.astype(bf16)
            out_ref[peer, depth:] = note


def combine_kernel(step_ref, volume_ref, noise_ref, score_ref, back_ref, out_ref, *, count):
    rows, width = score_ref.shape
    peers = back_ref.shape[0]
    chunks = LANES // rows
    depth = rows // chunks
    total = jnp.zeros((1, LANES), f32)
    for peer in range(peers):
        total = total + back_ref[peer, depth : depth + 8].astype(f32)[0:1]
    misfit = jnp.sum(total, keepdims=True)
    step = jnp.full((1, 1), step_ref[0], f32)
    weight = data_gain / jnp.sqrt(misfit / count + 1e-06)
    sway = jnp.sqrt(2.0 * step)
    for tile in range(width // LANES):
        at = slice(tile * LANES, (tile + 1) * LANES)
        got = [back_ref[tile * chunks + k, :depth].astype(f32) for k in range(chunks)]
        back = jnp.concatenate(
            [jnp.concatenate([g[:, k * rows : (k + 1) * rows] for g in got], axis=1) for k in range(chunks)], axis=0
        )
        moved = step * (score_ref[:, at] + weight * back)
        out_ref[0, :, at] = volume_ref[0, :, at] + moved + sway * noise_ref[0, :, at]


def per_device(
    volume,
    noise,
    measured,
    angles,
    offsets,
    step_size,
    lift_w,
    lift_b,
    conv_a,
    bias_a,
    conv_b,
    out_w,
):
    slices, rows, width = volume.shape
    views, det = measured.shape[2:]
    channels = lift_w.shape[0]
    peers = lax.axis_size("slab")
    height = peers * rows
    chunks = LANES // rows
    depth = rows // chunks

    def call(kernel, mebibytes, **kwargs):
        return pl.pallas_call(
            kernel, compiler_params=pltpu.CompilerParams(vmem_limit_bytes=mebibytes << 20), **kwargs
        )

    def spec(shape, dtype):
        return jax.ShapeDtypeStruct(shape, dtype)

    payload, first, last = call(
        pack_kernel,
        2,
        out_shape=(spec((peers, depth, LANES), bf16), spec((2, width), f32), spec((2, width), f32)),
        in_specs=[VMEM],
        out_specs=(VMEM,) * 3,
    )(volume)
    cells = lax.all_to_all(payload, "slab", 0, 0)
    low = lax.ppermute(last, "slab", [(i, i + 1) for i in range(peers - 1)])
    high = lax.ppermute(first, "slab", [(i + 1, i) for i in range(peers - 1)])

    def line(array):
        return array.reshape(1, -1)

    small = (line(angles), line(lift_w), line(lift_b), conv_a, line(bias_a), conv_b, line(out_w))
    wa, wb, wr, lift, bias, spread = call(
        prep_kernel,
        6,
        out_shape=(
            spec((2 * channels, 12 * channels), bf16),
            spec((48, 10 * channels), bf16),
            spec((16, 8 * channels), bf16),
            spec((2, channels, LANES), f32),
            spec((2 * channels, LANES), f32),
            spec((1, views), f32),
        ),
        in_specs=[HBM] * 7,
        out_specs=(VMEM,) * 6,
        scratch_shapes=[pltpu.VMEM(a.shape, a.dtype) for a in small] + [pltpu.SemaphoreType.DMA((7,))],
    )(*[pltpu.with_memory_space_constraint(a, pltpu.HBM) for a in small])

    nx = height
    wide = det + 2 * LANES
    lines = [
        pltpu.VMEM((rows, wide), bf16),
        pltpu.VMEM((nx // LANES, 2 * LANES, LANES), bf16),
    ]
    sent = call(
        data_kernel,
        12,
        out_shape=spec((peers, depth + 8, LANES), bf16),
        in_specs=[SMEM] * 2 + [VMEM, HBM],
        out_specs=VMEM,
        scratch_shapes=[
            pltpu.VMEM((rows, nx), bf16),
            pltpu.VMEM((rows, nx), f32),
            pltpu.VMEM((rows, LANES), f32),
            pltpu.VMEM((2 * LANES, LANES), jnp.int16),
            pltpu.VMEM((views, rows, wide), f32),
            pltpu.SemaphoreType.DMA((views,)),
            *lines,
            *lines,
        ],
    )(spread, pltpu.with_memory_space_constraint(line(offsets), pltpu.HBM), cells, pltpu.with_memory_space_constraint(measured, pltpu.HBM))
    returned = lax.all_to_all(sent, "slab", 0, 0)

    anchor = (lax.axis_index("slab") * rows).astype(jnp.int32).reshape(1)
    ring = pltpu.VMEM((3, 2 * channels, width), bf16)
    score = call(
        functools.partial(score_kernel, height=height),
        28,
        out_shape=spec((rows, width), f32),
        in_specs=[SMEM] + [VMEM] * 8,
        out_specs=VMEM,
        scratch_shapes=[
            pltpu.VMEM((rows + 16, width), f32),
            ring,
            ring,
            ring,
            pltpu.VMEM(((rows + 6) * channels, width), bf16),
            pltpu.VMEM(((rows + 2) * channels, width), bf16),
        ],
    )(anchor, low, volume, high, lift, bias, wa, wb, wr)
    return call(
        functools.partial(combine_kernel, count=slices * peers * rows * views * det),
        3,
        out_shape=spec(volume.shape, f32),
        in_specs=[SMEM] + [VMEM] * 4,
        out_specs=VMEM,
    )(step_size, volume, noise, score, returned)


def solution(mesh):
    placed = (
        P("groups", "slab", None),
        P("groups", "slab", None),
        P("groups", "slab", None, None),
        P("groups"),
        P("groups"),
        P("groups"),
        P(),
        P(),
        P(),
        P(),
        P(),
        P(),
    )
    return jax.shard_map(
        per_device, mesh=mesh, in_specs=placed, out_specs=P("groups", "slab", None), check_vma=False
    )
```

```python
import functools

import jax
import jax.numpy as jnp
from jax import lax
from jax.experimental import pallas as pl
from jax.experimental.pallas import tpu as pltpu
from jax.sharding import PartitionSpec as P


ANGLES = 180
LANES = 128
GROUP = 16

data_gain = 0.25

f32 = jnp.float32
bf16 = jnp.bfloat16
VMEM = pl.BlockSpec(memory_space=pltpu.VMEM)
SMEM = pl.BlockSpec(memory_space=pltpu.SMEM)
HBM = pl.BlockSpec(memory_space=pltpu.HBM)


def split(value, pieces=2):
    parts = []
    for _ in range(pieces):
        parts.append(value.astype(bf16).astype(f32))
        value = value - parts[-1]
    return parts


def pack_kernel(volume_ref, out_ref):
    rows = volume_ref.shape[1]
    peers = out_ref.shape[0]
    chunks = LANES // rows
    depth = rows // chunks
    edge = jnp.concatenate([volume_ref[0, :2], volume_ref[0, rows - 2 :]], axis=0)
    _, middle, final = split(edge, 3)
    blank = [jnp.zeros((4, LANES - 2 * rows), f32)] if 2 * rows < LANES else []
    none = jnp.zeros((4, LANES), f32)
    for peer in range(peers):
        at = slice(peer * rows, (peer + 1) * rows)
        piece = volume_ref[0, :, at]
        wide = jnp.concatenate([piece[k * depth : (k + 1) * depth] for k in range(chunks)], axis=1)
        out_ref[peer, :depth] = wide.astype(bf16)
        lower = jnp.concatenate([middle[:, at], final[:, at]] + blank, axis=1)
        out_ref[peer, depth:] = jnp.concatenate([lower, none], axis=0).astype(bf16)


def prep_kernel(*refs):
    sources, (wa_ref, wb_ref, wr_ref, lift_ref, shift_ref, spread_ref) = refs[:7], refs[7:13]
    held, sems = refs[13:20], refs[20]
    copies = [
        pltpu.make_async_copy(source, target, sems.at[k]) for k, (source, target) in enumerate(zip(sources, held))
    ]
    for copy in copies:
        copy.start()
    for copy in copies:
        copy.wait()
    angles_ref, gain_ref, base_ref, conv_a_ref, bias_ref, conv_b_ref, own_ref = held
    channels = conv_a_ref.shape[1]

    def column(row):
        return jnp.broadcast_to(row, (LANES, channels)).T

    lift_ref[0] = column(0.5 * gain_ref[...])
    lift_ref[1] = column(0.5 * base_ref[...])
    shift = column(0.5 * bias_ref[...])
    shift_ref[:channels] = shift
    shift_ref[channels:] = shift

    taps = [conv_a_ref[t].astype(f32) * 0.5 for t in range(9)]
    zero = jnp.zeros((channels, channels), f32)
    for r in range(2):
        for j in range(3):
            for e in range(0, 4, 2):
                pair = [taps[3 * (k - r) + j] if 0 <= k - r < 3 else zero for k in (e, e + 1)]
                at = (4 * j + e) * channels
                wa_ref[r * channels : (r + 1) * channels, at : at + 2 * channels] = jnp.concatenate(
                    pair, axis=1
                ).astype(bf16)

    own = column(own_ref[...])[:, :channels]
    row = lax.broadcasted_iota(jnp.int32, (GROUP, LANES), 0)
    half = lax.broadcasted_iota(jnp.int32, (GROUP, LANES), 1) // channels

    def both(line):
        return jnp.broadcast_to(jnp.concatenate([line, line], axis=1), (GROUP, LANES))

    folded = [split(jnp.sum(own * conv_b_ref[t].astype(f32), axis=0, keepdims=True)) for t in range(9)]
    mine = split(own_ref[...])
    for q in range(GROUP // 2 + 1):
        at = slice(q * LANES, (q + 1) * LANES)
        for j in range(3):
            for s in range(2):
                block = jnp.zeros((GROUP, LANES), f32)
                for i in range(3):
                    block = jnp.where(half + 2 * q - row == i, both(folded[3 * i + j][s]), block)
                first = (2 * j + s) * GROUP
                wb_ref[first : first + GROUP, at] = block.astype(bf16)
        if q < GROUP // 2:
            for s in range(2):
                block = jnp.where(half + 2 * q == row, both(mine[s]), 0.0)
                wr_ref[s * GROUP : (s + 1) * GROUP, at] = block.astype(bf16)

    level = jnp.abs(jnp.cos(jnp.pi * angles_ref[...].astype(f32) / ANGLES))
    spread_ref[...] = 0.6 + 0.4 * level


def shifted(block, step):
    width = block.shape[1]
    moved = pltpu.roll(block, (-step) % width, 1)
    lane = lax.broadcasted_iota(jnp.int32, (block.shape[0], LANES), 1)
    if step < 0:
        edge = jnp.where(lane == 0, jnp.zeros_like(moved[:, :LANES]), moved[:, :LANES])
        return jnp.concatenate([edge, moved[:, LANES:]], axis=1)
    edge = jnp.where(lane == LANES - 1, jnp.zeros_like(moved[:, -LANES:]), moved[:, -LANES:])
    return jnp.concatenate([moved[:, :-LANES], edge], axis=1)


def lifted(line, lift_ref, ring, at, kept_ref=None, kept_at=None, keep=None):
    channels = lift_ref.shape[1]
    tiles = line.shape[1] // LANES
    for c in range(0, channels, 16):
        gain, base = lift_ref[0, c : c + 16], lift_ref[1, c : c + 16]
        if keep is not None:
            gain, base = gain * keep, base * keep
        z = jnp.concatenate([gain] * tiles, axis=1) * line + jnp.concatenate([base] * tiles, axis=1)
        h = (z * jnp.tanh(z) + z).astype(bf16)
        ring[0, at + c : at + c + 16] = shifted(h, -1)
        ring[1, at + c : at + c + 16] = h
        ring[2, at + c : at + c + 16] = shifted(h, 1)
        if kept_ref is not None:
            kept_ref[pl.ds(pl.multiple_of(kept_at + c, 16), 16), :] = h


def convolved(p0, p1, wa_ref, bias_ref, store):
    width = p0.shape[2]
    for n in range(0, width, 256):
        rhs = jnp.concatenate([r[j, :, n : n + 256] for j in range(3) for r in (p0, p1)], axis=0)
        acc = jnp.dot(wa_ref[...], rhs, preferred_element_type=f32)
        z = acc + jnp.concatenate([bias_ref[...]] * 2, axis=1)
        store(slice(n, n + 256), (z * jnp.tanh(z) + z).astype(bf16))


def projected(h1, h0, wb_ref, wr_ref):
    conv = jnp.dot(wb_ref[:, : h1.shape[0]], h1, preferred_element_type=f32)
    kept = jnp.dot(wr_ref[:, : h0.shape[0]], h0, preferred_element_type=f32)
    taps = [conv[2 * j * GROUP : (2 * j + 1) * GROUP] + conv[(2 * j + 1) * GROUP : (2 * j + 2) * GROUP] for j in range(3)]
    total = kept[:GROUP] + kept[GROUP:] + taps[1]
    return total + shifted(taps[0], -1) + shifted(taps[2], 1)


def score_kernel(*refs, begin, count):
    given, refs = refs[: 1 if begin else 0], refs[1 if begin else 0 :]
    volume_ref, lift_ref, bias_ref, wa_ref, wb_ref, wr_ref, out_ref, edge_ref = refs[:8]
    last_ref, refs = (refs[8], refs[9:]) if not begin else (None, refs[8:])
    ring_a, ring_b, ring_c, h0_ref, h1_ref = refs
    rings = (ring_a, ring_b, ring_c)
    channels = lift_ref.shape[1]
    lead = 2 * channels if begin else 0

    def lift(pair, ring):
        for k in range(2):
            row = 2 * pair + k
            line = volume_ref[0, pl.ds(2 * begin + row, 1), :]
            lifted(line, lift_ref, ring, k * channels, h0_ref, row * channels)

    def step(g, p0, p1, p2):
        if p2 is not None:
            lift(g + 2, p2)

        def store(at, h):
            h1_ref[pl.ds(pl.multiple_of(lead + g * 2 * channels, 128), 2 * channels), at] = h

        convolved(p0, p1, wa_ref, bias_ref, store)

    lift(0, ring_a)
    lift(1, ring_b)
    if begin:
        h1_ref[:lead] = given[0][...]

    def three(it, carry):
        for k in range(3):
            step(it * 3 + k, *[rings[(k + i) % 3] for i in range(3)])
        return carry

    lax.fori_loop(0, count // 3, three, 0)
    for k in range(count % 3):
        assert k == count % 3 - 1
        step(count - 1, rings[k], rings[k + 1], None)

    low = 2 * begin if begin else 2
    high = 2 * (begin + count)
    for row in range(low, high, GROUP):
        size = min(GROUP, high - row)
        at = (row - low) * channels
        own = (row - 2 * begin) * channels
        total = projected(h1_ref[at : at + (size + 2) * channels], h0_ref[own : own + size * channels], wb_ref, wr_ref)
        out_ref[row : row + size] = total[:size]

    total = (2 * count) * channels + lead
    if begin:
        edge_ref[...] = h1_ref[total - 2 * channels : total]
    else:
        edge_ref[...] = h1_ref[: 2 * channels]
        last_ref[...] = h1_ref[total - 2 * channels : total]


def data_kernel(spread_ref, offset_ref, cells_in_ref, measured_ref, out_ref, cells_ref, back_ref, sum_ref, line_ref, sems, *scratch):
    rows, views, det = measured_ref.shape[1:]
    peers = cells_in_ref.shape[0]
    nx = cells_ref.shape[1]
    chunks = LANES // rows
    depth = rows // chunks
    blocks = nx // LANES
    sets = [scratch[2 * k : 2 * k + 2] for k in range(len(scratch) // 2)]
    body = slice(LANES, LANES + det)

    def fetch(view):
        return pltpu.make_async_copy(measured_ref.at[0, :, view], line_ref.at[view, :, body], sems.at[view])

    for view in range(views):
        fetch(view).start()

    for tile in range(nx // LANES):
        pieces = []
        for peer in range(tile * chunks, (tile + 1) * chunks):
            got = cells_in_ref[peer, :depth].astype(f32)
            pieces += [got[:, k * rows : (k + 1) * rows] for k in range(chunks)]
        cells_ref[:, tile * LANES : (tile + 1) * LANES] = (-jnp.concatenate(pieces, axis=0).T).astype(bf16)

    back_ref[...] = jnp.zeros_like(back_ref)
    sum_ref[...] = jnp.zeros_like(sum_ref)
    line_ref[:, :, :LANES] = jnp.zeros((views, rows, LANES), f32)
    line_ref[:, :, LANES + det :] = jnp.zeros((views, rows, LANES), f32)
    for low_ref, _ in sets:
        low_ref[...] = jnp.zeros_like(low_ref)

    cell = lax.broadcasted_iota(jnp.int32, (16, LANES), 1).astype(f32)
    place = lax.broadcasted_iota(jnp.int32, (16, LANES), 0)
    bins = jnp.concatenate([(place + 16 * k).astype(jnp.int16) for k in range(16)], axis=0)

    def forward(view, low_ref, tent_ref):
        spread = spread_ref[0, view]
        offset = offset_ref[0, view].astype(f32)
        windows = []
        for b in range(blocks):
            begin = (det - 1) * 0.5 + (b * LANES - (nx - 1) * 0.5) * spread + offset
            first = jnp.floor(begin * (1.0 / LANES))
            at = pl.ds(pl.multiple_of((first.astype(jnp.int32) + 1) * LANES, LANES), 2 * LANES)
            windows.append(at)
            target = cell * spread + (begin - first * LANES)
            under = jnp.floor(target)
            near = (1.0 - (target - under)).astype(bf16)
            far = (1.0 - ((under + 1.0) - target)).astype(bf16)
            spot = under.astype(jnp.int32)
            this = jnp.concatenate([spot.astype(jnp.int16)] * 16, axis=0)
            after = jnp.concatenate([(spot + 1).astype(jnp.int16)] * 16, axis=0)
            near = jnp.concatenate([near] * 16, axis=0)
            far = jnp.concatenate([far] * 16, axis=0)
            tent = jnp.where(bins == this, near, jnp.where(bins == after, far, jnp.zeros_like(far)))
            tent_ref[b] = tent
            line_ref[view, :, at] += lax.dot_general(
                cells_ref[:, b * LANES : (b + 1) * LANES],
                tent,
                (((1,), (1,)), ((), ())),
                preferred_element_type=f32,
            )
        misfit = line_ref[view, :, body]
        low_ref[:, body] = misfit.astype(bf16)
        square = misfit * misfit
        total = square[:, :LANES]
        for k in range(1, det // LANES):
            total = total + square[:, k * LANES : (k + 1) * LANES]
        sum_ref[...] += total
        return windows

    def backward(windows, low_ref, tent_ref):
        for b, at in enumerate(windows):
            back_ref[:, b * LANES : (b + 1) * LANES] += jnp.dot(
                low_ref[:, at], tent_ref[b], preferred_element_type=f32
            )

    def several(it, carry):
        for k in range(len(sets)):
            fetch(len(sets) * it + k).wait()
        windows = [forward(len(sets) * it + k, *sets[k]) for k in range(len(sets))]
        for k in range(len(sets)):
            backward(windows[k], *sets[k])
        return carry

    lax.fori_loop(0, views // len(sets), several, 0)

    whole = split(jnp.sum(sum_ref[...], keepdims=True), 3)
    lane = lax.broadcasted_iota(jnp.int32, (8, LANES), 1)
    third = lax.broadcasted_iota(jnp.int32, (8, LANES), 0) == 2
    got = [cells_in_ref[peer].astype(f32) for peer in range(peers)]
    for peer in range(peers):
        low, high = got[max(peer - 1, 0)], got[min(peer + 1, peers - 1)]
        note = jnp.concatenate(
            [low[depth - 2 : depth], high[:2], low[depth + 2 : depth + 4], high[depth : depth + 2]], axis=0
        )
        for k in range(3):
            note = jnp.where(third & (lane == rows + k), whole[k], note)
        out_ref[peer, depth:] = note.astype(bf16)
    for tile in range(nx // LANES):
        turned = back_ref[:, tile * LANES : (tile + 1) * LANES].T
        for k in range(chunks):
            peer = tile * chunks + k
            own = turned[k * rows : (k + 1) * rows]
            wide = jnp.concatenate([own[i * depth : (i + 1) * depth] for i in range(chunks)], axis=1)
            out_ref[peer, :depth] = wide.astype(bf16)


def finish_kernel(
    step_ref, anchor_ref, volume_ref, noise_ref, one_ref, two_ref, back_ref, head_ref, tail_ref, lift_ref, bias_ref,
    wa_ref, wb_ref, wr_ref, out_ref, ext_ref, ring_a, ring_b, h1_ref, score_ref, *, count, height, border,
):
    rows, width = score_ref.shape
    channels = lift_ref.shape[1]
    peers = back_ref.shape[0]
    chunks = LANES // rows
    depth = rows // chunks
    anchor = anchor_ref[0]

    tails = [back_ref[peer, depth:].astype(f32) for peer in range(peers)]
    lane = lax.broadcasted_iota(jnp.int32, (8, LANES), 1)
    third = lax.broadcasted_iota(jnp.int32, (8, LANES), 0) == 2
    total = tails[0]
    for tail in tails[1:]:
        total = total + tail
    misfit = jnp.sum(jnp.where(third & (lane >= rows) & (lane < rows + 3), total, 0.0), keepdims=True)

    ext_ref[2:4] = volume_ref[0, :2]
    ext_ref[8:10] = volume_ref[0, rows - 2 :]
    for tile in range(width // LANES):
        mine = tails[tile * chunks : (tile + 1) * chunks]
        upper = [t[0:2, LANES - rows :] for t in mine], [t[2:4, :rows] for t in mine]
        for side, target in ((0, 0), (1, 10)):
            parts = [upper[side]] + [
                [t[4 + 2 * side : 6 + 2 * side, k * rows : (k + 1) * rows] for t in mine] for k in range(2)
            ]
            parts = [jnp.concatenate(p, axis=1) for p in parts]
            ext_ref[target : target + 2, tile * LANES : (tile + 1) * LANES] = parts[0] + parts[1] + parts[2]

    score_ref[:border] = one_ref[:border]
    score_ref[border:] = two_ref[border:]
    inside = jnp.where(anchor > 0, 1.0, 0.0).astype(f32), jnp.where(anchor + rows < height, 1.0, 0.0).astype(f32)
    for side in range(2):
        for k in range(4):
            line = ext_ref[8 * side + k : 8 * side + k + 1, :]
            halo = (k < 2) == (side == 0)
            ring = (ring_a, ring_b)[k // 2]
            lifted(line, lift_ref, ring, (k % 2) * channels, keep=inside[side] if halo else None)

        def store(at, h):
            h1_ref[2 * channels * side : 2 * channels * (side + 1), at] = h

        convolved(ring_a, ring_b, wa_ref, bias_ref, store)
        if side == 0:
            h1_ref[2 * channels :] = head_ref[...]

            @pl.when(anchor == 0)
            def _():
                h1_ref[:channels] = jnp.zeros((channels, width), bf16)
        else:
            h1_ref[: 2 * channels] = tail_ref[...]

            @pl.when(anchor + rows == height)
            def _():
                h1_ref[3 * channels :] = jnp.zeros((channels, width), bf16)

        scores = projected(h1_ref[...], (ring_b, ring_a)[side][1], wb_ref, wr_ref)
        at = (rows - 2) * side
        score_ref[at : at + 2] = scores[:2]

    step = jnp.full((1, 1), step_ref[0], f32)
    weight = data_gain / jnp.sqrt(misfit / count + 1e-06)
    sway = jnp.sqrt(2.0 * step)
    for tile in range(width // LANES):
        at = slice(tile * LANES, (tile + 1) * LANES)
        got = [back_ref[tile * chunks + k, :depth].astype(f32) for k in range(chunks)]
        back = jnp.concatenate(
            [jnp.concatenate([g[:, k * rows : (k + 1) * rows] for g in got], axis=1) for k in range(chunks)], axis=0
        )
        moved = step * (score_ref[:, at] + weight * back)
        out_ref[0, :, at] = volume_ref[0, :, at] + moved + sway * noise_ref[0, :, at]


def per_device(
    volume,
    noise,
    measured,
    angles,
    offsets,
    step_size,
    lift_w,
    lift_b,
    conv_a,
    bias_a,
    conv_b,
    out_w,
):
    slices, rows, width = volume.shape
    views, det = measured.shape[2:]
    channels = lift_w.shape[0]
    peers = lax.axis_size("slab")
    height = peers * rows
    chunks = LANES // rows
    depth = rows // chunks

    def call(kernel, mebibytes, **kwargs):
        return pl.pallas_call(
            kernel, compiler_params=pltpu.CompilerParams(vmem_limit_bytes=mebibytes << 20), **kwargs
        )

    def spec(shape, dtype):
        return jax.ShapeDtypeStruct(shape, dtype)

    def line(array):
        return array.reshape(1, -1)

    def apart(array):
        return pltpu.with_memory_space_constraint(array, pltpu.HBM)

    nx = height
    wide = det + 2 * LANES
    pairs = rows // 2 - 1
    half = pairs // 6 * 3
    ring = pltpu.VMEM((3, 2 * channels, width), bf16)
    pair = spec((2 * channels, width), bf16)
    anchor = (lax.axis_index("slab") * rows).astype(jnp.int32).reshape(1)
    small = (line(angles), line(lift_w), line(lift_b), conv_a, line(bias_a), conv_b, line(out_w))

    def score_part(begin, count, *args):
        return call(
            functools.partial(score_kernel, begin=begin, count=count),
            20,
            out_shape=(spec((rows, width), f32), pair) + (() if begin else (pair,)),
            in_specs=[VMEM] * len(args),
            out_specs=(VMEM,) * (2 if begin else 3),
            scratch_shapes=[
                ring,
                ring,
                ring,
                pltpu.VMEM(((2 * count + 4) * channels, width), bf16),
                pltpu.VMEM(((2 * count + 2) * channels, width), bf16),
            ],
        )(*args)

    payload = call(
        pack_kernel, 2, out_shape=spec((peers, depth + 8, LANES), bf16), in_specs=[VMEM], out_specs=VMEM
    )(volume)
    cells = lax.all_to_all(payload, "slab", 0, 0)
    wa, wb, wr, lift, bias, spread = call(
        prep_kernel,
        6,
        out_shape=(
            spec((2 * channels, 12 * channels), bf16),
            spec((6 * GROUP, (GROUP + 2) * channels), bf16),
            spec((2 * GROUP, GROUP * channels), bf16),
            spec((2, channels, LANES), f32),
            spec((2 * channels, LANES), f32),
            spec((1, views), f32),
        ),
        in_specs=[HBM] * 7,
        out_specs=(VMEM,) * 6,
        scratch_shapes=[pltpu.VMEM(a.shape, a.dtype) for a in small] + [pltpu.SemaphoreType.DMA((7,))],
    )(*[apart(a) for a in small])
    consts = (lift, bias, wa, wb, wr)
    one, head, middle = score_part(0, half, volume, *consts)

    lines = [
        pltpu.VMEM((rows, wide), bf16),
        pltpu.VMEM((nx // LANES, 2 * LANES, LANES), bf16),
    ]
    sent = call(
        data_kernel,
        12,
        out_shape=spec((peers, depth + 8, LANES), bf16),
        in_specs=[SMEM] * 2 + [VMEM, HBM],
        out_specs=VMEM,
        scratch_shapes=[
            pltpu.VMEM((rows, nx), bf16),
            pltpu.VMEM((rows, nx), f32),
            pltpu.VMEM((rows, LANES), f32),
            pltpu.VMEM((views, rows, wide), f32),
            pltpu.SemaphoreType.DMA((views,)),
            *lines,
            *lines,
        ],
    )(spread, apart(line(offsets)), cells, apart(measured))
    returned = lax.all_to_all(sent, "slab", 0, 0)
    two, tail = score_part(half, pairs - half, middle, volume, *consts)
    return call(
        functools.partial(finish_kernel, count=slices * peers * rows * views * det, height=height, border=2 * half),
        12,
        out_shape=spec(volume.shape, f32),
        in_specs=[SMEM] * 2 + [VMEM] * 12,
        out_specs=VMEM,
        scratch_shapes=[
            pltpu.VMEM((16, width), f32),
            ring,
            ring,
            pltpu.VMEM((4 * channels, width), bf16),
            pltpu.VMEM((rows, width), f32),
        ],
    )(step_size, anchor, volume, noise, one, two, returned, head, tail, *consts)


def solution(mesh):
    placed = (
        P("groups", "slab", None),
        P("groups", "slab", None),
        P("groups", "slab", None, None),
        P("groups"),
        P("groups"),
        P("groups"),
        P(),
        P(),
        P(),
        P(),
        P(),
        P(),
    )
    return jax.shard_map(
        per_device, mesh=mesh, in_specs=placed, out_specs=P("groups", "slab", None), check_vma=False
    )
```

```python
import functools

import jax
import jax.numpy as jnp
from jax import lax
from jax.experimental import pallas as pl
from jax.experimental.pallas import tpu as pltpu
from jax.sharding import PartitionSpec as P


ANGLES = 180
LANES = 128
GROUP = 16
TURN = 5
SETS = 4

data_gain = 0.25

f32 = jnp.float32
bf16 = jnp.bfloat16
VMEM = pl.BlockSpec(memory_space=pltpu.VMEM)
SMEM = pl.BlockSpec(memory_space=pltpu.SMEM)
HBM = pl.BlockSpec(memory_space=pltpu.HBM)


def split(value, pieces=2):
    parts = []
    for _ in range(pieces):
        parts.append(value.astype(bf16).astype(f32))
        value = value - parts[-1]
    return parts


def pack_kernel(*refs):
    count = (len(refs) - 2) // 2
    sources, out_ref, held, sems = refs[:count], refs[count], refs[count + 1 : -1], refs[-1]
    copies = [
        pltpu.make_async_copy(source, target, sems.at[k]) for k, (source, target) in enumerate(zip(sources, held))
    ]
    for copy in copies:
        copy.start()
    copies[0].wait()
    volume_ref = held[0]
    rows = volume_ref.shape[1]
    peers = out_ref.shape[0]
    chunks = LANES // rows
    depth = rows // chunks
    edge = jnp.concatenate([volume_ref[0, :2], volume_ref[0, rows - 2 :]], axis=0)
    _, middle, final = split(edge, 3)
    blank = [jnp.zeros((4, LANES - 2 * rows), f32)] if 2 * rows < LANES else []
    none = jnp.zeros((4, LANES), f32)
    for peer in range(peers):
        at = slice(peer * rows, (peer + 1) * rows)
        piece = volume_ref[0, :, at]
        wide = jnp.concatenate([piece[k * depth : (k + 1) * depth] for k in range(chunks)], axis=1)
        out_ref[peer, :depth] = wide.astype(bf16)
        lower = jnp.concatenate([middle[:, at], final[:, at]] + blank, axis=1)
        out_ref[peer, depth:] = jnp.concatenate([lower, none], axis=0).astype(bf16)
    for copy in copies[1:]:
        copy.wait()


def prep_kernel(
    angles_ref, offsets_ref, gain_ref, base_ref, conv_a_ref, bias_ref, conv_b_ref, own_ref,
    wa_ref, wb_ref, wr_ref, lift_ref, shift_ref, table_ref,
):
    channels = conv_a_ref.shape[1]

    def column(row):
        return jnp.broadcast_to(row, (LANES, channels)).T

    lift_ref[0] = column(0.5 * gain_ref[...])
    lift_ref[1] = column(0.5 * base_ref[...])
    shift = column(0.5 * bias_ref[...])
    shift_ref[:channels] = shift
    shift_ref[channels:] = shift

    taps = [conv_a_ref[t].astype(f32) * 0.5 for t in range(9)]
    zero = jnp.zeros((channels, channels), f32)
    for r in range(2):
        for j in range(3):
            for e in range(0, 4, 2):
                pair = [taps[3 * (k - r) + j] if 0 <= k - r < 3 else zero for k in (e, e + 1)]
                at = (4 * j + e) * channels
                wa_ref[r * channels : (r + 1) * channels, at : at + 2 * channels] = jnp.concatenate(
                    pair, axis=1
                ).astype(bf16)

    own = column(own_ref[...])[:, :channels]
    row = lax.broadcasted_iota(jnp.int32, (GROUP, LANES), 0)
    half = lax.broadcasted_iota(jnp.int32, (GROUP, LANES), 1) // channels

    def both(line):
        return jnp.broadcast_to(jnp.concatenate([line, line], axis=1), (GROUP, LANES))

    folded = [split(jnp.sum(own * conv_b_ref[t].astype(f32), axis=0, keepdims=True)) for t in range(9)]
    mine = split(own_ref[...])
    for q in range(GROUP // 2 + 1):
        at = slice(q * LANES, (q + 1) * LANES)
        for j in range(3):
            for s in range(2):
                block = jnp.zeros((GROUP, LANES), f32)
                for i in range(3):
                    block = jnp.where(half + 2 * q - row == i, both(folded[3 * i + j][s]), block)
                first = (2 * j + s) * GROUP
                wb_ref[first : first + GROUP, at] = block.astype(bf16)
        if q < GROUP // 2:
            for s in range(2):
                block = jnp.where(half + 2 * q == row, both(mine[s]), 0.0)
                wr_ref[s * GROUP : (s + 1) * GROUP, at] = block.astype(bf16)

    level = jnp.abs(jnp.cos(jnp.pi * angles_ref[...].astype(f32) / ANGLES))
    table_ref[0:1] = 0.6 + 0.4 * level
    table_ref[1:2] = offsets_ref[...].astype(f32)


def shifted(block, step):
    width = block.shape[1]
    moved = pltpu.roll(block, (-step) % width, 1)
    lane = lax.broadcasted_iota(jnp.int32, (block.shape[0], LANES), 1)
    if step < 0:
        edge = jnp.where(lane == 0, jnp.zeros_like(moved[:, :LANES]), moved[:, :LANES])
        return jnp.concatenate([edge, moved[:, LANES:]], axis=1)
    edge = jnp.where(lane == LANES - 1, jnp.zeros_like(moved[:, -LANES:]), moved[:, -LANES:])
    return jnp.concatenate([moved[:, :-LANES], edge], axis=1)


def lifted(line, lift_ref, ring, at, kept_ref=None, kept_at=None, keep=None):
    channels = lift_ref.shape[1]
    tiles = line.shape[1] // LANES
    for c in range(0, channels, 16):
        gain, base = lift_ref[0, c : c + 16], lift_ref[1, c : c + 16]
        if keep is not None:
            gain, base = gain * keep, base * keep
        z = jnp.concatenate([gain] * tiles, axis=1) * line + jnp.concatenate([base] * tiles, axis=1)
        h = (z * jnp.tanh(z) + z).astype(bf16)
        ring[0, at + c : at + c + 16] = shifted(h, -1)
        ring[1, at + c : at + c + 16] = h
        ring[2, at + c : at + c + 16] = shifted(h, 1)
        if kept_ref is not None:
            kept_ref[pl.ds(pl.multiple_of(kept_at + c, 16), 16), :] = h


def convolved(p0, p1, wa_ref, bias_ref, store):
    width = p0.shape[2]
    for n in range(0, width, 256):
        rhs = jnp.concatenate([r[j, :, n : n + 256] for j in range(3) for r in (p0, p1)], axis=0)
        acc = jnp.dot(wa_ref[...], rhs, preferred_element_type=f32)
        z = acc + jnp.concatenate([bias_ref[...]] * 2, axis=1)
        store(slice(n, n + 256), (z * jnp.tanh(z) + z).astype(bf16))


def projected(h1, h0, wb_ref, wr_ref):
    conv = jnp.dot(wb_ref[:, : h1.shape[0]], h1, preferred_element_type=f32)
    kept = jnp.dot(wr_ref[:, : h0.shape[0]], h0, preferred_element_type=f32)
    taps = [conv[2 * j * GROUP : (2 * j + 1) * GROUP] + conv[(2 * j + 1) * GROUP : (2 * j + 2) * GROUP] for j in range(3)]
    total = kept[:GROUP] + kept[GROUP:] + taps[1]
    return total + shifted(taps[0], -1) + shifted(taps[2], 1)


def score_kernel(*refs, begin, count):
    given, refs = refs[: 1 if begin else 0], refs[1 if begin else 0 :]
    volume_ref, lift_ref, bias_ref, wa_ref, wb_ref, wr_ref, out_ref, edge_ref = refs[:8]
    last_ref, refs = (refs[8], refs[9:]) if not begin else (None, refs[8:])
    rings, (h0_ref, h1_ref) = refs[:-2], refs[-2:]
    turn = len(rings)
    channels = lift_ref.shape[1]
    lead = 2 * channels if begin else 0

    def lift(pair, ring):
        for k in range(2):
            row = 2 * pair + k
            line = volume_ref[0, pl.ds(2 * begin + row, 1), :]
            lifted(line, lift_ref, ring, k * channels, h0_ref, row * channels)

    def step(g, p0, p1, p2):
        if p2 is not None:
            lift(g + 2, p2)

        def store(at, h):
            h1_ref[pl.ds(pl.multiple_of(lead + g * 2 * channels, 128), 2 * channels), at] = h

        convolved(p0, p1, wa_ref, bias_ref, store)

    lift(0, rings[0])
    lift(1, rings[1])
    if begin:
        h1_ref[:lead] = given[0][...]

    def several(it, carry):
        for k in range(turn):
            step(it * turn + k, *[rings[(k + i) % turn] for i in range(3)])
        return carry

    lax.fori_loop(0, count // turn, several, 0)
    for k in range(count % turn):
        last = k == count % turn - 1
        step(count - count % turn + k, rings[k], rings[(k + 1) % turn], None if last else rings[(k + 2) % turn])

    low = 2 * begin if begin else 2
    high = 2 * (begin + count)
    for row in range(low, high, GROUP):
        size = min(GROUP, high - row)
        at = (row - low) * channels
        own = (row - 2 * begin) * channels
        total = projected(h1_ref[at : at + (size + 2) * channels], h0_ref[own : own + size * channels], wb_ref, wr_ref)
        out_ref[row : row + size] = total[:size]

    total = (2 * count) * channels + lead
    if begin:
        edge_ref[...] = h1_ref[total - 2 * channels : total]
    else:
        edge_ref[...] = h1_ref[: 2 * channels]
        last_ref[...] = h1_ref[total - 2 * channels : total]


def data_kernel(table_ref, cells_in_ref, measured_ref, out_ref, cells_ref, back_ref, sum_ref, line_ref, sems, *scratch):
    rows, views, det = measured_ref.shape[1:]
    peers = cells_in_ref.shape[0]
    nx = cells_ref.shape[1]
    chunks = LANES // rows
    depth = rows // chunks
    blocks = nx // LANES
    sets = [scratch[2 * k : 2 * k + 2] for k in range(len(scratch) // 2)]
    body = slice(LANES, LANES + det)

    def fetch(view):
        return pltpu.make_async_copy(measured_ref.at[0, :, view], line_ref.at[view, :, body], sems.at[view])

    for view in range(views):
        fetch(view).start()

    for tile in range(nx // LANES):
        pieces = []
        for peer in range(tile * chunks, (tile + 1) * chunks):
            got = cells_in_ref[peer, :depth].astype(f32)
            pieces += [got[:, k * rows : (k + 1) * rows] for k in range(chunks)]
        cells_ref[:, tile * LANES : (tile + 1) * LANES] = (-jnp.concatenate(pieces, axis=0).T).astype(bf16)

    back_ref[...] = jnp.zeros_like(back_ref)
    sum_ref[...] = jnp.zeros_like(sum_ref)
    for low_ref, _ in sets:
        low_ref[...] = jnp.zeros_like(low_ref)

    cell = lax.broadcasted_iota(jnp.int32, (16, LANES), 1).astype(f32)
    place = lax.broadcasted_iota(jnp.int32, (16, LANES), 0)
    bins = jnp.concatenate([(place + 16 * k).astype(jnp.int16) for k in range(16)], axis=0)

    def window(view, b):
        begin = (det - 1) * 0.5 + (b * LANES - (nx - 1) * 0.5) * table_ref[0, view] + table_ref[1, view]
        first = jnp.floor(begin * (1.0 / LANES))
        at = pl.ds(pl.multiple_of((first.astype(jnp.int32) + 1) * LANES, LANES), 2 * LANES)
        return at, begin - first * LANES

    def forward(view, low_ref, tent_ref):
        for b in range(blocks):
            at, begin = window(view, b)
            target = cell * table_ref[0, view] + begin
            under = jnp.floor(target)
            near = (1.0 - (target - under)).astype(bf16)
            far = (1.0 - ((under + 1.0) - target)).astype(bf16)
            spot = under.astype(jnp.int32)
            this = jnp.concatenate([spot.astype(jnp.int16)] * 16, axis=0)
            after = jnp.concatenate([(spot + 1).astype(jnp.int16)] * 16, axis=0)
            near = jnp.concatenate([near] * 16, axis=0)
            far = jnp.concatenate([far] * 16, axis=0)
            tent = jnp.where(bins == this, near, jnp.where(bins == after, far, jnp.zeros_like(far)))
            tent_ref[b] = tent
            line_ref[view, :, at] += lax.dot_general(
                cells_ref[:, b * LANES : (b + 1) * LANES],
                tent,
                (((1,), (1,)), ((), ())),
                preferred_element_type=f32,
            )
        misfit = line_ref[view, :, body]
        low_ref[:, body] = misfit.astype(bf16)
        square = misfit * misfit
        total = square[:, :LANES]
        for k in range(1, det // LANES):
            total = total + square[:, k * LANES : (k + 1) * LANES]
        sum_ref[...] += total

    def backward(view, low_ref, tent_ref):
        for b in range(blocks):
            at, _ = window(view, b)
            back_ref[:, b * LANES : (b + 1) * LANES] += jnp.dot(
                low_ref[:, at], tent_ref[b], preferred_element_type=f32
            )

    turn = len(sets)
    lead = turn // 2
    rounds = (views - lead) // turn
    for view in range(lead):
        fetch(view).wait()
    for view in range(lead):
        forward(view, *sets[view])

    def several(it, carry):
        for k in range(turn):
            fetch(it * turn + lead + k).wait()
        for k in range(turn):
            forward(it * turn + lead + k, *sets[(lead + k) % turn])
            backward(it * turn + k, *sets[k])
        return carry

    lax.fori_loop(0, rounds, several, 0)
    for view in range(rounds * turn + lead, views):
        fetch(view).wait()
    for view in range(rounds * turn, views):
        if view + lead < views:
            forward(view + lead, *sets[(view + lead) % turn])
        backward(view, *sets[view % turn])

    whole = split(jnp.sum(sum_ref[...], keepdims=True), 3)
    lane = lax.broadcasted_iota(jnp.int32, (8, LANES), 1)
    third = lax.broadcasted_iota(jnp.int32, (8, LANES), 0) == 2
    got = [cells_in_ref[peer].astype(f32) for peer in range(peers)]
    for peer in range(peers):
        low, high = got[max(peer - 1, 0)], got[min(peer + 1, peers - 1)]
        note = jnp.concatenate(
            [low[depth - 2 : depth], high[:2], low[depth + 2 : depth + 4], high[depth : depth + 2]], axis=0
        )
        for k in range(3):
            note = jnp.where(third & (lane == rows + k), whole[k], note)
        out_ref[peer, depth:] = note.astype(bf16)
    for tile in range(nx // LANES):
        turned = back_ref[:, tile * LANES : (tile + 1) * LANES].T
        for k in range(chunks):
            peer = tile * chunks + k
            own = turned[k * rows : (k + 1) * rows]
            wide = jnp.concatenate([own[i * depth : (i + 1) * depth] for i in range(chunks)], axis=1)
            out_ref[peer, :depth] = wide.astype(bf16)


def finish_kernel(
    anchor_ref, step_ref, volume_ref, noise_ref, one_ref, two_ref, back_ref, head_ref, tail_ref, lift_ref, bias_ref,
    wa_ref, wb_ref, wr_ref, out_ref, ext_ref, ring_a, ring_b, h1_ref, score_ref, *, count, height, border,
):
    rows, width = score_ref.shape
    channels = lift_ref.shape[1]
    peers = back_ref.shape[0]
    chunks = LANES // rows
    depth = rows // chunks
    anchor = anchor_ref[0]

    tails = [back_ref[peer, depth:].astype(f32) for peer in range(peers)]
    lane = lax.broadcasted_iota(jnp.int32, (8, LANES), 1)
    third = lax.broadcasted_iota(jnp.int32, (8, LANES), 0) == 2
    total = tails[0]
    for tail in tails[1:]:
        total = total + tail
    misfit = jnp.sum(jnp.where(third & (lane >= rows) & (lane < rows + 3), total, 0.0), keepdims=True)

    ext_ref[2:4] = volume_ref[0, :2]
    ext_ref[8:10] = volume_ref[0, rows - 2 :]
    for tile in range(width // LANES):
        mine = tails[tile * chunks : (tile + 1) * chunks]
        upper = [t[0:2, LANES - rows :] for t in mine], [t[2:4, :rows] for t in mine]
        for side, target in ((0, 0), (1, 10)):
            parts = [upper[side]] + [
                [t[4 + 2 * side : 6 + 2 * side, k * rows : (k + 1) * rows] for t in mine] for k in range(2)
            ]
            parts = [jnp.concatenate(p, axis=1) for p in parts]
            ext_ref[target : target + 2, tile * LANES : (tile + 1) * LANES] = parts[0] + parts[1] + parts[2]

    score_ref[:border] = one_ref[:border]
    score_ref[border:] = two_ref[border:]
    inside = jnp.where(anchor > 0, 1.0, 0.0).astype(f32), jnp.where(anchor + rows < height, 1.0, 0.0).astype(f32)
    for side in range(2):
        for k in range(4):
            line = ext_ref[8 * side + k : 8 * side + k + 1, :]
            halo = (k < 2) == (side == 0)
            ring = (ring_a, ring_b)[k // 2]
            lifted(line, lift_ref, ring, (k % 2) * channels, keep=inside[side] if halo else None)

        def store(at, h):
            h1_ref[2 * channels * side : 2 * channels * (side + 1), at] = h

        convolved(ring_a, ring_b, wa_ref, bias_ref, store)
        if side == 0:
            h1_ref[2 * channels :] = head_ref[...]

            @pl.when(anchor == 0)
            def _():
                h1_ref[:channels] = jnp.zeros((channels, width), bf16)
        else:
            h1_ref[: 2 * channels] = tail_ref[...]

            @pl.when(anchor + rows == height)
            def _():
                h1_ref[3 * channels :] = jnp.zeros((channels, width), bf16)

        scores = projected(h1_ref[...], (ring_b, ring_a)[side][1], wb_ref, wr_ref)
        at = (rows - 2) * side
        score_ref[at : at + 2] = scores[:2]

    step = step_ref[...].reshape(1, 1)
    weight = data_gain / jnp.sqrt(misfit / count + 1e-06)
    sway = jnp.sqrt(2.0 * step)
    for tile in range(width // LANES):
        at = slice(tile * LANES, (tile + 1) * LANES)
        got = [back_ref[tile * chunks + k, :depth].astype(f32) for k in range(chunks)]
        back = jnp.concatenate(
            [jnp.concatenate([g[:, k * rows : (k + 1) * rows] for g in got], axis=1) for k in range(chunks)], axis=0
        )
        moved = step * (score_ref[:, at] + weight * back)
        out_ref[0, :, at] = volume_ref[0, :, at] + moved + sway * noise_ref[0, :, at]


def call(kernel, mebibytes, **kwargs):
    params = pltpu.CompilerParams(vmem_limit_bytes=mebibytes << 20)
    return pl.pallas_call(kernel, compiler_params=params, **kwargs)


def spec(shape, dtype):
    return jax.ShapeDtypeStruct(shape, dtype)


def apart(array):
    return pltpu.with_memory_space_constraint(array, pltpu.HBM)


def data_call(table, cells, measured):
    rows, views, det = measured.shape[1:]
    peers = cells.shape[0]
    nx = peers * rows
    wide = det + 2 * LANES
    lines = [
        pltpu.VMEM((rows, wide), bf16),
        pltpu.VMEM((nx // LANES, 2 * LANES, LANES), bf16),
    ]
    return call(
        data_kernel,
        12,
        out_shape=spec((peers, rows * rows // LANES + 8, LANES), bf16),
        in_specs=[SMEM, VMEM, HBM],
        out_specs=VMEM,
        scratch_shapes=[
            pltpu.VMEM((rows, nx), bf16),
            pltpu.VMEM((rows, nx), f32),
            pltpu.VMEM((rows, LANES), f32),
            pltpu.VMEM((views, rows, wide), f32),
            pltpu.SemaphoreType.DMA((views,)),
            *lines * SETS,
        ],
    )(table, cells, apart(measured))


def per_device(
    volume,
    noise,
    measured,
    angles,
    offsets,
    step_size,
    lift_w,
    lift_b,
    conv_a,
    bias_a,
    conv_b,
    out_w,
):
    slices, rows, width = volume.shape
    views, det = measured.shape[2:]
    channels = lift_w.shape[0]
    peers = lax.axis_size("slab")
    height = peers * rows
    chunks = LANES // rows
    depth = rows // chunks

    def line(array):
        return array.reshape(1, -1)

    pairs = rows // 2 - 1
    half = pairs // 2
    ring = pltpu.VMEM((3, 2 * channels, width), bf16)
    pair = spec((2 * channels, width), bf16)
    anchor = (lax.axis_index("slab") * rows).astype(jnp.int32).reshape(1)
    small = (volume, line(angles), line(offsets), line(lift_w), line(lift_b), conv_a, line(bias_a), conv_b, line(out_w))

    def score_part(begin, count, *args):
        return call(
            functools.partial(score_kernel, begin=begin, count=count),
            24,
            out_shape=(spec((rows, width), f32), pair) + (() if begin else (pair,)),
            in_specs=[VMEM] * len(args),
            out_specs=(VMEM,) * (2 if begin else 3),
            scratch_shapes=[
                *[ring] * min(TURN, half),
                pltpu.VMEM(((2 * count + 4) * channels, width), bf16),
                pltpu.VMEM(((2 * count + 2) * channels, width), bf16),
            ],
        )(*args)

    payload, volume, *small = call(
        pack_kernel,
        4,
        out_shape=(spec((peers, depth + 8, LANES), bf16),) + tuple(spec(a.shape, a.dtype) for a in small),
        in_specs=[HBM] * len(small),
        out_specs=(VMEM,) * (len(small) + 1),
        scratch_shapes=[pltpu.SemaphoreType.DMA((len(small),))],
    )(*[apart(a) for a in small])
    cells = lax.all_to_all(payload, "slab", 0, 0)
    wa, wb, wr, lift, bias, table = call(
        prep_kernel,
        6,
        out_shape=(
            spec((2 * channels, 12 * channels), bf16),
            spec((6 * GROUP, (GROUP + 2) * channels), bf16),
            spec((2 * GROUP, GROUP * channels), bf16),
            spec((2, channels, LANES), f32),
            spec((2 * channels, LANES), f32),
            spec((2, views), f32),
        ),
        in_specs=[VMEM] * 8,
        out_specs=(VMEM,) * 6,
    )(*small)
    consts = (lift, bias, wa, wb, wr)
    one, head, middle = score_part(0, half, volume, *consts)

    sent = data_call(table, cells, measured)
    returned = lax.all_to_all(sent, "slab", 0, 0)
    two, tail = score_part(half, pairs - half, middle, volume, *consts)
    return call(
        functools.partial(finish_kernel, count=slices * peers * rows * views * det, height=height, border=2 * half),
        12,
        out_shape=spec(volume.shape, f32),
        in_specs=[SMEM] + [VMEM] * 13,
        out_specs=VMEM,
        scratch_shapes=[
            pltpu.VMEM((16, width), f32),
            ring,
            ring,
            pltpu.VMEM((4 * channels, width), bf16),
            pltpu.VMEM((rows, width), f32),
        ],
    )(anchor, step_size, volume, noise, one, two, returned, head, tail, *consts)


def solution(mesh):
    placed = (
        P("groups", "slab", None),
        P("groups", "slab", None),
        P("groups", "slab", None, None),
        P("groups"),
        P("groups"),
        P("groups"),
        P(),
        P(),
        P(),
        P(),
        P(),
        P(),
    )
    return jax.shard_map(
        per_device, mesh=mesh, in_specs=placed, out_specs=P("groups", "slab", None), check_vma=False
    )
```

```python
import functools

import jax
import jax.numpy as jnp
from jax import lax
from jax.experimental import pallas as pl
from jax.experimental.pallas import tpu as pltpu
from jax.sharding import PartitionSpec as P


ANGLES = 180
LANES = 128
GROUP = 16
TURN = 4
WAIT = 14
SETS = 4

data_gain = 0.25

f32 = jnp.float32
bf16 = jnp.bfloat16
VMEM = pl.BlockSpec(memory_space=pltpu.VMEM)
SMEM = pl.BlockSpec(memory_space=pltpu.SMEM)
HBM = pl.BlockSpec(memory_space=pltpu.HBM)


def split(value, pieces=2):
    parts = []
    for _ in range(pieces):
        parts.append(value.astype(bf16).astype(f32))
        value = value - parts[-1]
    return parts


def pack_kernel(*refs):
    count = (len(refs) - 2) // 2
    sources, out_ref, held, sems = refs[:count], refs[count], refs[count + 1 : -1], refs[-1]
    copies = [
        pltpu.make_async_copy(source, target, sems.at[k]) for k, (source, target) in enumerate(zip(sources, held))
    ]
    for copy in copies:
        copy.start()
    copies[0].wait()
    volume_ref = held[0]
    rows = volume_ref.shape[1]
    peers = out_ref.shape[0]
    chunks = LANES // rows
    depth = rows // chunks
    edge = jnp.concatenate([volume_ref[0, :2], volume_ref[0, rows - 2 :]], axis=0)
    _, middle, final = split(edge, 3)
    blank = [jnp.zeros((4, LANES - 2 * rows), f32)] if 2 * rows < LANES else []
    none = jnp.zeros((4, LANES), f32)
    for peer in range(peers):
        at = slice(peer * rows, (peer + 1) * rows)
        piece = volume_ref[0, :, at]
        wide = jnp.concatenate([piece[k * depth : (k + 1) * depth] for k in range(chunks)], axis=1)
        out_ref[peer, :depth] = wide.astype(bf16)
        lower = jnp.concatenate([middle[:, at], final[:, at]] + blank, axis=1)
        out_ref[peer, depth:] = jnp.concatenate([lower, none], axis=0).astype(bf16)
    for copy in copies[1:]:
        copy.wait()


def prep_kernel(
    angles_ref, offsets_ref, gain_ref, base_ref, conv_a_ref, bias_ref, conv_b_ref, own_ref,
    wa_ref, wb_ref, wr_ref, lift_ref, shift_ref, table_ref,
):
    channels = conv_a_ref.shape[1]

    def column(row):
        return jnp.broadcast_to(row, (LANES, channels)).T

    lift_ref[0] = column(0.5 * gain_ref[...])
    lift_ref[1] = column(0.5 * base_ref[...])
    shift = column(0.5 * bias_ref[...])
    shift_ref[:channels] = shift
    shift_ref[channels:] = shift

    taps = [conv_a_ref[t].astype(f32) * 0.5 for t in range(9)]
    zero = jnp.zeros((channels, channels), f32)
    for r in range(2):
        for j in range(3):
            for e in range(0, 4, 2):
                pair = [taps[3 * (k - r) + j] if 0 <= k - r < 3 else zero for k in (e, e + 1)]
                at = (4 * j + e) * channels
                wa_ref[r * channels : (r + 1) * channels, at : at + 2 * channels] = jnp.concatenate(
                    pair, axis=1
                ).astype(bf16)

    own = column(own_ref[...])[:, :channels]
    row = lax.broadcasted_iota(jnp.int32, (GROUP, LANES), 0)
    half = lax.broadcasted_iota(jnp.int32, (GROUP, LANES), 1) // channels

    def both(line):
        return jnp.broadcast_to(jnp.concatenate([line, line], axis=1), (GROUP, LANES))

    folded = [split(jnp.sum(own * conv_b_ref[t].astype(f32), axis=0, keepdims=True)) for t in range(9)]
    mine = split(own_ref[...])
    for q in range(GROUP // 2 + 1):
        at = slice(q * LANES, (q + 1) * LANES)
        for j in range(3):
            for s in range(2):
                block = jnp.zeros((GROUP, LANES), f32)
                for i in range(3):
                    block = jnp.where(half + 2 * q - row == i, both(folded[3 * i + j][s]), block)
                first = (2 * j + s) * GROUP
                wb_ref[first : first + GROUP, at] = block.astype(bf16)
        if q < GROUP // 2:
            for s in range(2):
                block = jnp.where(half + 2 * q == row, both(mine[s]), 0.0)
                wr_ref[s * GROUP : (s + 1) * GROUP, at] = block.astype(bf16)

    level = jnp.abs(jnp.cos(jnp.pi * angles_ref[...].astype(f32) / ANGLES))
    table_ref[0:1] = 0.6 + 0.4 * level
    table_ref[1:2] = offsets_ref[...].astype(f32)


def shifted(block, step):
    width = block.shape[1]
    moved = pltpu.roll(block, (-step) % width, 1)
    lane = lax.broadcasted_iota(jnp.int32, (block.shape[0], LANES), 1)
    if step < 0:
        edge = jnp.where(lane == 0, jnp.zeros_like(moved[:, :LANES]), moved[:, :LANES])
        return jnp.concatenate([edge, moved[:, LANES:]], axis=1)
    edge = jnp.where(lane == LANES - 1, jnp.zeros_like(moved[:, -LANES:]), moved[:, -LANES:])
    return jnp.concatenate([moved[:, :-LANES], edge], axis=1)


def lifted(line, lift_ref, ring, at, kept_ref=None, kept_at=None, keep=None):
    channels = lift_ref.shape[1]
    tiles = line.shape[1] // LANES
    for c in range(0, channels, 16):
        gain, base = lift_ref[0, c : c + 16], lift_ref[1, c : c + 16]
        if keep is not None:
            gain, base = gain * keep, base * keep
        z = jnp.concatenate([gain] * tiles, axis=1) * line + jnp.concatenate([base] * tiles, axis=1)
        h = (z * jnp.tanh(z) + z).astype(bf16)
        ring[0, at + c : at + c + 16] = shifted(h, -1)
        ring[1, at + c : at + c + 16] = h
        ring[2, at + c : at + c + 16] = shifted(h, 1)
        if kept_ref is not None:
            kept_ref[kept_at + c : kept_at + c + 16, :] = h


def convolved(p0, p1, wa_ref, bias_ref, store):
    width = p0.shape[2]
    for n in range(0, width, 256):
        rhs = jnp.concatenate([r[j, :, n : n + 256] for j in range(3) for r in (p0, p1)], axis=0)
        acc = jnp.dot(wa_ref[...], rhs, preferred_element_type=f32)
        z = acc + jnp.concatenate([bias_ref[...]] * 2, axis=1)
        store(slice(n, n + 256), (z * jnp.tanh(z) + z).astype(bf16))


def projected(h1, h0, wb_ref, wr_ref):
    conv = jnp.dot(wb_ref[:, : h1.shape[0]], h1, preferred_element_type=f32)
    kept = jnp.dot(wr_ref[:, : h0.shape[0]], h0, preferred_element_type=f32)
    taps = [conv[2 * j * GROUP : (2 * j + 1) * GROUP] + conv[(2 * j + 1) * GROUP : (2 * j + 2) * GROUP] for j in range(3)]
    total = kept[:GROUP] + kept[GROUP:] + taps[1]
    return total + shifted(taps[0], -1) + shifted(taps[2], 1)


def score_kernel(*refs, begin, count):
    given, refs = refs[: int(begin > 0)], refs[int(begin > 0) :]
    volume_ref, lift_ref, bias_ref, wa_ref, wb_ref, wr_ref, out_ref, edge_ref = refs[:8]
    last_ref, refs = (refs[8], refs[9:]) if not begin else (None, refs[8:])
    rings, (h0_ref, h1_ref) = refs[:-2], refs[-2:]
    turn = len(rings)
    channels = lift_ref.shape[1]
    lead = 2 * channels if begin else 0

    def lift(pair, ring):
        for k in range(2):
            row = 2 * pair + k
            line = volume_ref[0, 2 * begin + row : 2 * begin + row + 1, :]
            lifted(line, lift_ref, ring, k * channels, h0_ref, row * channels)

    def step(g, p0, p1, p2):
        if p2 is not None:
            lift(g + 2, p2)

        def store(at, h):
            h1_ref[lead + g * 2 * channels : lead + (g + 1) * 2 * channels, at] = h

        convolved(p0, p1, wa_ref, bias_ref, store)

    lift(0, rings[0])
    lift(1, rings[1])
    if begin:
        h1_ref[:lead] = given[0][...]

    low = 2 * begin if begin else 2
    done = low
    for k in range(count):
        step(k, rings[k % turn], rings[(k + 1) % turn], rings[(k + 2) % turn] if k + 1 < count else None)
        ready = 2 * (begin + k + 1)
        if ready - done >= WAIT or k + 1 == count:
            at = (done - low) * channels
            own = (done - 2 * begin) * channels
            size = ready - done
            total = projected(h1_ref[at : at + (size + 2) * channels], h0_ref[own : own + size * channels], wb_ref, wr_ref)
            out_ref[done : done + size] = total[:size]
            done = ready

    total = (2 * count) * channels + lead
    if begin:
        edge_ref[...] = h1_ref[total - 2 * channels : total]
    else:
        edge_ref[...] = h1_ref[: 2 * channels]
        last_ref[...] = h1_ref[total - 2 * channels : total]


def data_kernel(table_ref, cells_in_ref, measured_ref, out_ref, cells_ref, back_ref, sum_ref, line_ref, sems, *scratch):
    rows, views, det = measured_ref.shape[1:]
    peers = cells_in_ref.shape[0]
    nx = cells_ref.shape[1]
    chunks = LANES // rows
    depth = rows // chunks
    blocks = nx // LANES
    sets = [scratch[2 * k : 2 * k + 2] for k in range(len(scratch) // 2)]
    body = slice(LANES, LANES + det)

    def fetch(view):
        return pltpu.make_async_copy(measured_ref.at[0, :, view], line_ref.at[view, :, body], sems.at[view])

    for view in range(views):
        fetch(view).start()

    for tile in range(nx // LANES):
        pieces = []
        for peer in range(tile * chunks, (tile + 1) * chunks):
            got = cells_in_ref[peer, :depth].astype(f32)
            pieces += [got[:, k * rows : (k + 1) * rows] for k in range(chunks)]
        cells_ref[:, tile * LANES : (tile + 1) * LANES] = (-jnp.concatenate(pieces, axis=0).T).astype(bf16)

    back_ref[...] = jnp.zeros_like(back_ref)
    sum_ref[...] = jnp.zeros_like(sum_ref)
    for low_ref, _ in sets:
        low_ref[...] = jnp.zeros_like(low_ref)

    cell = lax.broadcasted_iota(jnp.int32, (16, LANES), 1).astype(f32)
    place = lax.broadcasted_iota(jnp.int32, (16, LANES), 0)
    bins = jnp.concatenate([(place + 16 * k).astype(jnp.int16) for k in range(16)], axis=0)

    def window(view, b):
        begin = (det - 1) * 0.5 + (b * LANES - (nx - 1) * 0.5) * table_ref[0, view] + table_ref[1, view]
        first = jnp.floor(begin * (1.0 / LANES))
        at = pl.ds(pl.multiple_of((first.astype(jnp.int32) + 1) * LANES, LANES), 2 * LANES)
        return at, begin - first * LANES

    def forward(view, low_ref, tent_ref):
        for b in range(blocks):
            at, begin = window(view, b)
            target = cell * table_ref[0, view] + begin
            under = jnp.floor(target)
            near = (1.0 - (target - under)).astype(bf16)
            far = (1.0 - ((under + 1.0) - target)).astype(bf16)
            spot = under.astype(jnp.int32)
            this = jnp.concatenate([spot.astype(jnp.int16)] * 16, axis=0)
            after = jnp.concatenate([(spot + 1).astype(jnp.int16)] * 16, axis=0)
            near = jnp.concatenate([near] * 16, axis=0)
            far = jnp.concatenate([far] * 16, axis=0)
            tent = jnp.where(bins == this, near, jnp.where(bins == after, far, jnp.zeros_like(far)))
            tent_ref[b] = tent
            line_ref[view, :, at] += lax.dot_general(
                cells_ref[:, b * LANES : (b + 1) * LANES],
                tent,
                (((1,), (1,)), ((), ())),
                preferred_element_type=f32,
            )
        misfit = line_ref[view, :, body]
        low_ref[:, body] = misfit.astype(bf16)
        square = misfit * misfit
        total = square[:, :LANES]
        for k in range(1, det // LANES):
            total = total + square[:, k * LANES : (k + 1) * LANES]
        sum_ref[...] += total

    def backward(view, low_ref, tent_ref):
        for b in range(blocks):
            at, _ = window(view, b)
            back_ref[:, b * LANES : (b + 1) * LANES] += jnp.dot(
                low_ref[:, at], tent_ref[b], preferred_element_type=f32
            )

    turn = len(sets)
    lead = turn // 2
    rounds = (views - lead) // turn
    for view in range(lead):
        fetch(view).wait()
    for view in range(lead):
        forward(view, *sets[view])

    def several(it, carry):
        for k in range(turn):
            fetch(it * turn + lead + k).wait()
        for k in range(turn):
            forward(it * turn + lead + k, *sets[(lead + k) % turn])
            backward(it * turn + k, *sets[k])
        return carry

    lax.fori_loop(0, rounds, several, 0)
    for view in range(rounds * turn + lead, views):
        fetch(view).wait()
    for view in range(rounds * turn, views):
        if view + lead < views:
            forward(view + lead, *sets[(view + lead) % turn])
        backward(view, *sets[view % turn])

    whole = split(jnp.sum(sum_ref[...], keepdims=True), 3)
    lane = lax.broadcasted_iota(jnp.int32, (8, LANES), 1)
    third = lax.broadcasted_iota(jnp.int32, (8, LANES), 0) == 2
    got = [cells_in_ref[peer].astype(f32) for peer in range(peers)]
    for peer in range(peers):
        low, high = got[max(peer - 1, 0)], got[min(peer + 1, peers - 1)]
        note = jnp.concatenate(
            [low[depth - 2 : depth], high[:2], low[depth + 2 : depth + 4], high[depth : depth + 2]], axis=0
        )
        for k in range(3):
            note = jnp.where(third & (lane == rows + k), whole[k], note)
        out_ref[peer, depth:] = note.astype(bf16)
    for tile in range(nx // LANES):
        turned = back_ref[:, tile * LANES : (tile + 1) * LANES].T
        for k in range(chunks):
            peer = tile * chunks + k
            own = turned[k * rows : (k + 1) * rows]
            wide = jnp.concatenate([own[i * depth : (i + 1) * depth] for i in range(chunks)], axis=1)
            out_ref[peer, :depth] = wide.astype(bf16)


def finish_kernel(
    anchor_ref, step_ref, volume_ref, noise_ref, one_ref, two_ref, back_ref, head_ref, tail_ref, lift_ref, bias_ref,
    wa_ref, wb_ref, wr_ref, out_ref, ext_ref, ring_a, ring_b, h1_ref, score_ref, done_ref, sems, *, count, height, border,
):
    rows, width = score_ref.shape
    channels = lift_ref.shape[1]
    peers = back_ref.shape[0]
    chunks = LANES // rows
    depth = rows // chunks
    anchor = anchor_ref[0]

    tails = [back_ref[peer, depth:].astype(f32) for peer in range(peers)]
    lane = lax.broadcasted_iota(jnp.int32, (8, LANES), 1)
    third = lax.broadcasted_iota(jnp.int32, (8, LANES), 0) == 2
    total = tails[0]
    for tail in tails[1:]:
        total = total + tail
    misfit = jnp.sum(jnp.where(third & (lane >= rows) & (lane < rows + 3), total, 0.0), keepdims=True)

    ext_ref[2:4] = volume_ref[0, :2]
    ext_ref[8:10] = volume_ref[0, rows - 2 :]
    for tile in range(width // LANES):
        mine = tails[tile * chunks : (tile + 1) * chunks]
        upper = [t[0:2, LANES - rows :] for t in mine], [t[2:4, :rows] for t in mine]
        for side, target in ((0, 0), (1, 10)):
            parts = [upper[side]] + [
                [t[4 + 2 * side : 6 + 2 * side, k * rows : (k + 1) * rows] for t in mine] for k in range(2)
            ]
            parts = [jnp.concatenate(p, axis=1) for p in parts]
            ext_ref[target : target + 2, tile * LANES : (tile + 1) * LANES] = parts[0] + parts[1] + parts[2]

    score_ref[:border] = one_ref[:border]
    score_ref[border:] = two_ref[border:]
    step = step_ref[...].reshape(1, 1)
    weight = data_gain / jnp.sqrt(misfit / count + 1e-06)
    sway = jnp.sqrt(2.0 * step)

    def combine(low, high, sem):
        for tile in range(width // LANES):
            at = slice(tile * LANES, (tile + 1) * LANES)
            got = [back_ref[tile * chunks + k, :depth].astype(f32) for k in range(chunks)]
            back = jnp.concatenate(
                [jnp.concatenate([g[:, k * rows : (k + 1) * rows] for g in got], axis=1) for k in range(chunks)], axis=0
            )[low:high]
            moved = step * (score_ref[low:high, at] + weight * back)
            done_ref[low:high, at] = volume_ref[0, low:high, at] + moved + sway * noise_ref[0, low:high, at]
        copy = pltpu.make_async_copy(done_ref.at[pl.ds(low, high - low)], out_ref.at[0, pl.ds(low, high - low)], sem)
        copy.start()
        return copy

    copies = [combine(8, rows - 8, sems.at[0])] if rows > 16 else []
    inside = jnp.where(anchor > 0, 1.0, 0.0).astype(f32), jnp.where(anchor + rows < height, 1.0, 0.0).astype(f32)
    for side in range(2):
        for k in range(4):
            line = ext_ref[8 * side + k : 8 * side + k + 1, :]
            halo = (k < 2) == (side == 0)
            ring = (ring_a, ring_b)[k // 2]
            lifted(line, lift_ref, ring, (k % 2) * channels, keep=inside[side] if halo else None)

        def store(at, h):
            h1_ref[2 * channels * side : 2 * channels * (side + 1), at] = h

        convolved(ring_a, ring_b, wa_ref, bias_ref, store)
        if side == 0:
            h1_ref[2 * channels :] = head_ref[...]

            @pl.when(anchor == 0)
            def _():
                h1_ref[:channels] = jnp.zeros((channels, width), bf16)
        else:
            h1_ref[: 2 * channels] = tail_ref[...]

            @pl.when(anchor + rows == height)
            def _():
                h1_ref[3 * channels :] = jnp.zeros((channels, width), bf16)

        scores = projected(h1_ref[...], (ring_b, ring_a)[side][1], wb_ref, wr_ref)
        at = (rows - 2) * side
        score_ref[at : at + 2] = scores[:2]

    for k, low in enumerate((0, rows - 8)):
        copies.append(combine(low, low + 8, sems.at[k + 1]))
    for copy in copies:
        copy.wait()


def call(kernel, mebibytes, **kwargs):
    params = pltpu.CompilerParams(vmem_limit_bytes=mebibytes << 20)
    return pl.pallas_call(kernel, compiler_params=params, **kwargs)


def spec(shape, dtype):
    return jax.ShapeDtypeStruct(shape, dtype)


def apart(array):
    return pltpu.with_memory_space_constraint(array, pltpu.HBM)


def data_call(table, cells, measured):
    rows, views, det = measured.shape[1:]
    peers = cells.shape[0]
    nx = peers * rows
    wide = det + 2 * LANES
    lines = [
        pltpu.VMEM((rows, wide), bf16),
        pltpu.VMEM((nx // LANES, 2 * LANES, LANES), bf16),
    ]
    return call(
        data_kernel,
        12,
        out_shape=spec((peers, rows * rows // LANES + 8, LANES), bf16),
        in_specs=[SMEM, VMEM, HBM],
        out_specs=VMEM,
        scratch_shapes=[
            pltpu.VMEM((rows, nx), bf16),
            pltpu.VMEM((rows, nx), f32),
            pltpu.VMEM((rows, LANES), f32),
            pltpu.VMEM((views, rows, wide), f32),
            pltpu.SemaphoreType.DMA((views,)),
            *lines * SETS,
        ],
    )(table, cells, apart(measured))


def per_device(
    volume,
    noise,
    measured,
    angles,
    offsets,
    step_size,
    lift_w,
    lift_b,
    conv_a,
    bias_a,
    conv_b,
    out_w,
):
    slices, rows, width = volume.shape
    views, det = measured.shape[2:]
    channels = lift_w.shape[0]
    peers = lax.axis_size("slab")
    height = peers * rows
    chunks = LANES // rows
    depth = rows // chunks

    def line(array):
        return array.reshape(1, -1)

    pairs = rows // 2 - 1
    half = pairs // 2
    ring = pltpu.VMEM((3, 2 * channels, width), bf16)
    pair = spec((2 * channels, width), bf16)
    anchor = (lax.axis_index("slab") * rows).astype(jnp.int32).reshape(1)
    small = (volume, line(angles), line(offsets), line(lift_w), line(lift_b), conv_a, line(bias_a), conv_b, line(out_w))

    def score_part(begin, count, *args):
        return call(
            functools.partial(score_kernel, begin=begin, count=count),
            24,
            out_shape=(spec((rows, width), f32), pair) + (() if begin else (pair,)),
            in_specs=[VMEM] * len(args),
            out_specs=(VMEM,) * (2 if begin else 3),
            scratch_shapes=[
                *[ring] * min(TURN, half),
                pltpu.VMEM(((2 * count + 4) * channels, width), bf16),
                pltpu.VMEM(((2 * count + 2) * channels, width), bf16),
            ],
        )(*args)

    payload, volume, *small = call(
        pack_kernel,
        4,
        out_shape=(spec((peers, depth + 8, LANES), bf16),) + tuple(spec(a.shape, a.dtype) for a in small),
        in_specs=[HBM] * len(small),
        out_specs=(VMEM,) * (len(small) + 1),
        scratch_shapes=[pltpu.SemaphoreType.DMA((len(small),))],
    )(*[apart(a) for a in small])
    cells = lax.all_to_all(payload, "slab", 0, 0)
    wa, wb, wr, lift, bias, table = call(
        prep_kernel,
        6,
        out_shape=(
            spec((2 * channels, 12 * channels), bf16),
            spec((6 * GROUP, (GROUP + 2) * channels), bf16),
            spec((2 * GROUP, GROUP * channels), bf16),
            spec((2, channels, LANES), f32),
            spec((2 * channels, LANES), f32),
            spec((2, views), f32),
        ),
        in_specs=[VMEM] * 8,
        out_specs=(VMEM,) * 6,
    )(*small)
    consts = (lift, bias, wa, wb, wr)
    one, head, middle = score_part(0, half, volume, *consts)

    sent = data_call(table, cells, measured)
    returned = lax.all_to_all(sent, "slab", 0, 0)
    two, tail = score_part(half, pairs - half, middle, volume, *consts)
    return call(
        functools.partial(finish_kernel, count=slices * peers * rows * views * det, height=height, border=2 * half),
        12,
        out_shape=spec(volume.shape, f32),
        in_specs=[SMEM] + [VMEM] * 13,
        out_specs=HBM,
        scratch_shapes=[
            pltpu.VMEM((16, width), f32),
            ring,
            ring,
            pltpu.VMEM((4 * channels, width), bf16),
            pltpu.VMEM((rows, width), f32),
            pltpu.VMEM((rows, width), f32),
            pltpu.SemaphoreType.DMA((3,)),
        ],
    )(anchor, step_size, volume, noise, one, two, returned, head, tail, *consts)


def solution(mesh):
    placed = (
        P("groups", "slab", None),
        P("groups", "slab", None),
        P("groups", "slab", None, None),
        P("groups"),
        P("groups"),
        P("groups"),
        P(),
        P(),
        P(),
        P(),
        P(),
        P(),
    )
    return jax.shard_map(
        per_device, mesh=mesh, in_specs=placed, out_specs=P("groups", "slab", None), check_vma=False
    )
```

```python
import functools

import jax
import jax.numpy as jnp
from jax import lax
from jax.experimental import pallas as pl
from jax.experimental.pallas import tpu as pltpu
from jax.sharding import PartitionSpec as P


ANGLES = 180
LANES = 128
GROUP = 16
TURN = 4
WAIT = 14
EARLY = 4
SETS = 4

data_gain = 0.25

f32 = jnp.float32
bf16 = jnp.bfloat16
VMEM = pl.BlockSpec(memory_space=pltpu.VMEM)
SMEM = pl.BlockSpec(memory_space=pltpu.SMEM)
HBM = pl.BlockSpec(memory_space=pltpu.HBM)


def split(value, pieces=2):
    parts = []
    for _ in range(pieces):
        parts.append(value.astype(bf16).astype(f32))
        value = value - parts[-1]
    return parts


def pack_kernel(*refs):
    count = (len(refs) - 2) // 2
    sources, out_ref, held, sems = refs[:count], refs[count], refs[count + 1 : -1], refs[-1]
    copies = [
        pltpu.make_async_copy(source, target, sems.at[k]) for k, (source, target) in enumerate(zip(sources, held))
    ]
    for copy in copies:
        copy.start()
    copies[0].wait()
    volume_ref = held[0]
    rows = volume_ref.shape[1]
    peers = out_ref.shape[0]
    chunks = LANES // rows
    depth = rows // chunks
    edge = jnp.concatenate([volume_ref[0, :2], volume_ref[0, rows - 2 :]], axis=0)
    _, middle, final = split(edge, 3)
    blank = [jnp.zeros((4, LANES - 2 * rows), f32)] if 2 * rows < LANES else []
    none = jnp.zeros((4, LANES), f32)
    for peer in range(peers):
        at = slice(peer * rows, (peer + 1) * rows)
        piece = volume_ref[0, :, at]
        wide = jnp.concatenate([piece[k * depth : (k + 1) * depth] for k in range(chunks)], axis=1)
        out_ref[peer, :depth] = wide.astype(bf16)
        lower = jnp.concatenate([middle[:, at], final[:, at]] + blank, axis=1)
        out_ref[peer, depth:] = jnp.concatenate([lower, none], axis=0).astype(bf16)
    for copy in copies[1:]:
        copy.wait()


def prep_kernel(
    angles_ref, offsets_ref, gain_ref, base_ref, conv_a_ref, bias_ref, conv_b_ref, own_ref,
    wa_ref, wb_ref, wr_ref, lift_ref, shift_ref, table_ref,
):
    channels = conv_a_ref.shape[1]

    def column(row):
        return jnp.broadcast_to(row, (LANES, channels)).T

    lift_ref[0] = column(0.5 * gain_ref[...])
    lift_ref[1] = column(0.5 * base_ref[...])
    shift = column(0.5 * bias_ref[...])
    shift_ref[:channels] = shift
    shift_ref[channels:] = shift

    taps = [conv_a_ref[t].astype(f32) * 0.5 for t in range(9)]
    zero = jnp.zeros((channels, channels), f32)
    for r in range(2):
        for j in range(3):
            for e in range(0, 4, 2):
                pair = [taps[3 * (k - r) + j] if 0 <= k - r < 3 else zero for k in (e, e + 1)]
                at = (4 * j + e) * channels
                wa_ref[r * channels : (r + 1) * channels, at : at + 2 * channels] = jnp.concatenate(
                    pair, axis=1
                ).astype(bf16)

    own = column(own_ref[...])[:, :channels]
    row = lax.broadcasted_iota(jnp.int32, (GROUP, LANES), 0)
    half = lax.broadcasted_iota(jnp.int32, (GROUP, LANES), 1) // channels

    def both(line):
        return jnp.broadcast_to(jnp.concatenate([line, line], axis=1), (GROUP, LANES))

    folded = [split(jnp.sum(own * conv_b_ref[t].astype(f32), axis=0, keepdims=True)) for t in range(9)]
    mine = split(own_ref[...])
    for q in range(GROUP // 2 + 1):
        at = slice(q * LANES, (q + 1) * LANES)
        for j in range(3):
            for s in range(2):
                block = jnp.zeros((GROUP, LANES), f32)
                for i in range(3):
                    block = jnp.where(half + 2 * q - row == i, both(folded[3 * i + j][s]), block)
                first = (2 * j + s) * GROUP
                wb_ref[first : first + GROUP, at] = block.astype(bf16)
        if q < GROUP // 2:
            for s in range(2):
                block = jnp.where(half + 2 * q == row, both(mine[s]), 0.0)
                wr_ref[s * GROUP : (s + 1) * GROUP, at] = block.astype(bf16)

    level = jnp.abs(jnp.cos(jnp.pi * angles_ref[...].astype(f32) / ANGLES))
    table_ref[0:1] = 0.6 + 0.4 * level
    table_ref[1:2] = offsets_ref[...].astype(f32)


def shifted(block, step):
    width = block.shape[1]
    moved = pltpu.roll(block, (-step) % width, 1)
    lane = lax.broadcasted_iota(jnp.int32, (block.shape[0], LANES), 1)
    if step < 0:
        edge = jnp.where(lane == 0, jnp.zeros_like(moved[:, :LANES]), moved[:, :LANES])
        return jnp.concatenate([edge, moved[:, LANES:]], axis=1)
    edge = jnp.where(lane == LANES - 1, jnp.zeros_like(moved[:, -LANES:]), moved[:, -LANES:])
    return jnp.concatenate([moved[:, :-LANES], edge], axis=1)


def lifted(line, lift_ref, ring, at, kept_ref=None, kept_at=None, keep=None):
    channels = lift_ref.shape[1]
    tiles = line.shape[1] // LANES
    for c in range(0, channels, 16):
        gain, base = lift_ref[0, c : c + 16], lift_ref[1, c : c + 16]
        if keep is not None:
            gain, base = gain * keep, base * keep
        z = jnp.concatenate([gain] * tiles, axis=1) * line + jnp.concatenate([base] * tiles, axis=1)
        h = (z * jnp.tanh(z) + z).astype(bf16)
        ring[0, at + c : at + c + 16] = shifted(h, -1)
        ring[1, at + c : at + c + 16] = h
        ring[2, at + c : at + c + 16] = shifted(h, 1)
        if kept_ref is not None:
            kept_ref[kept_at + c : kept_at + c + 16, :] = h


def convolved(p0, p1, wa_ref, bias_ref, store):
    width = p0.shape[2]
    for n in range(0, width, 256):
        rhs = jnp.concatenate([r[j, :, n : n + 256] for j in range(3) for r in (p0, p1)], axis=0)
        acc = jnp.dot(wa_ref[...], rhs, preferred_element_type=f32)
        z = acc + jnp.concatenate([bias_ref[...]] * 2, axis=1)
        store(slice(n, n + 256), (z * jnp.tanh(z) + z).astype(bf16))


def projected(h1, h0, wb_ref, wr_ref):
    conv = jnp.dot(wb_ref[:, : h1.shape[0]], h1, preferred_element_type=f32)
    kept = jnp.dot(wr_ref[:, : h0.shape[0]], h0, preferred_element_type=f32)
    taps = [conv[2 * j * GROUP : (2 * j + 1) * GROUP] + conv[(2 * j + 1) * GROUP : (2 * j + 2) * GROUP] for j in range(3)]
    total = kept[:GROUP] + kept[GROUP:] + taps[1]
    return total + shifted(taps[0], -1) + shifted(taps[2], 1)


def score_kernel(*refs, begin, count):
    given, refs = refs[0], refs[1:]
    volume_ref, lift_ref, bias_ref, wa_ref, wb_ref, wr_ref, out_ref, edge_ref = refs[:8]
    copies = []
    if begin:
        refs = refs[8:]
    else:
        last_ref, seen_ref, sems, refs = refs[8], refs[9], refs[10], refs[11:]
        for view in range(seen_ref.shape[0]):
            copies.append(pltpu.make_async_copy(given.at[0, :, view], seen_ref.at[view], sems.at[view]))
            copies[-1].start()
    rings, (h0_ref, h1_ref) = refs[:-2], refs[-2:]
    turn = len(rings)
    channels = lift_ref.shape[1]
    lead = 2 * channels if begin else 0

    def lift(pair, ring):
        for k in range(2):
            row = 2 * pair + k
            line = volume_ref[0, 2 * begin + row : 2 * begin + row + 1, :]
            lifted(line, lift_ref, ring, k * channels, h0_ref, row * channels)

    def step(g, p0, p1, p2):
        if p2 is not None:
            lift(g + 2, p2)

        def store(at, h):
            h1_ref[lead + g * 2 * channels : lead + (g + 1) * 2 * channels, at] = h

        convolved(p0, p1, wa_ref, bias_ref, store)

    lift(0, rings[0])
    lift(1, rings[1])
    if begin:
        h1_ref[:lead] = given[...]

    low = 2 * begin if begin else 2
    done = low
    for k in range(count):
        step(k, rings[k % turn], rings[(k + 1) % turn], rings[(k + 2) % turn] if k + 1 < count else None)
        ready = 2 * (begin + k + 1)
        if ready - done >= WAIT or k + 1 == count:
            at = (done - low) * channels
            own = (done - 2 * begin) * channels
            size = ready - done
            total = projected(h1_ref[at : at + (size + 2) * channels], h0_ref[own : own + size * channels], wb_ref, wr_ref)
            out_ref[done : done + size] = total[:size]
            done = ready

    total = (2 * count) * channels + lead
    if begin:
        edge_ref[...] = h1_ref[total - 2 * channels : total]
    else:
        edge_ref[...] = h1_ref[: 2 * channels]
        last_ref[...] = h1_ref[total - 2 * channels : total]
    for copy in copies:
        copy.wait()


def data_kernel(table_ref, cells_in_ref, seen_ref, measured_ref, out_ref, cells_ref, back_ref, sum_ref, line_ref, sems, *scratch):
    rows, views, det = measured_ref.shape[1:]
    peers = cells_in_ref.shape[0]
    nx = cells_ref.shape[1]
    chunks = LANES // rows
    depth = rows // chunks
    blocks = nx // LANES
    sets = [scratch[2 * k : 2 * k + 2] for k in range(len(scratch) // 2)]
    body = slice(LANES, LANES + det)

    def fetch(view):
        return pltpu.make_async_copy(measured_ref.at[0, :, view], line_ref.at[view, :, body], sems.at[view])

    early = seen_ref.shape[0]
    for view in range(early, views):
        fetch(view).start()
    for view in range(early):
        line_ref[view, :, body] = seen_ref[view]

    for tile in range(nx // LANES):
        pieces = []
        for peer in range(tile * chunks, (tile + 1) * chunks):
            got = cells_in_ref[peer, :depth].astype(f32)
            pieces += [got[:, k * rows : (k + 1) * rows] for k in range(chunks)]
        cells_ref[:, tile * LANES : (tile + 1) * LANES] = (-jnp.concatenate(pieces, axis=0).T).astype(bf16)

    back_ref[...] = jnp.zeros_like(back_ref)
    sum_ref[...] = jnp.zeros_like(sum_ref)
    for low_ref, _ in sets:
        low_ref[...] = jnp.zeros_like(low_ref)

    cell = lax.broadcasted_iota(jnp.int32, (16, LANES), 1).astype(f32)
    place = lax.broadcasted_iota(jnp.int32, (16, LANES), 0)
    bins = jnp.concatenate([(place + 16 * k).astype(jnp.int16) for k in range(16)], axis=0)

    def window(view, b):
        begin = (det - 1) * 0.5 + (b * LANES - (nx - 1) * 0.5) * table_ref[0, view] + table_ref[1, view]
        first = jnp.floor(begin * (1.0 / LANES))
        at = pl.ds(pl.multiple_of((first.astype(jnp.int32) + 1) * LANES, LANES), 2 * LANES)
        return at, begin - first * LANES

    def forward(view, low_ref, tent_ref):
        for b in range(blocks):
            at, begin = window(view, b)
            target = cell * table_ref[0, view] + begin
            under = jnp.floor(target)
            near = (1.0 - (target - under)).astype(bf16)
            far = (1.0 - ((under + 1.0) - target)).astype(bf16)
            spot = under.astype(jnp.int32)
            this = jnp.concatenate([spot.astype(jnp.int16)] * 16, axis=0)
            after = jnp.concatenate([(spot + 1).astype(jnp.int16)] * 16, axis=0)
            near = jnp.concatenate([near] * 16, axis=0)
            far = jnp.concatenate([far] * 16, axis=0)
            tent = jnp.where(bins == this, near, jnp.where(bins == after, far, jnp.zeros_like(far)))
            tent_ref[b] = tent
            line_ref[view, :, at] += lax.dot_general(
                cells_ref[:, b * LANES : (b + 1) * LANES],
                tent,
                (((1,), (1,)), ((), ())),
                preferred_element_type=f32,
            )
        misfit = line_ref[view, :, body]
        low_ref[:, body] = misfit.astype(bf16)
        square = misfit * misfit
        total = square[:, :LANES]
        for k in range(1, det // LANES):
            total = total + square[:, k * LANES : (k + 1) * LANES]
        sum_ref[...] += total

    def backward(view, low_ref, tent_ref):
        for b in range(blocks):
            at, _ = window(view, b)
            back_ref[:, b * LANES : (b + 1) * LANES] += jnp.dot(
                low_ref[:, at], tent_ref[b], preferred_element_type=f32
            )

    turn = len(sets)
    lead = turn // 2
    rounds = (views - lead) // turn
    for view in range(early, lead):
        fetch(view).wait()
    for view in range(lead):
        forward(view, *sets[view])

    def several(it, carry):
        for k in range(turn):
            view = it * turn + lead + k

            @pl.when(view >= early)
            def _():
                fetch(view).wait()

        for k in range(turn):
            forward(it * turn + lead + k, *sets[(lead + k) % turn])
            backward(it * turn + k, *sets[k])
        return carry

    lax.fori_loop(0, rounds, several, 0)
    for view in range(max(rounds * turn + lead, early), views):
        fetch(view).wait()
    for view in range(rounds * turn, views):
        if view + lead < views:
            forward(view + lead, *sets[(view + lead) % turn])
        backward(view, *sets[view % turn])

    whole = split(jnp.sum(sum_ref[...], keepdims=True), 3)
    lane = lax.broadcasted_iota(jnp.int32, (8, LANES), 1)
    third = lax.broadcasted_iota(jnp.int32, (8, LANES), 0) == 2
    got = [cells_in_ref[peer].astype(f32) for peer in range(peers)]
    for peer in range(peers):
        low, high = got[max(peer - 1, 0)], got[min(peer + 1, peers - 1)]
        note = jnp.concatenate(
            [low[depth - 2 : depth], high[:2], low[depth + 2 : depth + 4], high[depth : depth + 2]], axis=0
        )
        for k in range(3):
            note = jnp.where(third & (lane == rows + k), whole[k], note)
        out_ref[peer, depth:] = note.astype(bf16)
    for tile in range(nx // LANES):
        turned = back_ref[:, tile * LANES : (tile + 1) * LANES].T
        for k in range(chunks):
            peer = tile * chunks + k
            own = turned[k * rows : (k + 1) * rows]
            wide = jnp.concatenate([own[i * depth : (i + 1) * depth] for i in range(chunks)], axis=1)
            out_ref[peer, :depth] = wide.astype(bf16)


def finish_kernel(
    anchor_ref, step_ref, volume_ref, noise_ref, one_ref, two_ref, back_ref, head_ref, tail_ref, lift_ref, bias_ref,
    wa_ref, wb_ref, wr_ref, out_ref, ext_ref, ring_a, ring_b, h1_ref, score_ref, done_ref, sems, *, count, height, border,
):
    rows, width = score_ref.shape
    channels = lift_ref.shape[1]
    peers = back_ref.shape[0]
    chunks = LANES // rows
    depth = rows // chunks
    anchor = anchor_ref[0]

    tails = [back_ref[peer, depth:].astype(f32) for peer in range(peers)]
    lane = lax.broadcasted_iota(jnp.int32, (8, LANES), 1)
    third = lax.broadcasted_iota(jnp.int32, (8, LANES), 0) == 2
    total = tails[0]
    for tail in tails[1:]:
        total = total + tail
    misfit = jnp.sum(jnp.where(third & (lane >= rows) & (lane < rows + 3), total, 0.0), keepdims=True)

    ext_ref[2:4] = volume_ref[0, :2]
    ext_ref[8:10] = volume_ref[0, rows - 2 :]
    for tile in range(width // LANES):
        mine = tails[tile * chunks : (tile + 1) * chunks]
        upper = [t[0:2, LANES - rows :] for t in mine], [t[2:4, :rows] for t in mine]
        for side, target in ((0, 0), (1, 10)):
            parts = [upper[side]] + [
                [t[4 + 2 * side : 6 + 2 * side, k * rows : (k + 1) * rows] for t in mine] for k in range(2)
            ]
            parts = [jnp.concatenate(p, axis=1) for p in parts]
            ext_ref[target : target + 2, tile * LANES : (tile + 1) * LANES] = parts[0] + parts[1] + parts[2]

    score_ref[:border] = one_ref[:border]
    score_ref[border:] = two_ref[border:]
    step = step_ref[...].reshape(1, 1)
    weight = data_gain / jnp.sqrt(misfit / count + 1e-06)
    sway = jnp.sqrt(2.0 * step)

    def combine(low, high, sem):
        for tile in range(width // LANES):
            at = slice(tile * LANES, (tile + 1) * LANES)
            got = [back_ref[tile * chunks + k, :depth].astype(f32) for k in range(chunks)]
            back = jnp.concatenate(
                [jnp.concatenate([g[:, k * rows : (k + 1) * rows] for g in got], axis=1) for k in range(chunks)], axis=0
            )[low:high]
            moved = step * (score_ref[low:high, at] + weight * back)
            done_ref[low:high, at] = volume_ref[0, low:high, at] + moved + sway * noise_ref[0, low:high, at]
        copy = pltpu.make_async_copy(done_ref.at[pl.ds(low, high - low)], out_ref.at[0, pl.ds(low, high - low)], sem)
        copy.start()
        return copy

    copies = [combine(8, rows - 8, sems.at[0])] if rows > 16 else []
    inside = jnp.where(anchor > 0, 1.0, 0.0).astype(f32), jnp.where(anchor + rows < height, 1.0, 0.0).astype(f32)
    for side in range(2):
        for k in range(4):
            line = ext_ref[8 * side + k : 8 * side + k + 1, :]
            halo = (k < 2) == (side == 0)
            ring = (ring_a, ring_b)[k // 2]
            lifted(line, lift_ref, ring, (k % 2) * channels, keep=inside[side] if halo else None)

        def store(at, h):
            h1_ref[2 * channels * side : 2 * channels * (side + 1), at] = h

        convolved(ring_a, ring_b, wa_ref, bias_ref, store)
        if side == 0:
            h1_ref[2 * channels :] = head_ref[...]

            @pl.when(anchor == 0)
            def _():
                h1_ref[:channels] = jnp.zeros((channels, width), bf16)
        else:
            h1_ref[: 2 * channels] = tail_ref[...]

            @pl.when(anchor + rows == height)
            def _():
                h1_ref[3 * channels :] = jnp.zeros((channels, width), bf16)

        scores = projected(h1_ref[...], (ring_b, ring_a)[side][1], wb_ref, wr_ref)
        at = (rows - 2) * side
        score_ref[at : at + 2] = scores[:2]

    for k, low in enumerate((0, rows - 8)):
        copies.append(combine(low, low + 8, sems.at[k + 1]))
    for copy in copies:
        copy.wait()


def call(kernel, mebibytes, **kwargs):
    params = pltpu.CompilerParams(vmem_limit_bytes=mebibytes << 20)
    return pl.pallas_call(kernel, compiler_params=params, **kwargs)


def spec(shape, dtype):
    return jax.ShapeDtypeStruct(shape, dtype)


def apart(array):
    return pltpu.with_memory_space_constraint(array, pltpu.HBM)


def data_call(table, cells, seen, measured):
    rows, views, det = measured.shape[1:]
    peers = cells.shape[0]
    nx = peers * rows
    wide = det + 2 * LANES
    lines = [
        pltpu.VMEM((rows, wide), bf16),
        pltpu.VMEM((nx // LANES, 2 * LANES, LANES), bf16),
    ]
    return call(
        data_kernel,
        12,
        out_shape=spec((peers, rows * rows // LANES + 8, LANES), bf16),
        in_specs=[SMEM, VMEM, VMEM, HBM],
        out_specs=VMEM,
        scratch_shapes=[
            pltpu.VMEM((rows, nx), bf16),
            pltpu.VMEM((rows, nx), f32),
            pltpu.VMEM((rows, LANES), f32),
            pltpu.VMEM((views, rows, wide), f32),
            pltpu.SemaphoreType.DMA((views,)),
            *lines * SETS,
        ],
    )(table, cells, seen, apart(measured))


def per_device(
    volume,
    noise,
    measured,
    angles,
    offsets,
    step_size,
    lift_w,
    lift_b,
    conv_a,
    bias_a,
    conv_b,
    out_w,
):
    slices, rows, width = volume.shape
    views, det = measured.shape[2:]
    channels = lift_w.shape[0]
    peers = lax.axis_size("slab")
    height = peers * rows
    chunks = LANES // rows
    depth = rows // chunks

    def line(array):
        return array.reshape(1, -1)

    pairs = rows // 2 - 1
    half = pairs // 2
    ring = pltpu.VMEM((3, 2 * channels, width), bf16)
    pair = spec((2 * channels, width), bf16)
    anchor = (lax.axis_index("slab") * rows).astype(jnp.int32).reshape(1)
    small = (volume, line(angles), line(offsets), line(lift_w), line(lift_b), conv_a, line(bias_a), conv_b, line(out_w))

    def score_part(begin, count, *args):
        more = () if begin else (pair, spec((EARLY, rows, det), f32))
        return call(
            functools.partial(score_kernel, begin=begin, count=count),
            20,
            out_shape=(spec((rows, width), f32), pair) + more,
            in_specs=[VMEM if begin else HBM] + [VMEM] * (len(args) - 1),
            out_specs=(VMEM,) * (2 + len(more)),
            scratch_shapes=([] if begin else [pltpu.SemaphoreType.DMA((EARLY,))])
            + [
                *[ring] * min(TURN, half),
                pltpu.VMEM(((2 * count + 4) * channels, width), bf16),
                pltpu.VMEM(((2 * count + 2) * channels, width), bf16),
            ],
        )(*args)

    payload, volume, *small = call(
        pack_kernel,
        4,
        out_shape=(spec((peers, depth + 8, LANES), bf16),) + tuple(spec(a.shape, a.dtype) for a in small),
        in_specs=[HBM] * len(small),
        out_specs=(VMEM,) * (len(small) + 1),
        scratch_shapes=[pltpu.SemaphoreType.DMA((len(small),))],
    )(*[apart(a) for a in small])
    cells = lax.all_to_all(payload, "slab", 0, 0)
    wa, wb, wr, lift, bias, table = call(
        prep_kernel,
        6,
        out_shape=(
            spec((2 * channels, 12 * channels), bf16),
            spec((6 * GROUP, (GROUP + 2) * channels), bf16),
            spec((2 * GROUP, GROUP * channels), bf16),
            spec((2, channels, LANES), f32),
            spec((2 * channels, LANES), f32),
            spec((2, views), f32),
        ),
        in_specs=[VMEM] * 8,
        out_specs=(VMEM,) * 6,
    )(*small)
    consts = (lift, bias, wa, wb, wr)
    one, head, middle, seen = score_part(0, half, apart(measured), volume, *consts)

    sent = data_call(table, cells, seen, measured)
    returned = lax.all_to_all(sent, "slab", 0, 0)
    two, tail = score_part(half, pairs - half, middle, volume, *consts)
    return call(
        functools.partial(finish_kernel, count=slices * peers * rows * views * det, height=height, border=2 * half),
        12,
        out_shape=spec(volume.shape, f32),
        in_specs=[SMEM] + [VMEM] * 13,
        out_specs=HBM,
        scratch_shapes=[
            pltpu.VMEM((16, width), f32),
            ring,
            ring,
            pltpu.VMEM((4 * channels, width), bf16),
            pltpu.VMEM((rows, width), f32),
            pltpu.VMEM((rows, width), f32),
            pltpu.SemaphoreType.DMA((3,)),
        ],
    )(anchor, step_size, volume, noise, one, two, returned, head, tail, *consts)


def solution(mesh):
    placed = (
        P("groups", "slab", None),
        P("groups", "slab", None),
        P("groups", "slab", None, None),
        P("groups"),
        P("groups"),
        P("groups"),
        P(),
        P(),
        P(),
        P(),
        P(),
        P(),
    )
    return jax.shard_map(
        per_device, mesh=mesh, in_specs=placed, out_specs=P("groups", "slab", None), check_vma=False
    )
```

```python
import functools

import jax
import jax.numpy as jnp
from jax import lax
from jax.experimental import pallas as pl
from jax.experimental.pallas import tpu as pltpu
from jax.sharding import PartitionSpec as P


ANGLES = 180
LANES = 128
GROUP = 16
TURN = 4
WAIT = 14
EARLY = 4
PARTS = 2
SETS = 4

data_gain = 0.25

f32 = jnp.float32
bf16 = jnp.bfloat16
VMEM = pl.BlockSpec(memory_space=pltpu.VMEM)
SMEM = pl.BlockSpec(memory_space=pltpu.SMEM)
HBM = pl.BlockSpec(memory_space=pltpu.HBM)


def split(value, pieces=2):
    parts = []
    for _ in range(pieces):
        parts.append(value.astype(bf16).astype(f32))
        value = value - parts[-1]
    return parts


def pack_kernel(*refs):
    count = (len(refs) - 4) // 2
    sources, out_ref, held, (block_ref, sems, sent_sems) = refs[:count], refs[count], refs[count + 1 : -3], refs[-3:]
    volume_ref = held[0]
    rows, width = volume_ref.shape[1:]
    peers = out_ref.shape[0]
    chunks = LANES // rows
    depth = rows // chunks
    arriving = []
    for k in range(PARTS):
        at = pl.ds(k * width // PARTS, width // PARTS)
        copy = pltpu.make_async_copy(sources[0].at[0, :, at], volume_ref.at[0, :, at], sems.at[k])
        copy.start()
        arriving.append(copy)
    copies = [
        pltpu.make_async_copy(source, target, sems.at[PARTS + k])
        for k, (source, target) in enumerate(zip(sources[1:], held[1:]))
    ]
    for copy in copies:
        copy.start()
    blank = [jnp.zeros((4, LANES - 2 * rows), f32)] if 2 * rows < LANES else []
    none = jnp.zeros((4, LANES), f32)
    for k in range(PARTS):
        arriving[k].wait()
        mine = range(k * peers // PARTS, (k + 1) * peers // PARTS)
        for peer in mine:
            at = slice(peer * rows, (peer + 1) * rows)
            piece = volume_ref[0, :, at]
            wide = jnp.concatenate([piece[i * depth : (i + 1) * depth] for i in range(chunks)], axis=1)
            block_ref[peer, :depth] = wide.astype(bf16)
            _, middle, final = split(jnp.concatenate([piece[:2], piece[rows - 2 :]], axis=0), 3)
            lower = jnp.concatenate([middle, final] + blank, axis=1)
            block_ref[peer, depth:] = jnp.concatenate([lower, none], axis=0).astype(bf16)
        at = pl.ds(mine.start, len(mine))
        copies.append(pltpu.make_async_copy(block_ref.at[at], out_ref.at[at], sent_sems.at[k]))
        copies[-1].start()
    for copy in copies:
        copy.wait()


def prep_kernel(
    angles_ref, offsets_ref, gain_ref, base_ref, conv_a_ref, bias_ref, conv_b_ref, own_ref,
    wa_ref, wb_ref, wr_ref, lift_ref, shift_ref, table_ref,
):
    channels = conv_a_ref.shape[1]

    def column(row):
        return jnp.broadcast_to(row, (LANES, channels)).T

    lift_ref[0] = column(0.5 * gain_ref[...])
    lift_ref[1] = column(0.5 * base_ref[...])
    shift = column(0.5 * bias_ref[...])
    shift_ref[:channels] = shift
    shift_ref[channels:] = shift

    taps = [conv_a_ref[t].astype(f32) * 0.5 for t in range(9)]
    zero = jnp.zeros((channels, channels), f32)
    for r in range(2):
        for j in range(3):
            for e in range(0, 4, 2):
                pair = [taps[3 * (k - r) + j] if 0 <= k - r < 3 else zero for k in (e, e + 1)]
                at = (4 * j + e) * channels
                wa_ref[r * channels : (r + 1) * channels, at : at + 2 * channels] = jnp.concatenate(
                    pair, axis=1
                ).astype(bf16)

    own = column(own_ref[...])[:, :channels]
    row = lax.broadcasted_iota(jnp.int32, (GROUP, LANES), 0)
    half = lax.broadcasted_iota(jnp.int32, (GROUP, LANES), 1) // channels

    def both(line):
        return jnp.broadcast_to(jnp.concatenate([line, line], axis=1), (GROUP, LANES))

    folded = [split(jnp.sum(own * conv_b_ref[t].astype(f32), axis=0, keepdims=True)) for t in range(9)]
    mine = split(own_ref[...])
    for q in range(GROUP // 2 + 1):
        at = slice(q * LANES, (q + 1) * LANES)
        for j in range(3):
            for s in range(2):
                block = jnp.zeros((GROUP, LANES), f32)
                for i in range(3):
                    block = jnp.where(half + 2 * q - row == i, both(folded[3 * i + j][s]), block)
                first = (2 * j + s) * GROUP
                wb_ref[first : first + GROUP, at] = block.astype(bf16)
        if q < GROUP // 2:
            for s in range(2):
                block = jnp.where(half + 2 * q == row, both(mine[s]), 0.0)
                wr_ref[s * GROUP : (s + 1) * GROUP, at] = block.astype(bf16)

    level = jnp.abs(jnp.cos(jnp.pi * angles_ref[...].astype(f32) / ANGLES))
    table_ref[0:1] = 0.6 + 0.4 * level
    table_ref[1:2] = offsets_ref[...].astype(f32)


def shifted(block, step):
    width = block.shape[1]
    moved = pltpu.roll(block, (-step) % width, 1)
    lane = lax.broadcasted_iota(jnp.int32, (block.shape[0], LANES), 1)
    if step < 0:
        edge = jnp.where(lane == 0, jnp.zeros_like(moved[:, :LANES]), moved[:, :LANES])
        return jnp.concatenate([edge, moved[:, LANES:]], axis=1)
    edge = jnp.where(lane == LANES - 1, jnp.zeros_like(moved[:, -LANES:]), moved[:, -LANES:])
    return jnp.concatenate([moved[:, :-LANES], edge], axis=1)


def lifted(line, lift_ref, ring, at, kept_ref=None, kept_at=None, keep=None):
    channels = lift_ref.shape[1]
    tiles = line.shape[1] // LANES
    for c in range(0, channels, 16):
        gain, base = lift_ref[0, c : c + 16], lift_ref[1, c : c + 16]
        if keep is not None:
            gain, base = gain * keep, base * keep
        z = jnp.concatenate([gain] * tiles, axis=1) * line + jnp.concatenate([base] * tiles, axis=1)
        h = (z * jnp.tanh(z) + z).astype(bf16)
        ring[0, at + c : at + c + 16] = shifted(h, -1)
        ring[1, at + c : at + c + 16] = h
        ring[2, at + c : at + c + 16] = shifted(h, 1)
        if kept_ref is not None:
            kept_ref[kept_at + c : kept_at + c + 16, :] = h


def convolved(p0, p1, wa_ref, bias_ref, store, keep=None):
    width = p0.shape[2]
    for n in range(0, width, 256):
        rhs = jnp.concatenate([r[j, :, n : n + 256] for j in range(3) for r in (p0, p1)], axis=0)
        acc = jnp.dot(wa_ref[...], rhs, preferred_element_type=f32)
        z = acc + jnp.concatenate([bias_ref[...]] * 2, axis=1)
        if keep is not None:
            half = z.shape[0] // 2
            z = jnp.concatenate(
                [part if factor is None else part * factor for part, factor in zip((z[:half], z[half:]), keep)], axis=0
            )
        store(slice(n, n + 256), (z * jnp.tanh(z) + z).astype(bf16))


def projected(h1, h0, wb_ref, wr_ref):
    conv = jnp.dot(wb_ref[:, : h1.shape[0]], h1, preferred_element_type=f32)
    kept = jnp.dot(wr_ref[:, : h0.shape[0]], h0, preferred_element_type=f32)
    taps = [conv[2 * j * GROUP : (2 * j + 1) * GROUP] + conv[(2 * j + 1) * GROUP : (2 * j + 2) * GROUP] for j in range(3)]
    total = kept[:GROUP] + kept[GROUP:] + taps[1]
    return total + shifted(taps[0], -1) + shifted(taps[2], 1)


def score_kernel(*refs, begin, count):
    given, refs = refs[0], refs[1:]
    volume_ref, lift_ref, bias_ref, wa_ref, wb_ref, wr_ref, out_ref, edge_ref = refs[:8]
    copies = []
    if begin:
        refs = refs[8:]
    else:
        last_ref, seen_ref, sems, refs = refs[8], refs[9], refs[10], refs[11:]
        for view in range(seen_ref.shape[0]):
            copies.append(pltpu.make_async_copy(given.at[0, :, view], seen_ref.at[view], sems.at[view]))
            copies[-1].start()
    rings, (h0_ref, h1_ref) = refs[:-2], refs[-2:]
    turn = len(rings)
    channels = lift_ref.shape[1]
    lead = 2 * channels if begin else 0

    def lift(pair, ring):
        for k in range(2):
            row = 2 * pair + k
            line = volume_ref[0, 2 * begin + row : 2 * begin + row + 1, :]
            lifted(line, lift_ref, ring, k * channels, h0_ref, row * channels)

    def step(g, p0, p1, p2):
        if p2 is not None:
            lift(g + 2, p2)

        def store(at, h):
            h1_ref[lead + g * 2 * channels : lead + (g + 1) * 2 * channels, at] = h

        convolved(p0, p1, wa_ref, bias_ref, store)

    lift(0, rings[0])
    lift(1, rings[1])
    if begin:
        h1_ref[:lead] = given[...]

    low = 2 * begin if begin else 2
    done = low
    for k in range(count):
        step(k, rings[k % turn], rings[(k + 1) % turn], rings[(k + 2) % turn] if k + 1 < count else None)
        ready = 2 * (begin + k + 1)
        if ready - done >= WAIT or k + 1 == count:
            at = (done - low) * channels
            own = (done - 2 * begin) * channels
            size = ready - done
            total = projected(h1_ref[at : at + (size + 2) * channels], h0_ref[own : own + size * channels], wb_ref, wr_ref)
            out_ref[done : done + size] = total[:size]
            done = ready

    total = (2 * count) * channels + lead
    if begin:
        edge_ref[...] = h1_ref[total - 2 * channels : total]
    else:
        edge_ref[...] = h1_ref[: 2 * channels]
        last_ref[...] = h1_ref[total - 2 * channels : total]
    for copy in copies:
        copy.wait()


def data_kernel(table_ref, cells_in_ref, seen_ref, measured_ref, out_ref, cells_ref, back_ref, sum_ref, line_ref, sems, *scratch):
    rows, views, det = measured_ref.shape[1:]
    peers = cells_in_ref.shape[0]
    nx = cells_ref.shape[1]
    chunks = LANES // rows
    depth = rows // chunks
    blocks = nx // LANES
    sets = [scratch[2 * k : 2 * k + 2] for k in range(len(scratch) // 2)]
    body = slice(LANES, LANES + det)

    def fetch(view):
        return pltpu.make_async_copy(measured_ref.at[0, :, view], line_ref.at[view, :, body], sems.at[view])

    early = seen_ref.shape[0]
    for view in range(early, views):
        fetch(view).start()
    for view in range(early):
        line_ref[view, :, body] = seen_ref[view]

    for tile in range(nx // LANES):
        pieces = []
        for peer in range(tile * chunks, (tile + 1) * chunks):
            got = cells_in_ref[peer, :depth].astype(f32)
            pieces += [got[:, k * rows : (k + 1) * rows] for k in range(chunks)]
        cells_ref[:, tile * LANES : (tile + 1) * LANES] = (-jnp.concatenate(pieces, axis=0).T).astype(bf16)

    back_ref[...] = jnp.zeros_like(back_ref)
    sum_ref[...] = jnp.zeros_like(sum_ref)
    for low_ref, _ in sets:
        low_ref[...] = jnp.zeros_like(low_ref)

    cell = lax.broadcasted_iota(jnp.int32, (16, LANES), 1).astype(f32)
    place = lax.broadcasted_iota(jnp.int32, (16, LANES), 0)
    bins = jnp.concatenate([(place + 16 * k).astype(jnp.int16) for k in range(16)], axis=0)

    def window(view, b):
        begin = (det - 1) * 0.5 + (b * LANES - (nx - 1) * 0.5) * table_ref[0, view] + table_ref[1, view]
        first = jnp.floor(begin * (1.0 / LANES))
        at = pl.ds(pl.multiple_of((first.astype(jnp.int32) + 1) * LANES, LANES), 2 * LANES)
        return at, begin - first * LANES

    def forward(view, low_ref, tent_ref):
        for b in range(blocks):
            at, begin = window(view, b)
            target = cell * table_ref[0, view] + begin
            under = jnp.floor(target)
            near = (1.0 - (target - under)).astype(bf16)
            far = (1.0 - ((under + 1.0) - target)).astype(bf16)
            spot = under.astype(jnp.int32)
            this = jnp.concatenate([spot.astype(jnp.int16)] * 16, axis=0)
            after = jnp.concatenate([(spot + 1).astype(jnp.int16)] * 16, axis=0)
            near = jnp.concatenate([near] * 16, axis=0)
            far = jnp.concatenate([far] * 16, axis=0)
            tent = jnp.where(bins == this, near, jnp.where(bins == after, far, jnp.zeros_like(far)))
            tent_ref[b] = tent
            line_ref[view, :, at] += lax.dot_general(
                cells_ref[:, b * LANES : (b + 1) * LANES],
                tent,
                (((1,), (1,)), ((), ())),
                preferred_element_type=f32,
            )
        misfit = line_ref[view, :, body]
        low_ref[:, body] = misfit.astype(bf16)
        square = misfit * misfit
        total = square[:, :LANES]
        for k in range(1, det // LANES):
            total = total + square[:, k * LANES : (k + 1) * LANES]
        sum_ref[...] += total

    def backward(view, low_ref, tent_ref):
        for b in range(blocks):
            at, _ = window(view, b)
            back_ref[:, b * LANES : (b + 1) * LANES] += jnp.dot(
                low_ref[:, at], tent_ref[b], preferred_element_type=f32
            )

    turn = len(sets)
    lead = turn // 2
    rounds = (views - lead) // turn
    for view in range(early, lead):
        fetch(view).wait()
    for view in range(lead):
        forward(view, *sets[view])

    def several(it, carry):
        for k in range(turn):
            view = it * turn + lead + k

            @pl.when(view >= early)
            def _():
                fetch(view).wait()

        for k in range(turn):
            forward(it * turn + lead + k, *sets[(lead + k) % turn])
            backward(it * turn + k, *sets[k])
        return carry

    lax.fori_loop(0, rounds, several, 0)
    for view in range(max(rounds * turn + lead, early), views):
        fetch(view).wait()
    for view in range(rounds * turn, views):
        if view + lead < views:
            forward(view + lead, *sets[(view + lead) % turn])
        backward(view, *sets[view % turn])

    whole = split(jnp.sum(sum_ref[...], keepdims=True), 3)
    lane = lax.broadcasted_iota(jnp.int32, (8, LANES), 1)
    third = lax.broadcasted_iota(jnp.int32, (8, LANES), 0) == 2
    got = [cells_in_ref[peer].astype(f32) for peer in range(peers)]
    for peer in range(peers):
        low, high = got[max(peer - 1, 0)], got[min(peer + 1, peers - 1)]
        note = jnp.concatenate(
            [low[depth - 2 : depth], high[:2], low[depth + 2 : depth + 4], high[depth : depth + 2]], axis=0
        )
        for k in range(3):
            note = jnp.where(third & (lane == rows + k), whole[k], note)
        out_ref[peer, depth:] = note.astype(bf16)
    for tile in range(nx // LANES):
        turned = back_ref[:, tile * LANES : (tile + 1) * LANES].T
        for k in range(chunks):
            peer = tile * chunks + k
            own = turned[k * rows : (k + 1) * rows]
            wide = jnp.concatenate([own[i * depth : (i + 1) * depth] for i in range(chunks)], axis=1)
            out_ref[peer, :depth] = wide.astype(bf16)


def finish_kernel(
    anchor_ref, step_ref, volume_ref, noise_ref, one_ref, two_ref, back_ref, head_ref, tail_ref, lift_ref, bias_ref,
    wa_ref, wb_ref, wr_ref, out_ref, ext_ref, score_ref, done_ref, sems, *scratch, count, height, border,
):
    rows, width = score_ref.shape
    channels = lift_ref.shape[1]
    peers = back_ref.shape[0]
    chunks = LANES // rows
    depth = rows // chunks
    anchor = anchor_ref[0]
    rings, h1_refs = scratch[:4], scratch[4:]

    tails = [back_ref[peer, depth:].astype(f32) for peer in range(peers)]
    lane = lax.broadcasted_iota(jnp.int32, (8, LANES), 1)
    third = lax.broadcasted_iota(jnp.int32, (8, LANES), 0) == 2
    total = tails[0]
    for tail in tails[1:]:
        total = total + tail
    misfit = jnp.sum(jnp.where(third & (lane >= rows) & (lane < rows + 3), total, 0.0), keepdims=True)

    ext_ref[2:4] = volume_ref[0, :2]
    ext_ref[8:10] = volume_ref[0, rows - 2 :]
    for tile in range(width // LANES):
        mine = tails[tile * chunks : (tile + 1) * chunks]
        upper = [t[0:2, LANES - rows :] for t in mine], [t[2:4, :rows] for t in mine]
        for side, target in ((0, 0), (1, 10)):
            parts = [upper[side]] + [
                [t[4 + 2 * side : 6 + 2 * side, k * rows : (k + 1) * rows] for t in mine] for k in range(2)
            ]
            parts = [jnp.concatenate(p, axis=1) for p in parts]
            ext_ref[target : target + 2, tile * LANES : (tile + 1) * LANES] = parts[0] + parts[1] + parts[2]

    score_ref[:border] = one_ref[:border]
    score_ref[border:] = two_ref[border:]
    step = step_ref[...].reshape(1, 1)
    weight = data_gain / jnp.sqrt(misfit / count + 1e-06)
    sway = jnp.sqrt(2.0 * step)

    def combine(low, high, sem):
        for tile in range(width // LANES):
            at = slice(tile * LANES, (tile + 1) * LANES)
            got = [back_ref[tile * chunks + k, :depth].astype(f32) for k in range(chunks)]
            back = jnp.concatenate(
                [jnp.concatenate([g[:, k * rows : (k + 1) * rows] for g in got], axis=1) for k in range(chunks)], axis=0
            )[low:high]
            moved = step * (score_ref[low:high, at] + weight * back)
            done_ref[low:high, at] = volume_ref[0, low:high, at] + moved + sway * noise_ref[0, low:high, at]
        copy = pltpu.make_async_copy(done_ref.at[pl.ds(low, high - low)], out_ref.at[0, pl.ds(low, high - low)], sem)
        copy.start()
        return copy

    copies = [combine(8, rows - 8, sems.at[0])] if rows > 16 else []
    inside = jnp.where(anchor > 0, 1.0, 0.0).astype(f32), jnp.where(anchor + rows < height, 1.0, 0.0).astype(f32)
    for side in range(2):
        own = rings[2 * side : 2 * side + 2]
        for k in range(4):
            line = ext_ref[8 * side + k : 8 * side + k + 1, :]
            halo = (k < 2) == (side == 0)
            lifted(line, lift_ref, own[k // 2], (k % 2) * channels, keep=inside[side] if halo else None)
    for side in range(2):
        own = rings[2 * side : 2 * side + 2]
        h1_ref = h1_refs[side]
        at = 2 * channels * side

        def store(columns, h):
            h1_ref[at : at + 2 * channels, columns] = h

        convolved(*own, wa_ref, bias_ref, store, keep=((inside[0], None), (None, inside[1]))[side])
        h1_ref[2 * channels - at : 4 * channels - at] = (head_ref, tail_ref)[side][...]
        scores = projected(h1_ref[...], own[1 - side][1], wb_ref, wr_ref)
        row = (rows - 2) * side
        score_ref[row : row + 2] = scores[:2]

    for k, low in enumerate((0, rows - 8)):
        copies.append(combine(low, low + 8, sems.at[k + 1]))
    for copy in copies:
        copy.wait()


def call(kernel, mebibytes, **kwargs):
    params = pltpu.CompilerParams(vmem_limit_bytes=mebibytes << 20)
    return pl.pallas_call(kernel, compiler_params=params, **kwargs)


def spec(shape, dtype):
    return jax.ShapeDtypeStruct(shape, dtype)


def apart(array):
    return pltpu.with_memory_space_constraint(array, pltpu.HBM)


def data_call(table, cells, seen, measured):
    rows, views, det = measured.shape[1:]
    peers = cells.shape[0]
    nx = peers * rows
    wide = det + 2 * LANES
    lines = [
        pltpu.VMEM((rows, wide), bf16),
        pltpu.VMEM((nx // LANES, 2 * LANES, LANES), bf16),
    ]
    return call(
        data_kernel,
        12,
        out_shape=spec((peers, rows * rows // LANES + 8, LANES), bf16),
        in_specs=[SMEM, VMEM, VMEM, HBM],
        out_specs=VMEM,
        scratch_shapes=[
            pltpu.VMEM((rows, nx), bf16),
            pltpu.VMEM((rows, nx), f32),
            pltpu.VMEM((rows, LANES), f32),
            pltpu.VMEM((views, rows, wide), f32),
            pltpu.SemaphoreType.DMA((views,)),
            *lines * SETS,
        ],
    )(table, cells, seen, apart(measured))


def per_device(
    volume,
    noise,
    measured,
    angles,
    offsets,
    step_size,
    lift_w,
    lift_b,
    conv_a,
    bias_a,
    conv_b,
    out_w,
):
    slices, rows, width = volume.shape
    views, det = measured.shape[2:]
    channels = lift_w.shape[0]
    peers = lax.axis_size("slab")
    height = peers * rows
    chunks = LANES // rows
    depth = rows // chunks

    def line(array):
        return array.reshape(1, -1)

    pairs = rows // 2 - 1
    half = pairs // 2
    ring = pltpu.VMEM((3, 2 * channels, width), bf16)
    pair = spec((2 * channels, width), bf16)
    anchor = (lax.axis_index("slab") * rows).astype(jnp.int32).reshape(1)
    small = (volume, line(angles), line(offsets), line(lift_w), line(lift_b), conv_a, line(bias_a), conv_b, line(out_w))

    def score_part(begin, count, *args):
        more = () if begin else (pair, spec((EARLY, rows, det), f32))
        return call(
            functools.partial(score_kernel, begin=begin, count=count),
            20,
            out_shape=(spec((rows, width), f32), pair) + more,
            in_specs=[VMEM if begin else HBM] + [VMEM] * (len(args) - 1),
            out_specs=(VMEM,) * (2 + len(more)),
            scratch_shapes=([] if begin else [pltpu.SemaphoreType.DMA((EARLY,))])
            + [
                *[ring] * min(TURN, half),
                pltpu.VMEM(((2 * count + 4) * channels, width), bf16),
                pltpu.VMEM(((2 * count + 2) * channels, width), bf16),
            ],
        )(*args)

    payload, volume, *small = call(
        pack_kernel,
        4,
        out_shape=(spec((peers, depth + 8, LANES), bf16),) + tuple(spec(a.shape, a.dtype) for a in small),
        in_specs=[HBM] * len(small),
        out_specs=(HBM,) + (VMEM,) * len(small),
        scratch_shapes=[
            pltpu.VMEM((peers, depth + 8, LANES), bf16),
            pltpu.SemaphoreType.DMA((len(small) - 1 + PARTS,)),
            pltpu.SemaphoreType.DMA((PARTS,)),
        ],
    )(*[apart(a) for a in small])
    cells = lax.all_to_all(payload, "slab", 0, 0)
    wa, wb, wr, lift, bias, table = call(
        prep_kernel,
        6,
        out_shape=(
            spec((2 * channels, 12 * channels), bf16),
            spec((6 * GROUP, (GROUP + 2) * channels), bf16),
            spec((2 * GROUP, GROUP * channels), bf16),
            spec((2, channels, LANES), f32),
            spec((2 * channels, LANES), f32),
            spec((2, views), f32),
        ),
        in_specs=[VMEM] * 8,
        out_specs=(VMEM,) * 6,
    )(*small)
    consts = (lift, bias, wa, wb, wr)
    one, head, middle, seen = score_part(0, half, apart(measured), volume, *consts)

    sent = data_call(table, cells, seen, measured)
    returned = lax.all_to_all(sent, "slab", 0, 0)
    two, tail = score_part(half, pairs - half, middle, volume, *consts)
    return call(
        functools.partial(finish_kernel, count=slices * peers * rows * views * det, height=height, border=2 * half),
        12,
        out_shape=spec(volume.shape, f32),
        in_specs=[SMEM] + [VMEM] * 13,
        out_specs=HBM,
        scratch_shapes=[
            pltpu.VMEM((16, width), f32),
            pltpu.VMEM((rows, width), f32),
            pltpu.VMEM((rows, width), f32),
            pltpu.SemaphoreType.DMA((3,)),
            *[ring] * 4,
            *[pltpu.VMEM((4 * channels, width), bf16)] * 2,
        ],
    )(anchor, step_size, volume, noise, one, two, returned, head, tail, *consts)


def solution(mesh):
    placed = (
        P("groups", "slab", None),
        P("groups", "slab", None),
        P("groups", "slab", None, None),
        P("groups"),
        P("groups"),
        P("groups"),
        P(),
        P(),
        P(),
        P(),
        P(),
        P(),
    )
    return jax.shard_map(
        per_device, mesh=mesh, in_specs=placed, out_specs=P("groups", "slab", None), check_vma=False
    )
```

```python
import functools

import jax
import jax.numpy as jnp
from jax import lax
from jax.experimental import pallas as pl
from jax.experimental.pallas import tpu as pltpu
from jax.sharding import PartitionSpec as P


ANGLES = 180
LANES = 128
GROUP = 16
TURN = 4
WAIT = 14
EARLY = 4
PARTS = 2
SETS = 3

data_gain = 0.25

f32 = jnp.float32
bf16 = jnp.bfloat16
VMEM = pl.BlockSpec(memory_space=pltpu.VMEM)
SMEM = pl.BlockSpec(memory_space=pltpu.SMEM)
HBM = pl.BlockSpec(memory_space=pltpu.HBM)


def split(value, pieces=2):
    parts = []
    for _ in range(pieces):
        parts.append(value.astype(bf16).astype(f32))
        value = value - parts[-1]
    return parts


def pack_kernel(*refs):
    count = (len(refs) - 4) // 2
    sources, out_ref, held, (block_ref, sems, sent_sems) = refs[:count], refs[count], refs[count + 1 : -3], refs[-3:]
    volume_ref = held[0]
    rows, width = volume_ref.shape[1:]
    peers = out_ref.shape[0]
    chunks = LANES // rows
    depth = rows // chunks
    arriving = []
    for k in range(PARTS):
        at = pl.ds(k * width // PARTS, width // PARTS)
        copy = pltpu.make_async_copy(sources[0].at[0, :, at], volume_ref.at[0, :, at], sems.at[k])
        copy.start()
        arriving.append(copy)
    copies = [
        pltpu.make_async_copy(source, target, sems.at[PARTS + k])
        for k, (source, target) in enumerate(zip(sources[1:], held[1:]))
    ]
    for copy in copies:
        copy.start()
    blank = [jnp.zeros((4, LANES - 2 * rows), f32)] if 2 * rows < LANES else []
    none = jnp.zeros((4, LANES), f32)
    for k in range(PARTS):
        arriving[k].wait()
        mine = range(k * peers // PARTS, (k + 1) * peers // PARTS)
        for peer in mine:
            at = slice(peer * rows, (peer + 1) * rows)
            piece = volume_ref[0, :, at]
            wide = jnp.concatenate([piece[i * depth : (i + 1) * depth] for i in range(chunks)], axis=1)
            slot = peers - 1 - peer
            block_ref[slot, :depth] = wide.astype(bf16)
            _, middle, final = split(jnp.concatenate([piece[:2], piece[rows - 2 :]], axis=0), 3)
            lower = jnp.concatenate([middle, final] + blank, axis=1)
            block_ref[slot, depth:] = jnp.concatenate([lower, none], axis=0).astype(bf16)
        at = pl.ds(peers - mine.stop, len(mine))
        copies.append(pltpu.make_async_copy(block_ref.at[at], out_ref.at[at], sent_sems.at[k]))
        copies[-1].start()
    for copy in copies:
        copy.wait()


def prep_kernel(
    angles_ref, offsets_ref, gain_ref, base_ref, conv_a_ref, bias_ref, conv_b_ref, own_ref,
    wa_ref, wb_ref, wr_ref, lift_ref, shift_ref, table_ref,
):
    channels = conv_a_ref.shape[1]

    def column(row):
        return jnp.broadcast_to(row, (LANES, channels)).T

    lift_ref[0] = column(0.5 * gain_ref[...])
    lift_ref[1] = column(0.5 * base_ref[...])
    shift = column(0.5 * bias_ref[...])
    shift_ref[:channels] = shift
    shift_ref[channels:] = shift

    taps = [conv_a_ref[t].astype(f32) * 0.5 for t in range(9)]
    zero = jnp.zeros((channels, channels), f32)
    for r in range(2):
        for j in range(3):
            for e in range(0, 4, 2):
                pair = [taps[3 * (k - r) + j] if 0 <= k - r < 3 else zero for k in (e, e + 1)]
                at = (4 * j + e) * channels
                wa_ref[r * channels : (r + 1) * channels, at : at + 2 * channels] = jnp.concatenate(
                    pair, axis=1
                ).astype(bf16)

    own = column(own_ref[...])[:, :channels]
    row = lax.broadcasted_iota(jnp.int32, (GROUP, LANES), 0)
    half = lax.broadcasted_iota(jnp.int32, (GROUP, LANES), 1) // channels

    def both(line):
        return jnp.broadcast_to(jnp.concatenate([line, line], axis=1), (GROUP, LANES))

    folded = [split(jnp.sum(own * conv_b_ref[t].astype(f32), axis=0, keepdims=True)) for t in range(9)]
    mine = split(own_ref[...])
    for q in range(GROUP // 2 + 1):
        at = slice(q * LANES, (q + 1) * LANES)
        for j in range(3):
            for s in range(2):
                block = jnp.zeros((GROUP, LANES), f32)
                for i in range(3):
                    block = jnp.where(half + 2 * q - row == i, both(folded[3 * i + j][s]), block)
                first = (2 * j + s) * GROUP
                wb_ref[first : first + GROUP, at] = block.astype(bf16)
        if q < GROUP // 2:
            for s in range(2):
                block = jnp.where(half + 2 * q == row, both(mine[s]), 0.0)
                wr_ref[s * GROUP : (s + 1) * GROUP, at] = block.astype(bf16)

    level = jnp.abs(jnp.cos(jnp.pi * angles_ref[...].astype(f32) / ANGLES))
    table_ref[0:1] = 0.6 + 0.4 * level
    table_ref[1:2] = offsets_ref[...].astype(f32)


def shifted(block, step):
    width = block.shape[1]
    moved = pltpu.roll(block, (-step) % width, 1)
    lane = lax.broadcasted_iota(jnp.int32, (block.shape[0], LANES), 1)
    if step < 0:
        edge = jnp.where(lane == 0, jnp.zeros_like(moved[:, :LANES]), moved[:, :LANES])
        return jnp.concatenate([edge, moved[:, LANES:]], axis=1)
    edge = jnp.where(lane == LANES - 1, jnp.zeros_like(moved[:, -LANES:]), moved[:, -LANES:])
    return jnp.concatenate([moved[:, :-LANES], edge], axis=1)


def lifted(line, lift_ref, ring, at, kept_ref=None, kept_at=None, keep=None):
    channels = lift_ref.shape[1]
    tiles = line.shape[1] // LANES
    for c in range(0, channels, 16):
        gain, base = lift_ref[0, c : c + 16], lift_ref[1, c : c + 16]
        if keep is not None:
            gain, base = gain * keep, base * keep
        z = jnp.concatenate([gain] * tiles, axis=1) * line + jnp.concatenate([base] * tiles, axis=1)
        h = (z * jnp.tanh(z) + z).astype(bf16)
        ring[0, at + c : at + c + 16] = shifted(h, -1)
        ring[1, at + c : at + c + 16] = h
        ring[2, at + c : at + c + 16] = shifted(h, 1)
        if kept_ref is not None:
            kept_ref[kept_at + c : kept_at + c + 16, :] = h


def convolved(p0, p1, wa_ref, bias_ref, store, keep=None):
    width = p0.shape[2]
    for n in range(0, width, 256):
        rhs = jnp.concatenate([r[j, :, n : n + 256] for j in range(3) for r in (p0, p1)], axis=0)
        acc = jnp.dot(wa_ref[...], rhs, preferred_element_type=f32)
        z = acc + jnp.concatenate([bias_ref[...]] * 2, axis=1)
        if keep is not None:
            half = z.shape[0] // 2
            z = jnp.concatenate(
                [part if factor is None else part * factor for part, factor in zip((z[:half], z[half:]), keep)], axis=0
            )
        store(slice(n, n + 256), (z * jnp.tanh(z) + z).astype(bf16))


def projected(h1, h0, wb_ref, wr_ref):
    conv = jnp.dot(wb_ref[:, : h1.shape[0]], h1, preferred_element_type=f32)
    kept = jnp.dot(wr_ref[:, : h0.shape[0]], h0, preferred_element_type=f32)
    taps = [conv[2 * j * GROUP : (2 * j + 1) * GROUP] + conv[(2 * j + 1) * GROUP : (2 * j + 2) * GROUP] for j in range(3)]
    total = kept[:GROUP] + kept[GROUP:] + taps[1]
    return total + shifted(taps[0], -1) + shifted(taps[2], 1)


def score_kernel(*refs, begin, count):
    given, refs = refs[0], refs[1:]
    volume_ref, lift_ref, bias_ref, wa_ref, wb_ref, wr_ref, out_ref, edge_ref = refs[:8]
    copies = []
    if begin:
        refs = refs[8:]
    else:
        last_ref, seen_ref, sems, refs = refs[8], refs[9], refs[10], refs[11:]
        for view in range(seen_ref.shape[0]):
            copies.append(pltpu.make_async_copy(given.at[0, :, view], seen_ref.at[view], sems.at[view]))
            copies[-1].start()
    rings, (h0_ref, h1_ref) = refs[:-2], refs[-2:]
    turn = len(rings)
    channels = lift_ref.shape[1]
    lead = 2 * channels if begin else 0

    def lift(pair, ring):
        for k in range(2):
            row = 2 * pair + k
            line = volume_ref[0, 2 * begin + row : 2 * begin + row + 1, :]
            lifted(line, lift_ref, ring, k * channels, h0_ref, row * channels)

    def step(g, p0, p1, p2):
        if p2 is not None:
            lift(g + 2, p2)

        def store(at, h):
            h1_ref[lead + g * 2 * channels : lead + (g + 1) * 2 * channels, at] = h

        convolved(p0, p1, wa_ref, bias_ref, store)

    lift(0, rings[0])
    lift(1, rings[1])
    if begin:
        h1_ref[:lead] = given[...]

    low = 2 * begin if begin else 2
    done = low
    for k in range(count):
        step(k, rings[k % turn], rings[(k + 1) % turn], rings[(k + 2) % turn] if k + 1 < count else None)
        ready = 2 * (begin + k + 1)
        if ready - done >= WAIT or k + 1 == count:
            at = (done - low) * channels
            own = (done - 2 * begin) * channels
            size = ready - done
            total = projected(h1_ref[at : at + (size + 2) * channels], h0_ref[own : own + size * channels], wb_ref, wr_ref)
            out_ref[done : done + size] = total[:size]
            done = ready

    total = (2 * count) * channels + lead
    if begin:
        edge_ref[...] = h1_ref[total - 2 * channels : total]
    else:
        edge_ref[...] = h1_ref[: 2 * channels]
        last_ref[...] = h1_ref[total - 2 * channels : total]
    for copy in copies:
        copy.wait()


def data_kernel(table_ref, cells_in_ref, seen_ref, measured_ref, out_ref, cells_ref, back_ref, sum_ref, line_ref, sems, *scratch):
    rows, views, det = measured_ref.shape[1:]
    peers = cells_in_ref.shape[0]
    nx = cells_ref.shape[1]
    chunks = LANES // rows
    depth = rows // chunks
    blocks = nx // LANES
    sets = [scratch[2 * k : 2 * k + 2] for k in range(len(scratch) // 2)]
    body = slice(LANES, LANES + det)

    def fetch(view):
        return pltpu.make_async_copy(measured_ref.at[0, :, view], line_ref.at[view, :, body], sems.at[view])

    early = seen_ref.shape[0]
    for view in range(early, views):
        fetch(view).start()
    for view in range(early):
        line_ref[view, :, body] = seen_ref[view]

    for tile in range(nx // LANES):
        pieces = []
        for peer in range(tile * chunks, (tile + 1) * chunks):
            got = cells_in_ref[peers - 1 - peer, :depth].astype(f32)
            pieces += [got[:, k * rows : (k + 1) * rows] for k in range(chunks)]
        cells_ref[:, tile * LANES : (tile + 1) * LANES] = (-jnp.concatenate(pieces, axis=0).T).astype(bf16)

    back_ref[...] = jnp.zeros_like(back_ref)
    sum_ref[...] = jnp.zeros_like(sum_ref)
    for low_ref, _ in sets:
        low_ref[...] = jnp.zeros_like(low_ref)

    cell = lax.broadcasted_iota(jnp.int32, (16, LANES), 1).astype(f32)
    place = lax.broadcasted_iota(jnp.int32, (16, LANES), 0)
    bins = jnp.concatenate([(place + 16 * k).astype(jnp.int16) for k in range(16)], axis=0)

    def window(view, b):
        begin = (det - 1) * 0.5 + (b * LANES - (nx - 1) * 0.5) * table_ref[0, view] + table_ref[1, view]
        first = jnp.floor(begin * (1.0 / LANES))
        at = pl.ds(pl.multiple_of((first.astype(jnp.int32) + 1) * LANES, LANES), 2 * LANES)
        return at, begin - first * LANES

    def forward(view, low_ref, tent_ref):
        for b in range(blocks):
            at, begin = window(view, b)
            target = cell * table_ref[0, view] + begin
            under = jnp.floor(target)
            near = (1.0 - (target - under)).astype(bf16)
            far = (1.0 - ((under + 1.0) - target)).astype(bf16)
            spot = under.astype(jnp.int32)
            this = jnp.concatenate([spot.astype(jnp.int16)] * 16, axis=0)
            after = jnp.concatenate([(spot + 1).astype(jnp.int16)] * 16, axis=0)
            near = jnp.concatenate([near] * 16, axis=0)
            far = jnp.concatenate([far] * 16, axis=0)
            tent = jnp.where(bins == this, near, jnp.where(bins == after, far, jnp.zeros_like(far)))
            tent_ref[b] = tent
            line_ref[view, :, at] += lax.dot_general(
                cells_ref[:, b * LANES : (b + 1) * LANES],
                tent,
                (((1,), (1,)), ((), ())),
                preferred_element_type=f32,
            )
        misfit = line_ref[view, :, body]
        low_ref[:, body] = misfit.astype(bf16)
        square = misfit * misfit
        total = square[:, :LANES]
        for k in range(1, det // LANES):
            total = total + square[:, k * LANES : (k + 1) * LANES]
        sum_ref[...] += total

    def backward(view, low_ref, tent_ref):
        for b in range(blocks):
            at, _ = window(view, b)
            back_ref[:, b * LANES : (b + 1) * LANES] += jnp.dot(
                low_ref[:, at], tent_ref[b], preferred_element_type=f32
            )

    turn = len(sets)
    lead = turn // 2
    rounds = (views - lead) // turn
    for view in range(early, lead):
        fetch(view).wait()
    for view in range(lead):
        forward(view, *sets[view])

    def several(it, carry):
        for k in range(turn):
            view = it * turn + lead + k

            @pl.when(view >= early)
            def _():
                fetch(view).wait()

        for k in range(turn):
            forward(it * turn + lead + k, *sets[(lead + k) % turn])
            backward(it * turn + k, *sets[k])
        return carry

    lax.fori_loop(0, rounds, several, 0)
    for view in range(max(rounds * turn + lead, early), views):
        fetch(view).wait()
    for view in range(rounds * turn, views):
        if view + lead < views:
            forward(view + lead, *sets[(view + lead) % turn])
        backward(view, *sets[view % turn])

    whole = split(jnp.sum(sum_ref[...], keepdims=True), 3)
    lane = lax.broadcasted_iota(jnp.int32, (8, LANES), 1)
    third = lax.broadcasted_iota(jnp.int32, (8, LANES), 0) == 2
    got = [cells_in_ref[peers - 1 - peer].astype(f32) for peer in range(peers)]
    for peer in range(peers):
        low, high = got[max(peer - 1, 0)], got[min(peer + 1, peers - 1)]
        note = jnp.concatenate(
            [low[depth - 2 : depth], high[:2], low[depth + 2 : depth + 4], high[depth : depth + 2]], axis=0
        )
        for k in range(3):
            note = jnp.where(third & (lane == rows + k), whole[k], note)
        out_ref[peers - 1 - peer, depth:] = note.astype(bf16)
    for tile in range(nx // LANES):
        turned = back_ref[:, tile * LANES : (tile + 1) * LANES].T
        for k in range(chunks):
            peer = tile * chunks + k
            own = turned[k * rows : (k + 1) * rows]
            wide = jnp.concatenate([own[i * depth : (i + 1) * depth] for i in range(chunks)], axis=1)
            out_ref[peers - 1 - peer, :depth] = wide.astype(bf16)


def finish_kernel(
    anchor_ref, step_ref, volume_ref, noise_ref, one_ref, two_ref, back_ref, head_ref, tail_ref, lift_ref, bias_ref,
    wa_ref, wb_ref, wr_ref, out_ref, ext_ref, score_ref, done_ref, sems, *scratch, count, height, border,
):
    rows, width = score_ref.shape
    channels = lift_ref.shape[1]
    peers = back_ref.shape[0]
    chunks = LANES // rows
    depth = rows // chunks
    anchor = anchor_ref[0]
    rings, h1_refs = scratch[:4], scratch[4:]

    tails = [back_ref[peers - 1 - peer, depth:].astype(f32) for peer in range(peers)]
    lane = lax.broadcasted_iota(jnp.int32, (8, LANES), 1)
    third = lax.broadcasted_iota(jnp.int32, (8, LANES), 0) == 2
    total = tails[0]
    for tail in tails[1:]:
        total = total + tail
    misfit = jnp.sum(jnp.where(third & (lane >= rows) & (lane < rows + 3), total, 0.0), keepdims=True)

    ext_ref[2:4] = volume_ref[0, :2]
    ext_ref[8:10] = volume_ref[0, rows - 2 :]
    for tile in range(width // LANES):
        mine = tails[tile * chunks : (tile + 1) * chunks]
        upper = [t[0:2, LANES - rows :] for t in mine], [t[2:4, :rows] for t in mine]
        for side, target in ((0, 0), (1, 10)):
            parts = [upper[side]] + [
                [t[4 + 2 * side : 6 + 2 * side, k * rows : (k + 1) * rows] for t in mine] for k in range(2)
            ]
            parts = [jnp.concatenate(p, axis=1) for p in parts]
            ext_ref[target : target + 2, tile * LANES : (tile + 1) * LANES] = parts[0] + parts[1] + parts[2]

    score_ref[:border] = one_ref[:border]
    score_ref[border:] = two_ref[border:]
    step = step_ref[...].reshape(1, 1)
    weight = data_gain / jnp.sqrt(misfit / count + 1e-06)
    sway = jnp.sqrt(2.0 * step)

    def combine(low, high, sem):
        for tile in range(width // LANES):
            at = slice(tile * LANES, (tile + 1) * LANES)
            got = [back_ref[peers - 1 - tile * chunks - k, :depth].astype(f32) for k in range(chunks)]
            back = jnp.concatenate(
                [jnp.concatenate([g[:, k * rows : (k + 1) * rows] for g in got], axis=1) for k in range(chunks)], axis=0
            )[low:high]
            moved = step * (score_ref[low:high, at] + weight * back)
            done_ref[low:high, at] = volume_ref[0, low:high, at] + moved + sway * noise_ref[0, low:high, at]
        copy = pltpu.make_async_copy(done_ref.at[pl.ds(low, high - low)], out_ref.at[0, pl.ds(low, high - low)], sem)
        copy.start()
        return copy

    copies = [combine(8, rows - 8, sems.at[0])] if rows > 16 else []
    inside = jnp.where(anchor > 0, 1.0, 0.0).astype(f32), jnp.where(anchor + rows < height, 1.0, 0.0).astype(f32)
    for side in range(2):
        own = rings[2 * side : 2 * side + 2]
        for k in range(4):
            line = ext_ref[8 * side + k : 8 * side + k + 1, :]
            halo = (k < 2) == (side == 0)
            lifted(line, lift_ref, own[k // 2], (k % 2) * channels, keep=inside[side] if halo else None)
    for side in range(2):
        own = rings[2 * side : 2 * side + 2]
        h1_ref = h1_refs[side]
        at = 2 * channels * side

        def store(columns, h):
            h1_ref[at : at + 2 * channels, columns] = h

        convolved(*own, wa_ref, bias_ref, store, keep=((inside[0], None), (None, inside[1]))[side])
        h1_ref[2 * channels - at : 4 * channels - at] = (head_ref, tail_ref)[side][...]
        scores = projected(h1_ref[...], own[1 - side][1], wb_ref, wr_ref)
        row = (rows - 2) * side
        score_ref[row : row + 2] = scores[:2]

    for k, low in enumerate((0, rows - 8)):
        copies.append(combine(low, low + 8, sems.at[k + 1]))
    for copy in copies:
        copy.wait()


def call(kernel, mebibytes, **kwargs):
    params = pltpu.CompilerParams(vmem_limit_bytes=mebibytes << 20)
    return pl.pallas_call(kernel, compiler_params=params, **kwargs)


def spec(shape, dtype):
    return jax.ShapeDtypeStruct(shape, dtype)


def apart(array):
    return pltpu.with_memory_space_constraint(array, pltpu.HBM)


def data_call(table, cells, seen, measured):
    rows, views, det = measured.shape[1:]
    peers = cells.shape[0]
    nx = peers * rows
    wide = det + 2 * LANES
    lines = [
        pltpu.VMEM((rows, wide), bf16),
        pltpu.VMEM((nx // LANES, 2 * LANES, LANES), bf16),
    ]
    return call(
        data_kernel,
        12,
        out_shape=spec((peers, rows * rows // LANES + 8, LANES), bf16),
        in_specs=[SMEM, VMEM, VMEM, HBM],
        out_specs=VMEM,
        scratch_shapes=[
            pltpu.VMEM((rows, nx), bf16),
            pltpu.VMEM((rows, nx), f32),
            pltpu.VMEM((rows, LANES), f32),
            pltpu.VMEM((views, rows, wide), f32),
            pltpu.SemaphoreType.DMA((views,)),
            *lines * SETS,
        ],
    )(table, cells, seen, apart(measured))


def per_device(
    volume,
    noise,
    measured,
    angles,
    offsets,
    step_size,
    lift_w,
    lift_b,
    conv_a,
    bias_a,
    conv_b,
    out_w,
):
    slices, rows, width = volume.shape
    views, det = measured.shape[2:]
    channels = lift_w.shape[0]
    peers = lax.axis_size("slab")
    height = peers * rows
    chunks = LANES // rows
    depth = rows // chunks

    def line(array):
        return array.reshape(1, -1)

    pairs = rows // 2 - 1
    order = [list(reversed(range(peers)))]
    half = pairs // 2
    ring = pltpu.VMEM((3, 2 * channels, width), bf16)
    pair = spec((2 * channels, width), bf16)
    anchor = (lax.axis_index("slab") * rows).astype(jnp.int32).reshape(1)
    small = (volume, line(angles), line(offsets), line(lift_w), line(lift_b), conv_a, line(bias_a), conv_b, line(out_w))

    def score_part(begin, count, *args):
        more = () if begin else (pair, spec((EARLY, rows, det), f32))
        return call(
            functools.partial(score_kernel, begin=begin, count=count),
            20,
            out_shape=(spec((rows, width), f32), pair) + more,
            in_specs=[VMEM if begin else HBM] + [VMEM] * (len(args) - 1),
            out_specs=(VMEM,) * (2 + len(more)),
            scratch_shapes=([] if begin else [pltpu.SemaphoreType.DMA((EARLY,))])
            + [
                *[ring] * min(TURN, half),
                pltpu.VMEM(((2 * count + 4) * channels, width), bf16),
                pltpu.VMEM(((2 * count + 2) * channels, width), bf16),
            ],
        )(*args)

    payload, volume, *small = call(
        pack_kernel,
        4,
        out_shape=(spec((peers, depth + 8, LANES), bf16),) + tuple(spec(a.shape, a.dtype) for a in small),
        in_specs=[HBM] * len(small),
        out_specs=(HBM,) + (VMEM,) * len(small),
        scratch_shapes=[
            pltpu.VMEM((peers, depth + 8, LANES), bf16),
            pltpu.SemaphoreType.DMA((len(small) - 1 + PARTS,)),
            pltpu.SemaphoreType.DMA((PARTS,)),
        ],
    )(*[apart(a) for a in small])
    cells = lax.all_to_all(payload, "slab", 0, 0, axis_index_groups=order)
    wa, wb, wr, lift, bias, table = call(
        prep_kernel,
        6,
        out_shape=(
            spec((2 * channels, 12 * channels), bf16),
            spec((6 * GROUP, (GROUP + 2) * channels), bf16),
            spec((2 * GROUP, GROUP * channels), bf16),
            spec((2, channels, LANES), f32),
            spec((2 * channels, LANES), f32),
            spec((2, views), f32),
        ),
        in_specs=[VMEM] * 8,
        out_specs=(VMEM,) * 6,
    )(*small)
    consts = (lift, bias, wa, wb, wr)
    one, head, middle, seen = score_part(0, half, apart(measured), volume, *consts)

    sent = data_call(table, cells, seen, measured)
    returned = lax.all_to_all(sent, "slab", 0, 0, axis_index_groups=order)
    two, tail = score_part(half, pairs - half, middle, volume, *consts)
    return call(
        functools.partial(finish_kernel, count=slices * peers * rows * views * det, height=height, border=2 * half),
        12,
        out_shape=spec(volume.shape, f32),
        in_specs=[SMEM] + [VMEM] * 13,
        out_specs=HBM,
        scratch_shapes=[
            pltpu.VMEM((16, width), f32),
            pltpu.VMEM((rows, width), f32),
            pltpu.VMEM((rows, width), f32),
            pltpu.SemaphoreType.DMA((3,)),
            *[ring] * 4,
            *[pltpu.VMEM((4 * channels, width), bf16)] * 2,
        ],
    )(anchor, step_size, volume, noise, one, two, returned, head, tail, *consts)


def solution(mesh):
    placed = (
        P("groups", "slab", None),
        P("groups", "slab", None),
        P("groups", "slab", None, None),
        P("groups"),
        P("groups"),
        P("groups"),
        P(),
        P(),
        P(),
        P(),
        P(),
        P(),
    )
    return jax.shard_map(
        per_device, mesh=mesh, in_specs=placed, out_specs=P("groups", "slab", None), check_vma=False
    )
```
